32 devices in a mesh: seq: 4 (over x, core), fsdp: 8 (over z, y).
Axes of the slice: x: 2, y: 2, z: 4, core: 2. Of those that a mesh axis runs over, the one named last changes fastest.
Arguments:
- inputs: bfloat16 [8, 1536, 1152], P('fsdp', 'seq'), may hold values from -6 to 6
- image_ids: int32 [8, 1536], P('fsdp', 'seq'), may hold values from 0 to 2, never falling along the last dimension, each value on 1 to 729 neighbouring positions
- pad_mask: int32 [8, 1536], P('fsdp', 'seq'), may hold values 0 or 1
- cotangent: bfloat16 [8, 1536, 1152], P('fsdp', 'seq'), may hold values from -6 to 6
- w_qkv: bfloat16 [1152, 3456], P('fsdp'), may hold values from -0.1875 to 0.1875
- w_out: bfloat16 [1152, 1152], P('fsdp'), may hold values from -1.5 to 1.5
- w_up: bfloat16 [1152, 4304], P('fsdp'), may hold values from -0.1875 to 0.1875
- w_down: bfloat16 [4304, 1152], P('fsdp'), may hold values from -0.09375 to 0.09375
- ln1_gain: float32 [1152], replicated, may hold values from 0.5 to 1.5
- ln1_shift: float32 [1152], replicated, may hold values from -4 to 4
- q_bias: float32 [1152], replicated, may hold values from -4 to 4
- v_bias: float32 [1152], replicated, may hold values from -4 to 4
- out_bias: float32 [1152], replicated, may hold values from -4 to 4
- ln2_gain: float32 [1152], replicated, may hold values from 0.5 to 1.5
- ln2_shift: float32 [1152], replicated, may hold values from -4 to 4
- up_bias: float32 [4304], replicated, may hold values from -4 to 4
- down_bias: float32 [1152], replicated, may hold values from -4 to 4
Outputs:
- layer_out: bfloat16 [8, 1536, 1152], P('fsdp', 'seq')
- grad_inputs: bfloat16 [8, 1536, 1152], P('fsdp', 'seq')
- grad_w_qkv: float32 [1152, 3456], P('fsdp', 'seq')
- grad_w_out: float32 [1152, 1152], P('fsdp', 'seq')
- grad_w_up: float32 [1152, 4304], P('fsdp', 'seq')
- grad_w_down: float32 [4304, 1152], P('fsdp', 'seq')
- grad_ln1_gain: float32 [1152], replicated
- grad_ln1_shift: float32 [1152], replicated
- grad_q_bias: float32 [1152], replicated
- grad_v_bias: float32 [1152], replicated
- grad_out_bias: float32 [1152], replicated
- grad_ln2_gain: float32 [1152], replicated
- grad_ln2_shift: float32 [1152], replicated
- grad_up_bias: float32 [4304], replicated
- grad_down_bias: float32 [1152], replicated
The draws below stay inside these ranges and needn't reach their ends.
Inputs may be any that keep to these rules, and one draw needn't show every extreme that they name: `image_ids`: within a group ids never fall; every image has 1 to 729 tokens, one of them exactly 729, and all 3 ids occur.
All inputs are finite; a program needn't handle non-finite values. No bound on the sum of `pad_mask` on one device may be relied on, other than what follows from the above.
Results may differ from the reference program's by a relative error of at most 0.015.
Values may be sent and summed in bfloat16 or wider, within the bound.
No kernel may reach another device: no remote copies, remote signals or barrier semaphores. Data moves between devices by JAX's collectives and lax.ppermute only.
A program may use at most 192 MiB of HBM per device.

```python
import math
import jax
import jax.numpy as jnp
import numpy as np
from jax import lax

D = 1152
HEADS = 16
HD = 72
FF = 4304
IMG_TOK = 729
GROUPS = 8
RUN = 1536
IMAGES = 3


def place_ends(drawn, own_key, smallest, largest):
    place = [jax.random.randint(jax.random.fold_in(own_key, axis), (), 0, length) for axis, length in enumerate(drawn.shape)]
    widest = drawn.shape.index(max(drawn.shape))
    neighbour = place[:widest] + [(place[widest] + 1) % drawn.shape[widest]] + place[widest + 1:]
    return drawn.at[tuple(place)].set(smallest).at[tuple(neighbour)].set(largest)


def level_of(stream_key, dims, shards, low, largest):
    def one(dim, blocks):
        heights = jax.random.uniform(jax.random.fold_in(jax.random.fold_in(stream_key, 6), dim), (blocks,), jnp.float32, low / len(shards), largest / len(shards))
        return jnp.repeat(jnp.exp(heights), dims[dim] // blocks).reshape((-1,) + (1,) * (len(dims) - dim - 1))

    level = one(*shards[0])
    for cut in shards[1:]:
        level = level * one(*cut)
    return level


def split_up(amount, total, bound, lean):
    portions = [(1 << 20) // math.isqrt(grade ** lean) + 1 for grade in range(2, amount + 1)]
    rest, counts = total - bound - (amount - 1), [1] * (amount - 1)
    while rest > 0:
        free = [i for i in range(amount - 1) if counts[i] < bound]
        mass, left = sum([portions[i] for i in free]), rest
        for i in free:
            extra = min(bound - counts[i], max(1, left * portions[i] // mass), rest)
            counts[i] = counts[i] + extra
            rest = rest - extra
    return np.array([bound] + counts)


def ragged(key, amount, total, bound, lean):
    if amount == 2:
        one = jax.random.randint(key, (), max(1, total - bound), min(bound, total - 1) + 1)
        return jnp.stack([one, total - one])
    tallies = jnp.asarray(split_up(amount, total, bound, lean), jnp.int32)
    twos = (amount - 1) // 2
    donor, receiver = tallies[1:1 + 2 * twos:2], tallies[2:2 + 2 * twos:2]
    room = jnp.minimum(donor - 1, bound - receiver)
    shifted = jax.random.randint(jax.random.fold_in(key, 1), (twos,), 0, 1 << 20) % (room + 1)
    tallies = tallies.at[1:1 + 2 * twos:2].set(donor - shifted).at[2:2 + 2 * twos:2].set(receiver + shifted)
    return tallies[jax.random.permutation(jax.random.fold_in(key, 2), amount)]


def scatter_about(rng, dims, scale, bound, split=(), kind=jnp.bfloat16):
    level = level_of(rng, dims, split, -0.22, 0.18) if split else 1.0
    values = jax.random.normal(rng, dims, jnp.float32) * scale * level
    return jnp.minimum(jnp.maximum(values, -bound), bound).astype(kind)


def setup_inputs(seed: int = 0) -> dict:
    key_of = jax.random.split(jax.random.key(seed), 18)
    return {
        "inputs": scatter_about(key_of[0], (GROUPS, RUN, D), 1.0, 6.0, ((0, 8), (1, 4))),
        "image_ids": jax.vmap(lambda own: jnp.searchsorted(jnp.cumsum(ragged(own, IMAGES, RUN, IMG_TOK, 0)), jnp.arange(RUN), side="right"))(jax.random.split(key_of[1], GROUPS)).reshape((GROUPS, RUN)).astype(jnp.int32),
        "pad_mask": place_ends((jax.random.randint(key_of[2], (GROUPS, RUN), 0, 8) < 1).astype(jnp.int32), jax.random.fold_in(key_of[2], 1), 0, 1),
        "cotangent": scatter_about(key_of[3], (GROUPS, RUN, D), 1.0, 6.0, ((0, 8), (1, 4))),
        "w_qkv": scatter_about(key_of[4], (D, 3 * D), D ** -0.5, 0.1875, ((0, 8),)),
        "w_out": scatter_about(key_of[5], (D, D), (max(1, D // 64)) ** -0.5, 1.5, ((0, 8),)),
        "w_up": scatter_about(key_of[6], (D, FF), D ** -0.5, 0.1875, ((0, 8),)),
        "w_down": scatter_about(key_of[7], (FF, D), FF ** -0.5, 0.09375, ((0, 8),)),
        "ln1_gain": jnp.clip(1.0 + 0.1 * jax.random.normal(key_of[8], (D,), jnp.float32), 0.5, 1.5),
        "ln1_shift": scatter_about(key_of[9], (D,), 0.3, 4.0, (), jnp.float32),
        "q_bias": scatter_about(key_of[10], (D,), 0.3, 4.0, (), jnp.float32),
        "v_bias": scatter_about(key_of[11], (D,), 0.3, 4.0, (), jnp.float32),
        "out_bias": scatter_about(key_of[12], (D,), 0.3, 4.0, (), jnp.float32),
        "ln2_gain": jnp.clip(1.0 + 0.1 * jax.random.normal(key_of[13], (D,), jnp.float32), 0.5, 1.5),
        "ln2_shift": scatter_about(key_of[14], (D,), 0.3, 4.0, (), jnp.float32),
        "up_bias": scatter_about(key_of[15], (FF,), 0.3, 4.0, (), jnp.float32),
        "down_bias": scatter_about(key_of[16], (D,), 0.3, 4.0, (), jnp.float32),
    }


EPSILON = 1e-06
HIGHEST = lax.Precision.HIGHEST

@jax.custom_vjp
def low(v):
    return lax.optimization_barrier(v.astype(jnp.bfloat16)).astype(jnp.float32)

@jax.custom_vjp
def low_back(v):
    return v

def low_keep(v):
    return (low(v), None)

def low_pass(kept, grad):
    return (grad,)

def back_keep(v):
    return (v, None)

def back_low(kept, grad):
    return (low(grad),)
low.defvjp(low_keep, low_pass)
low_back.defvjp(back_keep, back_low)

def layer_norm(values, gain, shift):
    average = lax.optimization_barrier(jnp.mean(values, axis=-1, keepdims=True))
    centred = values - average
    spread = lax.optimization_barrier(jnp.mean(centred * centred, axis=-1, keepdims=True))
    return centred * lax.rsqrt(spread + EPSILON) * gain + shift

def block_attention(queries, start, keys, values, image_row, key_valid):
    size = queries.shape[0]
    length = keys.shape[0]
    query_ids = lax.dynamic_slice_in_dim(image_row, start.astype(jnp.int32), size)
    query_pos = start.astype(jnp.int32) + jnp.arange(size, dtype=jnp.int32)
    key_pos = jnp.arange(length, dtype=jnp.int32)
    allowed = (query_ids[:, None] == image_row[None, :]) & (key_valid[None, :] | (query_pos[:, None] == key_pos[None, :]))
    raw_scores = jnp.einsum('qhd,khd->hqk', queries, keys, precision=HIGHEST) * HD ** (-0.5)
    raw_scores = low_back(raw_scores)
    masked = jnp.where(allowed[None], raw_scores, -1e+30)
    top_score = lax.optimization_barrier(jnp.max(masked, axis=-1, keepdims=True))
    expo = jnp.exp(masked - top_score)
    total = lax.optimization_barrier(jnp.sum(expo, axis=-1, keepdims=True))
    probs = low(expo / total)
    return jnp.einsum('hqk,khd->qhd', probs, values, precision=HIGHEST)

def group_attention(queries, keys, values, image_row, key_valid):
    length = queries.shape[0]
    block_rows = min(512, length)
    count = length // block_rows
    blocks = queries.reshape(count, block_rows, HEADS, HD)
    starts = jnp.arange(count, dtype=jnp.int32) * block_rows

    def one_block(item):
        return block_attention(item[0], item[1], keys, values, image_row, key_valid)
    outputs = lax.map(jax.checkpoint(one_block), (blocks, starts))
    return outputs.reshape(length, HEADS, HD)

def reference(inputs, image_ids, pad_mask, cotangent, w_qkv, w_out, w_up, w_down, ln1_gain, ln1_shift, q_bias, v_bias, out_bias, ln2_gain, ln2_shift, up_bias, down_bias):
    groups, length, width = inputs.shape
    key_valid = pad_mask == 0
    keep = (1 - pad_mask).astype(jnp.float32)

    def attend_all(queries, keys, values):
        shaped = (queries.reshape(groups, length, HEADS, HD), keys.reshape(groups, length, HEADS, HD), values.reshape(groups, length, HEADS, HD), image_ids, key_valid)

        def one_group(item):
            return group_attention(item[0], item[1], item[2], item[3], item[4])
        return lax.map(one_group, shaped).reshape(groups * length, width)

    def forward(x_float, weight_qkv, weight_out, weight_up, weight_down, gain_one, shift_one, bias_query, bias_value, bias_out, gain_two, shift_two, bias_up, bias_down):
        h_one = low(layer_norm(x_float, gain_one, shift_one))
        projected = jnp.dot(h_one, weight_qkv, precision=HIGHEST)
        queries = low(low_back(projected[:, :width] + bias_query))
        keys = low(low_back(projected[:, width:2 * width]))
        values = low(low_back(projected[:, 2 * width:] + bias_value))
        attended = low(low_back(attend_all(queries, keys, values)))
        branch = low_back(jnp.dot(attended, weight_out, precision=HIGHEST) + bias_out)
        x_one = x_float + branch
        h_two = low(layer_norm(x_one, gain_two, shift_two))
        hidden = low_back(jnp.dot(h_two, weight_up, precision=HIGHEST) + bias_up)
        active = low(jax.nn.gelu(hidden, approximate=True))
        mixed = low_back(jnp.dot(active, weight_down, precision=HIGHEST) + bias_down)
        return x_one + mixed
    x_float = inputs.reshape(groups * length, width).astype(jnp.float32)
    params = (w_qkv.astype(jnp.float32), w_out.astype(jnp.float32), w_up.astype(jnp.float32), w_down.astype(jnp.float32), ln1_gain, ln1_shift, q_bias, v_bias, out_bias, ln2_gain, ln2_shift, up_bias, down_bias)
    result, backward = jax.vjp(forward, x_float, *params)
    seed_grad = cotangent.reshape(groups * length, width).astype(jnp.float32) * keep.reshape(groups * length)[:, None]
    grads = backward(seed_grad)
    layer_out = result.reshape(groups, length, width).astype(jnp.bfloat16)
    grad_inputs = grads[0].reshape(groups, length, width).astype(jnp.bfloat16)
    return (layer_out, grad_inputs, grads[1], grads[2], grads[3], grads[4], grads[5], grads[6], grads[7], grads[8], grads[9], grads[10], grads[11], grads[12], grads[13])
```

```python
import functools
import math

import jax
import jax.numpy as jnp
from jax import lax
from jax.experimental import pallas as pl
from jax.experimental.pallas import tpu as pltpu
from jax.sharding import PartitionSpec as P

HEADS = 16
HD = 72
EPSILON = 1e-06
SCALING = HD ** (-0.5)
LOG2E = math.log2(math.e)
NEG = -1e30
BF = jnp.bfloat16
F32 = jnp.float32


def windows(heads, width):
    out = []
    for h in range(heads):
        lo = h * HD // 128 * 128
        out.append((lo, min(width, -(-(h * HD + HD) // 128) * 128)))
    return out


def head_lanes(lo, h, shape):
    lane = lax.broadcasted_iota(jnp.int32, shape, 1) + lo
    return (lane >= h * HD) & (lane < h * HD + HD)


def head_pieces(wins, outs):
    pieces = {}
    for (lo, hi), out in zip(wins, outs):
        for c in range(lo, hi, 128):
            part = out[:, c - lo : min(c + 128, hi) - lo]
            pieces[c] = part if c not in pieces else pieces[c] + part
    return pieces.items()


def lanes(width):
    return -(-width // 128) * 128


def load_blocks(blocks, target, slots, first, sems):
    rows = blocks[0].shape[0]
    copies = []
    for i, block in enumerate(blocks):
        start = pl.multiple_of(slots[first + i] * rows, 8)
        copies.append(pltpu.make_async_copy(block, target.at[pl.ds(start, rows)], sems.at[i]))
        copies[-1].start()
    for copy in copies:
        copy.wait()


def forward_kernel(heads, tile, bounds, q_ref, k_ref, v_ref, qid_ref, kid_ref, o_ref, lse_ref, s_ref):
    i = pl.program_id(0)
    lo, hi = bounds[0, i], bounds[1, i]
    wins = windows(heads, q_ref.shape[1])
    rel = lax.broadcasted_iota(jnp.int32, (tile, tile), 0) - lax.broadcasted_iota(jnp.int32, (tile, tile), 1)
    qid = jnp.concatenate([qid_ref[...]] * (tile // 128), axis=1)
    queries = []
    for h, (a, b) in enumerate(wins):
        w = q_ref[:, a:b]
        queries.append(jnp.where(head_lanes(a, h, w.shape), w, jnp.zeros_like(w)))

    def scores(t, tops):
        rows = pl.ds(pl.multiple_of(t * tile, tile), tile)
        allowed = (qid == kid_ref[:, rows]) | (rel == (t - i) * tile)
        new = []
        for h, (a, b) in enumerate(wins):
            s = lax.dot_general(queries[h], k_ref[rows, a:b], (((1,), (1,)), ((), ())), preferred_element_type=F32)
            s = jnp.where(allowed, s * (SCALING * LOG2E), NEG)
            s_ref[h, :, rows] = s
            top = tops[h]
            for c in range(0, tile, 128):
                top = jnp.maximum(top, s[:, c : c + 128])
            new.append(top)
        return tuple(new)

    tops = lax.fori_loop(lo, hi, scores, tuple(jnp.full((tile, 128), NEG, F32) for _ in range(heads)))
    tops = [jnp.broadcast_to(jnp.max(t, axis=1, keepdims=True), (tile, 128)) for t in tops]

    def attend(t, carry):
        rows = pl.ds(pl.multiple_of(t * tile, tile), tile)
        new = []
        for h, (a, b) in enumerate(wins):
            total, acc = carry[h]
            p = jnp.exp2(s_ref[h, :, rows] - jnp.concatenate([tops[h]] * (tile // 128), axis=1))
            for c in range(0, tile, 128):
                total = total + p[:, c : c + 128]
            acc = acc + jnp.dot(p.astype(BF), v_ref[rows, a:b], preferred_element_type=F32)
            new.append((total, acc))
        return tuple(new)

    start = tuple((jnp.zeros((tile, 128), F32), jnp.zeros((tile, b - a), F32)) for a, b in wins)
    carry = lax.fori_loop(lo, hi, attend, start)
    lane = lax.broadcasted_iota(jnp.int32, (tile, 128), 1)
    lse = jnp.zeros((tile, 128), F32)
    outs = []
    for h, (a, b) in enumerate(wins):
        total = jnp.sum(carry[h][0], axis=1, keepdims=True)
        out = carry[h][1] * (1.0 / total)
        outs.append(jnp.where(head_lanes(a, h, out.shape), out, 0.0))
        lse = jnp.where(lane == h, tops[h] + jnp.log2(total), lse)
    for c, part in head_pieces(wins, outs):
        o_ref[:, c : c + part.shape[1]] = part.astype(BF)
    lse_ref[...] = lse


def whole_block(shape):
    return pl.BlockSpec(shape, lambda *_: (0, 0))


def kept_block(shape):
    return pl.BlockSpec(shape, lambda *_: (0, 0), pipeline_mode=pl.Buffered(1))


def row_block(tile, width):
    return pl.BlockSpec((tile, width), lambda i, *_: (i, 0))


def slot_block(tile, width):
    return pl.BlockSpec((tile, width), lambda i, slots: (slots[i], 0))


def attention_forward(q, k, v, qid, kid, bounds, heads, tile):
    n, width = q.shape
    return pl.pallas_call(
        functools.partial(forward_kernel, heads, tile),
        out_shape=(jax.ShapeDtypeStruct((n, width), BF), jax.ShapeDtypeStruct((n, 128), F32)),
        grid_spec=pltpu.PrefetchScalarGridSpec(
            num_scalar_prefetch=1,
            grid=(n // tile,),
            in_specs=[
                row_block(tile, width),
                whole_block((n, width)),
                whole_block((n, width)),
                row_block(tile, 128),
                whole_block((1, n)),
            ],
            out_specs=[row_block(tile, width), row_block(tile, 128)],
            scratch_shapes=[pltpu.VMEM((heads, tile, n), F32)],
        ),
        compiler_params=pltpu.CompilerParams(vmem_limit_bytes=48 << 20),
        cost_estimate=pl.CostEstimate(flops=4 * n * n * 128 * heads, bytes_accessed=10 * n * width, transcendentals=n * n * heads),
        name="attention_forward",
    )(bounds, q, k, v, qid, kid)


def backward_kernel(
    heads, tile, count, bounds, slots, q_ref, k_ref, v_ref, o_ref, lse_ref, qid_ref, kid_ref, *refs
):
    blocks, (out_ref, go_ref, dk_acc, dv_acc, dq_acc, sems) = refs[:count], refs[count:]
    i = pl.program_id(0)
    lo, hi = bounds[0, i], bounds[1, i]
    width = q_ref.shape[1]
    wins = windows(heads, width)

    @pl.when(i == 0)
    def _():
        load_blocks(blocks, go_ref, slots, 0, sems)
        dk_acc[...] = jnp.zeros_like(dk_acc)
        dv_acc[...] = jnp.zeros_like(dv_acc)

    here = pl.ds(pl.multiple_of(i * tile, tile), tile)
    rel = lax.broadcasted_iota(jnp.int32, (tile, tile), 1) - lax.broadcasted_iota(jnp.int32, (tile, tile), 0)
    lane = lax.broadcasted_iota(jnp.int32, (tile, 128), 1)
    inner = jnp.zeros((tile, 128), F32)
    queries, grads = [], []
    for h, (a, b) in enumerate(wins):
        w, g = q_ref[:, a:b], go_ref[here, a:b]
        on = head_lanes(a, h, w.shape)
        queries.append(jnp.where(on, w, jnp.zeros_like(w)))
        g = jnp.where(on, g, jnp.zeros_like(g))
        grads.append(g)
        r = jnp.sum(o_ref[:, a:b].astype(F32) * g.astype(F32), axis=1, keepdims=True)
        inner = jnp.where(lane == h, r, inner)
        dq_acc[h, :, : b - a] = jnp.zeros((tile, b - a), F32)
    inner = inner.T
    lse = lse_ref[...].T
    qid = qid_ref[...]

    def step(t, carry):
        rows = pl.ds(pl.multiple_of(t * tile, tile), tile)
        allowed = (jnp.concatenate([kid_ref[rows, :]] * (tile // 128), axis=1) == qid) | (rel == (t - i) * tile)
        for h, (a, b) in enumerate(wins):
            key = k_ref[rows, a:b]
            s = lax.dot_general(key, queries[h], (((1,), (1,)), ((), ())), preferred_element_type=F32)
            p = jnp.exp2(jnp.where(allowed, s * (SCALING * LOG2E) - lse[h : h + 1, :], NEG))
            dp = lax.dot_general(v_ref[rows, a:b], grads[h], (((1,), (1,)), ((), ())), preferred_element_type=F32)
            ds = (p * (dp - inner[h : h + 1, :])).astype(BF)
            dv_acc[rows, a:b] += jnp.dot(p.astype(BF), grads[h], preferred_element_type=F32)
            dk_acc[rows, a:b] += jnp.dot(ds, queries[h], preferred_element_type=F32)
            dq_acc[h, :, : b - a] += lax.dot_general(ds, key, (((0,), (0,)), ((), ())), preferred_element_type=F32)
        return carry

    lax.fori_loop(lo, hi, step, 0)
    outs = []
    for h, (a, b) in enumerate(wins):
        outs.append(jnp.where(head_lanes(a, h, (tile, b - a)), dq_acc[h, :, : b - a] * SCALING, 0.0))
    for c, part in head_pieces(wins, outs):
        out_ref[here, c : c + part.shape[1]] = part.astype(BF)

    @pl.when(i == pl.num_programs(0) - 1)
    def _():
        out_ref[:, width : 2 * width] = (dk_acc[...] * SCALING).astype(BF)
        out_ref[:, 2 * width : 3 * width] = dv_acc[...].astype(BF)
        padding = out_ref.shape[1] - 3 * width
        if padding:
            out_ref[:, 3 * width :] = jnp.zeros((out_ref.shape[0], padding), BF)


def attention_backward(q, k, v, o, go_blocks, slots, lse, qid, kid, bounds, heads, tile):
    n, width = q.shape
    count = len(go_blocks)
    return pl.pallas_call(
        functools.partial(backward_kernel, heads, tile, count),
        out_shape=jax.ShapeDtypeStruct((n, lanes(3 * width)), BF),
        grid_spec=pltpu.PrefetchScalarGridSpec(
            num_scalar_prefetch=2,
            grid=(n // tile,),
            in_specs=[
                row_block(tile, width),
                whole_block((n, width)),
                whole_block((n, width)),
                row_block(tile, width),
                row_block(tile, 128),
                pl.BlockSpec((1, tile), lambda i, *_: (0, i)),
                whole_block((n, 128)),
            ]
            + [pl.BlockSpec(memory_space=pl.ANY)] * count,
            out_specs=whole_block((n, lanes(3 * width))),
            scratch_shapes=[
                pltpu.VMEM((n, width), BF),
                pltpu.VMEM((n, width), F32),
                pltpu.VMEM((n, width), F32),
                pltpu.VMEM((heads, tile, 256), F32),
                pltpu.SemaphoreType.DMA((count,)),
            ],
        ),
        compiler_params=pltpu.CompilerParams(vmem_limit_bytes=48 << 20),
        cost_estimate=pl.CostEstimate(flops=10 * n * n * 128 * heads, bytes_accessed=16 * n * width, transcendentals=n * n * heads),
        name="attention_backward",
    )(bounds, slots, q, k, v, o, lse, qid, kid, *go_blocks)


def tile_bounds(ids, tile):
    first, last = ids[::tile], ids[tile - 1 :: tile]
    lo = jnp.sum((last[None, :] < first[:, None]).astype(jnp.int32), axis=1)
    hi = jnp.sum((first[None, :] <= last[:, None]).astype(jnp.int32), axis=1)
    return jnp.stack([lo, hi])


def normalise(values):
    average = jnp.mean(values, axis=-1, keepdims=True)
    centred = values - average
    spread = jnp.mean(centred * centred, axis=-1, keepdims=True)
    inverse = lax.rsqrt(spread + EPSILON)
    return centred * inverse, inverse


def norm_back(normal, inverse, gain, grad):
    scaled = grad * gain
    first = jnp.mean(scaled, axis=-1, keepdims=True)
    second = jnp.mean(scaled * normal, axis=-1, keepdims=True)
    return (scaled - first - normal * second) * inverse


def gelu_both(u):
    root = math.sqrt(2.0 / math.pi)
    bent = jnp.tanh(root * (u + 0.044715 * u * u * u))
    half = 0.5 * (1.0 + bent)
    slope = half + 0.5 * u * (1.0 - bent * bent) * (root + 3 * 0.044715 * root * u * u)
    return u * half, slope


def dot(a, b):
    return jnp.dot(a, b, preferred_element_type=F32)


def dot_bt(a, b):
    return lax.dot_general(a, b, (((1,), (1,)), ((), ())), preferred_element_type=F32)


def dot_at(a, b):
    return lax.dot_general(a, b, (((0,), (0,)), ((), ())), preferred_element_type=F32)


def project_kernel(count, bands, slots, *refs):
    xs, pieces = refs[:count], refs[count : count + bands]
    gain, shift, q_bias, v_bias, x_out, h_out, q_out, k_out, v_out, w_out, x_now, sems = refs[count + bands :]
    j = pl.program_id(0)

    @pl.when(j == 0)
    def _():
        load_blocks(pieces, w_out, slots, count, sems)

    for i in range(count):

        @pl.when(j == i)
        def _(i=i):
            x_now[...] = xs[i][...]

    x = x_now[...]
    x_out[...] = x
    normal, _ = normalise(x.astype(F32))
    h = (normal * gain[...] + shift[...]).astype(BF)
    h_out[...] = h
    projected = dot(h, w_out[...])
    width = q_out.shape[1]
    q_out[...] = (projected[:, :width] + q_bias[...]).astype(BF)
    k_out[...] = projected[:, width : 2 * width].astype(BF)
    v_out[...] = (projected[:, 2 * width : 3 * width] + v_bias[...]).astype(BF)


def project(xs, pieces, slots, gain, shift, q_bias, v_bias):
    rows, width = xs[0].shape
    count, bands, cols = len(xs), len(pieces), q_bias.shape[1]
    n, columns = rows * count, pieces[0].shape[1]
    shape = jax.ShapeDtypeStruct
    return pl.pallas_call(
        functools.partial(project_kernel, count, bands),
        out_shape=[shape((n, width), BF)] * 2 + [shape((n, cols), BF)] * 3 + [shape((width, columns), BF)],
        grid_spec=pltpu.PrefetchScalarGridSpec(
            num_scalar_prefetch=1,
            grid=(count,),
            in_specs=[kept_block((rows, width))] * count
            + [pl.BlockSpec(memory_space=pl.ANY)] * bands
            + [kept_block((1, width))] * 2
            + [kept_block((1, cols))] * 2,
            out_specs=[slot_block(rows, width)] * 2
            + [slot_block(rows, cols)] * 3
            + [whole_block((width, columns))],
            scratch_shapes=[pltpu.VMEM((rows, width), BF), pltpu.SemaphoreType.DMA((bands,))],
        ),
        compiler_params=pltpu.CompilerParams(vmem_limit_bytes=48 << 20),
        cost_estimate=pl.CostEstimate(flops=2 * n * width * columns, bytes_accessed=8 * n * width, transcendentals=n),
        name="norm_project",
    )(slots, *xs, *pieces, gain, shift, q_bias, v_bias)


def widen_kernel(count, bands, slots, x_ref, *refs):
    os, pieces = refs[:count], refs[count : count + bands]
    (out_bias, gain, shift, w_up, up_bias, x_out, o_out, h_out, a_out, slope_out, w_out, o_now, sems) = refs[count + bands :]
    j = pl.program_id(0)
    cols = os[0].shape[1]

    @pl.when(j == 0)
    def _():
        load_blocks(pieces, w_out, slots, count, sems)

    for v in range(count):

        @pl.when(slots[0] == v)
        def _(v=v):
            for i in range(count):
                o_now[:, (v ^ i) * cols : (v ^ i) * cols + cols] = os[i][...]

    o = o_now[...]
    x = x_ref[...].astype(F32) + (dot(o, w_out[...]) + out_bias[...])

    @pl.when(j == 0)
    def _():
        x_out[...] = x
        o_out[...] = o

    normal, _ = normalise(x)
    h = (normal * gain[...] + shift[...]).astype(BF)
    h_out[...] = h
    value, slope = gelu_both(dot(h, w_up[...]) + up_bias[...])
    a_out[...] = value.astype(BF)
    slope_out[...] = slope


def widen(x_all, os, pieces, slots, out_bias, gain, shift, w_up, up_bias, rows):
    n, width = x_all.shape
    count, bands, cols, hidden = len(os), len(pieces), os[0].shape[1], w_up.shape[1]
    shape = jax.ShapeDtypeStruct
    return pl.pallas_call(
        functools.partial(widen_kernel, count, bands),
        out_shape=[
            shape((rows, width), F32),
            shape((rows, width), BF),
            shape((n, width), BF),
            shape((n, hidden), BF),
            shape((n, hidden), F32),
            shape((width, width), BF),
        ],
        grid_spec=pltpu.PrefetchScalarGridSpec(
            num_scalar_prefetch=1,
            grid=(count,),
            in_specs=[slot_block(rows, width)]
            + [slot_block(rows, cols)] * count
            + [pl.BlockSpec(memory_space=pl.ANY)] * bands
            + [kept_block((1, width))] * 3
            + [kept_block((width, hidden)), kept_block((1, hidden))],
            out_specs=[whole_block((rows, width))] * 2
            + [row_block(rows, width)]
            + [row_block(rows, hidden)] * 2
            + [whole_block((width, width))],
            scratch_shapes=[pltpu.VMEM((rows, width), BF), pltpu.SemaphoreType.DMA((bands,))],
        ),
        compiler_params=pltpu.CompilerParams(vmem_limit_bytes=56 << 20),
        cost_estimate=pl.CostEstimate(flops=2 * n * width * (width + hidden), bytes_accessed=16 * n * width, transcendentals=n * hidden),
        name="out_norm_up",
    )(slots, x_all, *os, *pieces, out_bias, gain, shift, w_up, up_bias)


def narrow_kernel(gy_ref, a_ref, slope_ref, w_up, w_down, gu_out, dh_out, y_out, sum_out):
    @pl.when(pl.program_id(0) == 0)
    def _():
        sum_out[...] = jnp.zeros_like(sum_out)

    gu = (dot(gy_ref[...], w_down[...]) * slope_ref[...]).astype(BF)
    gu_out[...] = gu
    dh_out[...] = dot_bt(gu, w_up[...]).astype(BF)
    y_out[...] = dot_bt(a_ref[...], w_down[...]).astype(BF)
    sum_out[...] += jnp.sum(gu.astype(F32), axis=0, keepdims=True)


def narrow(gy, active, slope, w_up, w_down, rows):
    n, width = gy.shape
    hidden = w_up.shape[1]
    shape = jax.ShapeDtypeStruct
    return pl.pallas_call(
        narrow_kernel,
        out_shape=[shape((n, hidden), BF), shape((n, width), BF), shape((n, width), BF), shape((1, hidden), F32)],
        grid_spec=pl.GridSpec(
            grid=(n // rows,),
            in_specs=[row_block(rows, width)] + [row_block(rows, hidden)] * 2 + [kept_block((width, hidden))] * 2,
            out_specs=[row_block(rows, hidden)] + [row_block(rows, width)] * 2 + [whole_block((1, hidden))],
        ),
        compiler_params=pltpu.CompilerParams(vmem_limit_bytes=56 << 20),
        cost_estimate=pl.CostEstimate(flops=6 * n * width * hidden, bytes_accessed=16 * n * width, transcendentals=0),
        name="down_and_back",
    )(gy, active, slope, w_up, w_down)


def middle_kernel(count, terms, slots, *refs):
    parts, (x_ref, gy_ref, gain, w_out, dx_out, sum_out) = refs[:terms], refs[terms : terms + 6]
    go_outs, ga_outs = refs[terms + 6 : terms + 6 + count], refs[terms + 6 + count :]
    grad = sum(part[...].astype(F32) for part in parts)
    normal, inverse = normalise(x_ref[...])
    dx = gy_ref[...].astype(F32) + norm_back(normal, inverse, gain[...], grad)
    dx_out[...] = dx
    ga = dx.astype(BF)
    sum_out[0:1, :] = jnp.sum(grad * normal, axis=0, keepdims=True)
    sum_out[1:2, :] = jnp.sum(grad, axis=0, keepdims=True)
    sum_out[2:3, :] = jnp.sum(ga.astype(F32), axis=0, keepdims=True)
    go = dot_bt(ga, w_out[...]).astype(BF)
    cols = go_outs[0].shape[1]
    for v in range(count):

        @pl.when(slots[0] == v)
        def _(v=v):
            for i in range(count):
                start = (v ^ i) * cols
                go_outs[i][...] = go[:, start : start + cols]
                ga_outs[i][...] = ga[:, start : start + cols]


def middle(parts, x_one, gy, gain, w_out, slots, count):
    rows, width = x_one.shape
    cols, terms = width // count, len(parts)
    shape = jax.ShapeDtypeStruct
    block = kept_block((rows, width))
    outs = pl.pallas_call(
        functools.partial(middle_kernel, count, terms),
        out_shape=[shape((rows, width), F32), shape((8, width), F32)] + [shape((rows, cols), BF)] * (2 * count),
        grid_spec=pltpu.PrefetchScalarGridSpec(
            num_scalar_prefetch=1,
            grid=(1,),
            in_specs=[block] * (terms + 2) + [kept_block((1, width)), kept_block((width, width))],
            out_specs=[whole_block((rows, width)), whole_block((8, width))] + [whole_block((rows, cols))] * (2 * count),
        ),
        compiler_params=pltpu.CompilerParams(vmem_limit_bytes=48 << 20),
        cost_estimate=pl.CostEstimate(flops=2 * rows * width * width, bytes_accessed=20 * rows * width, transcendentals=rows),
        name="norm_back_out",
    )(slots, *parts, x_one, gy, gain, w_out)
    return outs[0], outs[1], outs[2 : 2 + count], outs[2 + count :]


def swap(value, axis, bits):
    size = lax.axis_size(axis)
    return lax.ppermute(value, axis, [(i, i ^ bits) for i in range(size)])


def seq_gather(block):
    size = lax.axis_size("seq")
    got = [None] * size
    got[0] = block
    for far in range(2, size, 2):
        got[far] = swap(block, "seq", far)
    for j in range(0, size, 2):
        got[j + 1] = swap(got[j], "seq", 1)
    return got


def seq_scatter(part):
    size = lax.axis_size("seq")
    terms = []
    for j in [*range(2, size, 2), 0]:
        terms.append(swap(part(j + 1).astype(BF), "seq", 1))
    totals = []
    for j, got in zip(range(2, size, 2), terms):
        held = (part(j).astype(F32) + got.astype(F32)).astype(BF)
        totals.append(swap(held, "seq", j))
    return [part(0), terms[-1], *totals]


def add_up(terms):
    return sum(term.astype(F32) for term in terms)


def ring_order(size):
    half = size // 2
    return [2 * p if p < half else 2 * (size - 1 - p) + 1 for p in range(size)]


def ring_index(pos, size):
    pos = pos % size
    return jnp.where(pos < size // 2, 2 * pos, 2 * (size - 1 - pos) + 1)


def ring_perms(size):
    order = ring_order(size)
    ahead = [(order[p], order[(p + 1) % size]) for p in range(size)]
    return ahead, [(b, a) for a, b in ahead]


def ring_position(size):
    f = lax.axis_index("fsdp")
    return jnp.where(f % 2 == 0, f // 2, size - 1 - f // 2)


def ring_gather(block):
    size = lax.axis_size("fsdp")
    ahead, back = ring_perms(size)
    pos = ring_position(size)
    pieces, owners = [block], [ring_index(pos, size)]
    one, two = block, block
    for t in range(1, size // 2 + 1):
        one = lax.ppermute(one, "fsdp", ahead)
        pieces.append(one)
        owners.append(ring_index(pos - t, size))
        if t < size // 2:
            two = lax.ppermute(two, "fsdp", back)
            pieces.append(two)
            owners.append(ring_index(pos + t, size))
    return pieces, owners


def ring_scatter_sum(part):
    size = lax.axis_size("fsdp")
    ahead, back = ring_perms(size)
    pos = ring_position(size)
    half = size // 2
    one = part(ring_index(pos + half, size)).astype(BF)
    two = part(ring_index(pos - (half - 1), size)).astype(BF)
    for t in range(1, half):
        one = lax.ppermute(one, "fsdp", ahead)
        one = (one.astype(F32) + part(ring_index(pos + half - t, size))).astype(BF)
        two = lax.ppermute(two, "fsdp", back)
        if t < half - 1:
            two = (two.astype(F32) + part(ring_index(pos - (half - 1) + t, size))).astype(BF)
    one = lax.ppermute(one, "fsdp", ahead)
    return part(ring_index(pos, size)) + one.astype(F32) + two.astype(F32)


def total_sum(vector):
    for axis in ("seq", "fsdp"):
        bits = 1
        while bits < lax.axis_size(axis):
            vector = vector + swap(vector, axis, bits)
            bits *= 2
    return vector


def local(
    inputs, image_ids, pad_mask, cotangent, w_qkv, w_out, w_up, w_down, ln1_gain, ln1_shift,
    q_bias, v_bias, out_bias, ln2_gain, ln2_shift, up_bias, down_bias,
):
    ns, nf = lax.axis_size("seq"), lax.axis_size("fsdp")
    s, f = lax.axis_index("seq"), lax.axis_index("fsdp")
    rows, width = inputs.shape[1:]
    n = rows * ns
    hidden = w_up.shape[1]
    mine = hidden // ns
    wide = lanes(mine)
    cols = width // ns
    band = w_up.shape[0]
    ratio = nf // ns
    heads = HEADS // ns
    tile = 256
    order = [s ^ j for j in range(ns)]

    def pad_lanes(array, size):
        return jnp.pad(array, ((0, 0), (0, size - array.shape[1])))

    down_t = w_down.T
    both = ("seq", "fsdp")
    pieces = []
    for c in range(ratio):
        perm = []
        for ss in range(ns):
            for ff in range(nf):
                e = (ff % ratio - c) % ratio
                perm.append((ss * nf + ff, (ff // ratio) * nf + ratio * ss + e))
        e = (f % ratio - c) % ratio
        piece = lax.dynamic_slice_in_dim(down_t, (ratio * s + e) * band, band, axis=0)
        pieces.append(lax.ppermute(piece, both, perm))
    blocks = []
    for h in range(ratio):
        block = pieces[0]
        for c in range(1, ratio):
            block = jnp.where((f % ratio + c) % ratio == h, pieces[c], block)
        blocks.append(block)
    down_mine = pad_lanes(jnp.concatenate(blocks, axis=1), wide)

    x_own = inputs[0]
    x_blocks = seq_gather(x_own)
    code_blocks = seq_gather(image_ids * 2 + pad_mask)
    qkv_mine = pad_lanes(
        jnp.concatenate(
            [lax.dynamic_slice_in_dim(w_qkv, t * width + s * cols, cols, axis=1) for t in range(3)], axis=1
        ),
        lanes(3 * cols),
    )
    qkv_pieces, owners = ring_gather(qkv_mine)
    out_pieces, _ = ring_gather(w_out)
    slots = jnp.stack([jnp.asarray(i, jnp.int32) for i in order + owners])
    up_mine = pad_lanes(lax.dynamic_slice_in_dim(w_up, s * mine, mine, axis=1), wide)
    full_up = lax.all_gather(up_mine, "fsdp", axis=0, tiled=True)
    full_down = lax.all_gather(down_mine, "fsdp", axis=0, tiled=True)

    keep = (1 - pad_mask[0]).astype(F32)[:, None]
    gy_own = (cotangent[0].astype(F32) * keep).astype(BF)
    gy_rel = jnp.concatenate(seq_gather(gy_own), axis=0)

    codes = jnp.zeros((n,), jnp.int32)
    for j in range(ns):
        codes = lax.dynamic_update_slice(codes, code_blocks[j][0], (order[j] * rows,))
    ids = codes // 2
    key_ids = jnp.where(codes % 2 == 0, ids, -1)
    bounds = tile_bounds(ids, tile)
    ids_col = jnp.broadcast_to(ids[:, None], (n, 128))
    keys_col = jnp.broadcast_to(key_ids[:, None], (n, 128))

    def row(vector):
        return vector[None, :]

    q_part = row(lax.dynamic_slice_in_dim(q_bias, s * cols, cols))
    v_part = row(lax.dynamic_slice_in_dim(v_bias, s * cols, cols))
    x_all, h_one, q, k, v, full_qkv = project(x_blocks, qkv_pieces, slots, row(ln1_gain), row(ln1_shift), q_part, v_part)
    o, lse = attention_forward(q, k, v, ids_col, key_ids[None], bounds, heads, tile)

    up_part = pad_lanes(row(lax.dynamic_slice_in_dim(up_bias, s * mine, mine)), wide)
    x_one, o_own, h_two, active, slope, full_out = widen(
        x_all, seq_gather(o), out_pieces, slots, row(out_bias), row(ln2_gain), row(ln2_shift), full_up, up_part, rows
    )
    gu, dh_two, mixed, sum_up = narrow(gy_rel, active, slope, full_up, full_down, rows)

    def block_of(array):
        return lambda j: array[j * rows : (j + 1) * rows]

    dx_one, sums_two, go_parts, ga_parts = middle(
        seq_scatter(block_of(dh_two)), x_one, gy_own, row(ln2_gain), full_out, slots, ns
    )
    go_blocks = [part if j == 0 else swap(part, "seq", j) for j, part in enumerate(go_parts)]

    gqkv = attention_backward(q, k, v, o, go_blocks, slots, lse, ids[None], keys_col, bounds, heads, tile)
    grad_qkv_part = dot_at(h_one, gqkv).astype(BF)
    dh_one_part = dot_bt(gqkv, full_qkv).astype(BF)

    layer_out = (x_one + add_up(seq_scatter(block_of(mixed))) + down_bias).astype(BF)
    grad_up_part = dot_at(h_two, gu).astype(BF)
    grad_down_part = dot_at(gy_rel, active).astype(BF)
    sum_down_bias = jnp.sum(gy_own.astype(F32), axis=0)

    def bands(*arrays):
        return lambda owner: jnp.stack(
            [lax.dynamic_slice_in_dim(a, owner * band, band, axis=0).astype(F32) for a in arrays]
        )

    grad_up, grad_down_t = ring_scatter_sum(bands(grad_up_part, grad_down_part))
    grad_up = grad_up[:, :mine]
    grad_down_t = grad_down_t[:, :mine].astype(BF)
    grad_out_part = add_up(seq_scatter(lambda j: dot_at(o_own, ga_parts[j]))).astype(BF)
    grad_out = ring_scatter_sum(bands(grad_out_part))[0]

    got = []
    for c in range(ratio):
        perm = []
        for ss in range(ns):
            for ff in range(nf):
                h = (ff % ratio + c) % ratio
                perm.append((ss * nf + ff, (ff // ratio) * nf + ratio * ss + h))
        h = (f % ratio + c) % ratio
        piece = lax.dynamic_slice_in_dim(grad_down_t, h * w_down.shape[0], w_down.shape[0], axis=1)
        got.append(lax.ppermute(piece, both, perm))
    blocks = []
    for e in range(ratio):
        block = got[0]
        for c in range(1, ratio):
            block = jnp.where((e + c) % ratio == f % ratio, got[c], block)
        blocks.append(block)
    grad_down = jnp.concatenate(blocks, axis=0).T.astype(F32)

    def rows_of(array):
        return lambda j: lax.dynamic_slice_in_dim(array, order[j] * rows, rows, axis=0)

    dh_one = add_up(seq_scatter(rows_of(dh_one_part)))
    normal_x, inverse_x = normalise(x_own.astype(F32))
    sum_ln1_gain = jnp.sum(dh_one * normal_x, axis=0)
    sum_ln1_shift = jnp.sum(dh_one, axis=0)
    grad_inputs = (dx_one + norm_back(normal_x, inverse_x, ln1_gain, dh_one)).astype(BF)

    grad_qkv_mine = ring_scatter_sum(bands(grad_qkv_part))[0].astype(BF)
    thirds = [grad_qkv_mine[:, t * cols : (t + 1) * cols] for t in range(3)]
    got = []
    for p in range(3):
        perm = [((3 * d + p) % ns, d) for d in range(ns)]
        section = [0] * ns
        for d in range(ns):
            section[(3 * d + p) % ns] = (3 * d + p) // ns
        which = sum(jnp.where(s == i, t, 0) for i, t in enumerate(section))
        piece = jnp.where(which == 0, thirds[0], jnp.where(which == 1, thirds[1], thirds[2]))
        got.append(lax.ppermute(piece, "seq", perm))
    grad_qkv = jnp.concatenate(got, axis=1).astype(F32)

    def spread(vector, size, start):
        return lax.dynamic_update_slice(jnp.zeros((size,), F32), vector, (start,))

    sum_qkv = jnp.sum(gqkv.astype(F32), axis=0)
    sum_q = spread(sum_qkv[:cols], width, s * cols)
    sum_v = spread(sum_qkv[2 * cols : 3 * cols], width, s * cols)
    sum_hidden = spread(sum_up[0, :mine], hidden, s * mine)
    vectors = [sum_ln1_gain, sum_ln1_shift, sum_q, sum_v, sums_two[2], sums_two[0], sums_two[1], sum_hidden, sum_down_bias]
    totals = total_sum(jnp.concatenate(vectors))
    sums, start = [], 0
    for vector in vectors:
        sums.append(totals[start : start + vector.shape[0]])
        start += vector.shape[0]
    return (layer_out[None], grad_inputs[None], grad_qkv, grad_out, grad_up, grad_down, *sums)


def solution(mesh):
    tokens, weights, shared = P("fsdp", "seq", None), P("fsdp", None), P()
    marks, grads = P("fsdp", "seq"), P("fsdp", "seq")
    return jax.shard_map(
        local,
        mesh=mesh,
        in_specs=(tokens, marks, marks, tokens) + (weights,) * 4 + (shared,) * 9,
        out_specs=(tokens, tokens) + (grads,) * 4 + (shared,) * 9,
        check_vma=False,
    )
```

```python
import functools
import math

import jax
import jax.numpy as jnp
from jax import lax
from jax.experimental import pallas as pl
from jax.experimental.pallas import tpu as pltpu
from jax.sharding import PartitionSpec as P

HEADS = 16
HD = 72
EPSILON = 1e-06
SCALING = HD ** (-0.5)
LOG2E = math.log2(math.e)
NEG = -1e30
BF = jnp.bfloat16
F32 = jnp.float32


def windows(heads, width):
    out = []
    for h in range(heads):
        lo = h * HD // 128 * 128
        out.append((lo, min(width, -(-(h * HD + HD) // 128) * 128)))
    return out


def head_lanes(lo, h, shape):
    lane = lax.broadcasted_iota(jnp.int32, shape, 1) + lo
    return (lane >= h * HD) & (lane < h * HD + HD)


def head_pieces(wins, outs):
    pieces = {}
    for (lo, hi), out in zip(wins, outs):
        for c in range(lo, hi, 128):
            part = out[:, c - lo : min(c + 128, hi) - lo]
            pieces[c] = part if c not in pieces else pieces[c] + part
    return pieces.items()


def lanes(width):
    return -(-width // 128) * 128


def load_blocks(blocks, target, slots, first, sems):
    rows = blocks[0].shape[0]
    copies = []
    for i, block in enumerate(blocks):
        start = pl.multiple_of(slots[first + i] * rows, 8)
        copies.append(pltpu.make_async_copy(block, target.at[pl.ds(start, rows)], sems.at[i]))
        copies[-1].start()
    for copy in copies:
        copy.wait()


def marks(code):
    ids = lax.shift_right_logical(code, 1)
    keys = jnp.where((code & 1) == 0, ids, -1)
    return ids.astype(F32), keys.astype(F32)


def key_tiles(mine, ids, tile):
    before = jnp.sum(jnp.where(ids < jnp.min(mine), 1.0, 0.0)).astype(jnp.int32)
    upto = jnp.sum(jnp.where(ids <= jnp.max(mine), 1.0, 0.0)).astype(jnp.int32)
    return before // tile, (upto + tile - 1) // tile


def column(row, width):
    return jnp.broadcast_to(row, (width, row.shape[1])).T


def forward_kernel(heads, tile, q_ref, k_ref, v_ref, code_ref, o_ref, lse_ref, s_ref):
    i = pl.program_id(0)
    mine, _ = marks(code_ref[0:1, pl.ds(pl.multiple_of(i * tile, tile), tile)])
    lo, hi = key_tiles(mine, marks(code_ref[0:1, :])[0], tile)
    wins = windows(heads, q_ref.shape[1])
    rel = lax.broadcasted_iota(jnp.int32, (tile, tile), 0) - lax.broadcasted_iota(jnp.int32, (tile, tile), 1)
    qid = jnp.concatenate([column(mine, 128)] * (tile // 128), axis=1)
    queries = []
    for h, (a, b) in enumerate(wins):
        w = q_ref[:, a:b]
        queries.append(jnp.where(head_lanes(a, h, w.shape), w, jnp.zeros_like(w)))

    def scores(t, tops):
        rows = pl.ds(pl.multiple_of(t * tile, tile), tile)
        allowed = (qid == marks(code_ref[0:1, rows])[1]) | (rel == (t - i) * tile)
        new = []
        for h, (a, b) in enumerate(wins):
            s = lax.dot_general(queries[h], k_ref[rows, a:b], (((1,), (1,)), ((), ())), preferred_element_type=F32)
            s = jnp.where(allowed, s * (SCALING * LOG2E), NEG)
            s_ref[h, :, rows] = s
            top = tops[h]
            for c in range(0, tile, 128):
                top = jnp.maximum(top, s[:, c : c + 128])
            new.append(top)
        return tuple(new)

    tops = lax.fori_loop(lo, hi, scores, tuple(jnp.full((tile, 128), NEG, F32) for _ in range(heads)))
    tops = [jnp.broadcast_to(jnp.max(t, axis=1, keepdims=True), (tile, 128)) for t in tops]

    def attend(t, carry):
        rows = pl.ds(pl.multiple_of(t * tile, tile), tile)
        new = []
        for h, (a, b) in enumerate(wins):
            total, acc = carry[h]
            p = jnp.exp2(s_ref[h, :, rows] - jnp.concatenate([tops[h]] * (tile // 128), axis=1))
            for c in range(0, tile, 128):
                total = total + p[:, c : c + 128]
            acc = acc + jnp.dot(p.astype(BF), v_ref[rows, a:b], preferred_element_type=F32)
            new.append((total, acc))
        return tuple(new)

    start = tuple((jnp.zeros((tile, 128), F32), jnp.zeros((tile, b - a), F32)) for a, b in wins)
    carry = lax.fori_loop(lo, hi, attend, start)
    lane = lax.broadcasted_iota(jnp.int32, (tile, 128), 1)
    lse = jnp.zeros((tile, 128), F32)
    outs = []
    for h, (a, b) in enumerate(wins):
        total = jnp.sum(carry[h][0], axis=1, keepdims=True)
        out = carry[h][1] * (1.0 / total)
        outs.append(jnp.where(head_lanes(a, h, out.shape), out, 0.0))
        lse = jnp.where(lane == h, tops[h] + jnp.log2(total), lse)
    for c, part in head_pieces(wins, outs):
        o_ref[c : c + part.shape[1], :] = part.T.astype(BF)
    lse_ref[...] = lse.T[: lse_ref.shape[0], :]


def whole_block(shape):
    return pl.BlockSpec(shape, lambda *_: (0, 0))


def kept_block(shape):
    return pl.BlockSpec(shape, lambda *_: (0, 0), pipeline_mode=pl.Buffered(1))


def row_block(tile, width):
    return pl.BlockSpec((tile, width), lambda i, *_: (i, 0))


def lane_block(height, tile):
    return pl.BlockSpec((height, tile), lambda i, *_: (0, i))


def slot_block(tile, width):
    return pl.BlockSpec((tile, width), lambda i, slots: (slots[i], 0))


def attention_forward(q, k, v, code, heads, tile):
    n, width = q.shape
    return pl.pallas_call(
        functools.partial(forward_kernel, heads, tile),
        out_shape=(jax.ShapeDtypeStruct((width, n), BF), jax.ShapeDtypeStruct((8, n), F32)),
        grid_spec=pl.GridSpec(
            grid=(n // tile,),
            in_specs=[row_block(tile, width), whole_block((n, width)), whole_block((n, width)), whole_block((8, n))],
            out_specs=[lane_block(width, tile), lane_block(8, tile)],
            scratch_shapes=[pltpu.VMEM((heads, tile, n), F32)],
        ),
        compiler_params=pltpu.CompilerParams(vmem_limit_bytes=56 << 20),
        cost_estimate=pl.CostEstimate(flops=4 * n * n * 128 * heads, bytes_accessed=10 * n * width, transcendentals=n * n * heads),
        name="attention_forward",
    )(q, k, v, code)


def backward_kernel(
    heads, tile, count, first, slots, q_ref, k_ref, v_ref, o_ref, lse_ref, code_ref, *refs
):
    blocks, (out_ref, go_ref, dk_acc, dv_acc, dq_acc, kid_ref, sems) = refs[:count], refs[count:]
    i = pl.program_id(0)
    qid, _ = marks(code_ref[0:1, pl.ds(pl.multiple_of(i * tile, tile), tile)])
    lo, hi = key_tiles(qid, marks(code_ref[0:1, :])[0], tile)
    width = q_ref.shape[1]
    wins = windows(heads, width)

    @pl.when(i == 0)
    def _():
        load_blocks(blocks, go_ref, slots, 0, sems)
        dk_acc[...] = jnp.zeros_like(dk_acc)
        dv_acc[...] = jnp.zeros_like(dv_acc)
        for t in range(0, kid_ref.shape[0], tile):
            kid_ref[t : t + tile, :] = column(marks(code_ref[0:1, t : t + tile])[1], 128)

    here = pl.ds(pl.multiple_of(i * tile, tile), tile)
    rel = lax.broadcasted_iota(jnp.int32, (tile, tile), 1) - lax.broadcasted_iota(jnp.int32, (tile, tile), 0)
    go = go_ref[here, first : first + width]
    product = go.astype(F32).T * o_ref[...].astype(F32)
    inner = [jnp.sum(product[h * HD : (h + 1) * HD, :], axis=0, keepdims=True) for h in range(heads)]
    queries, grads = [], []
    for h, (a, b) in enumerate(wins):
        w, g = q_ref[:, a:b], go[:, a:b]
        on = head_lanes(a, h, w.shape)
        queries.append(jnp.where(on, w, jnp.zeros_like(w)))
        g = jnp.where(on, g, jnp.zeros_like(g))
        grads.append(g)
        dq_acc[h, :, : b - a] = jnp.zeros((tile, b - a), F32)
    lse = lse_ref[...]

    def step(t, carry):
        rows = pl.ds(pl.multiple_of(t * tile, tile), tile)
        allowed = (jnp.concatenate([kid_ref[rows, :]] * (tile // 128), axis=1) == qid) | (rel == (t - i) * tile)
        for h, (a, b) in enumerate(wins):
            key = k_ref[rows, a:b]
            s = lax.dot_general(key, queries[h], (((1,), (1,)), ((), ())), preferred_element_type=F32)
            p = jnp.exp2(jnp.where(allowed, s * (SCALING * LOG2E) - lse[h : h + 1, :], NEG))
            dp = lax.dot_general(v_ref[rows, a:b], grads[h], (((1,), (1,)), ((), ())), preferred_element_type=F32)
            ds = (p * (dp - inner[h])).astype(BF)
            dv_acc[rows, a:b] += jnp.dot(p.astype(BF), grads[h], preferred_element_type=F32)
            dk_acc[rows, a:b] += jnp.dot(ds, queries[h], preferred_element_type=F32)
            dq_acc[h, :, : b - a] += lax.dot_general(ds, key, (((0,), (0,)), ((), ())), preferred_element_type=F32)
        return carry

    lax.fori_loop(lo, hi, step, 0)
    outs = []
    for h, (a, b) in enumerate(wins):
        outs.append(jnp.where(head_lanes(a, h, (tile, b - a)), dq_acc[h, :, : b - a] * SCALING, 0.0))
    for c, part in head_pieces(wins, outs):
        out_ref[here, c : c + part.shape[1]] = part.astype(BF)

    @pl.when(i == pl.num_programs(0) - 1)
    def _():
        out_ref[:, width : 2 * width] = (dk_acc[...] * SCALING).astype(BF)
        out_ref[:, 2 * width : 3 * width] = dv_acc[...].astype(BF)


def attention_backward(q, k, v, o, go_blocks, first, slots, lse, code, heads, tile):
    n, width = q.shape
    count = len(go_blocks)
    return pl.pallas_call(
        functools.partial(backward_kernel, heads, tile, count, first),
        out_shape=jax.ShapeDtypeStruct((n, 3 * width), BF),
        grid_spec=pltpu.PrefetchScalarGridSpec(
            num_scalar_prefetch=1,
            grid=(n // tile,),
            in_specs=[
                row_block(tile, width),
                whole_block((n, width)),
                whole_block((n, width)),
                lane_block(width, tile),
                lane_block(8, tile),
                whole_block((8, n)),
            ]
            + [pl.BlockSpec(memory_space=pl.ANY)] * count,
            out_specs=whole_block((n, 3 * width)),
            scratch_shapes=[
                pltpu.VMEM((n, go_blocks[0].shape[1]), BF),
                pltpu.VMEM((n, width), F32),
                pltpu.VMEM((n, width), F32),
                pltpu.VMEM((heads, tile, 256), F32),
                pltpu.VMEM((n, 128), F32),
                pltpu.SemaphoreType.DMA((count,)),
            ],
        ),
        compiler_params=pltpu.CompilerParams(vmem_limit_bytes=56 << 20),
        cost_estimate=pl.CostEstimate(flops=10 * n * n * 128 * heads, bytes_accessed=16 * n * width, transcendentals=n * n * heads),
        name="attention_backward",
    )(slots, q, k, v, o, lse, code, *go_blocks)


def normalise(values):
    average = jnp.mean(values, axis=-1, keepdims=True)
    centred = values - average
    spread = jnp.mean(centred * centred, axis=-1, keepdims=True)
    inverse = lax.rsqrt(spread + EPSILON)
    return centred * inverse, inverse


def norm_back(normal, inverse, gain, grad):
    scaled = grad * gain
    first = jnp.mean(scaled, axis=-1, keepdims=True)
    second = jnp.mean(scaled * normal, axis=-1, keepdims=True)
    return (scaled - first - normal * second) * inverse


def gelu_both(u):
    root = math.sqrt(2.0 / math.pi)
    bent = jnp.tanh(root * (u + 0.044715 * u * u * u))
    half = 0.5 * (1.0 + bent)
    slope = half + 0.5 * u * (1.0 - bent * bent) * (root + 3 * 0.044715 * root * u * u)
    return u * half, slope


def dot(a, b):
    return jnp.dot(a, b, preferred_element_type=F32)


def dot_bt(a, b):
    return lax.dot_general(a, b, (((1,), (1,)), ((), ())), preferred_element_type=F32)


def dot_at(a, b):
    return lax.dot_general(a, b, (((0,), (0,)), ((), ())), preferred_element_type=F32)


def project_kernel(counts, bands, slots, *refs):
    xs, pieces = refs[: sum(counts)], refs[sum(counts) : sum(counts) + bands]
    gain, shift, q_bias, v_bias, x_out, h_out, q_out, k_out, v_out, w_out, out_out, code_out, x_now, sems = refs[
        sum(counts) + bands :
    ]
    j = pl.program_id(0)
    rows, cols = q_out.shape

    @pl.when(j == 0)
    def _():
        load_blocks(pieces, w_out, slots, len(counts), sems)
        out_out[:, :cols] = w_out[:, 3 * cols :]

    at = 0
    for i, count in enumerate(counts):

        @pl.when(j == i)
        def _(parts=xs[at : at + count]):
            start = 0
            for part in parts:
                size = min(part.shape[0], rows - start)
                x_now[start : start + size, :] = part[:size, :]
                start += size
            last = parts[-1].shape[0] - 16
            code = parts[-1][last:, :rows].astype(F32)[0:1, :]
            code_out[...] = jnp.broadcast_to(code, code_out.shape).astype(jnp.int32)

        at += count
    x = x_now[...]
    x_out[...] = x
    normal, _ = normalise(x.astype(F32))
    h = (normal * gain[...] + shift[...]).astype(BF)
    h_out[...] = h
    projected = dot(h, w_out[...])
    q_out[...] = (projected[:, :cols] + q_bias[...]).astype(BF)
    k_out[...] = projected[:, cols : 2 * cols].astype(BF)
    v_out[...] = (projected[:, 2 * cols : 3 * cols] + v_bias[...]).astype(BF)


def project(xs, pieces, slots, gain, shift, q_bias, v_bias, rows):
    width, cols, bands = xs[0][0].shape[1], q_bias.shape[1], len(pieces)
    counts = tuple(len(parts) for parts in xs)
    xs = [part for parts in xs for part in parts]
    n, columns = rows * len(counts), pieces[0].shape[1]
    shape = jax.ShapeDtypeStruct
    return pl.pallas_call(
        functools.partial(project_kernel, counts, bands),
        out_shape=[shape((n, width), BF)] * 2
        + [shape((n, cols), BF)] * 3
        + [shape((width, columns), BF), shape((width, lanes(cols)), BF), shape((8, n), jnp.int32)],
        grid_spec=pltpu.PrefetchScalarGridSpec(
            num_scalar_prefetch=1,
            grid=(len(counts),),
            in_specs=[kept_block(part.shape) for part in xs]
            + [pl.BlockSpec(memory_space=pl.ANY)] * bands
            + [kept_block((1, width))] * 2
            + [kept_block((1, cols))] * 2,
            out_specs=[slot_block(rows, width)] * 2
            + [slot_block(rows, cols)] * 3
            + [
                whole_block((width, columns)),
                whole_block((width, lanes(cols))),
                pl.BlockSpec((8, rows), lambda i, slots: (0, slots[i])),
            ],
            scratch_shapes=[pltpu.VMEM((rows, width), BF), pltpu.SemaphoreType.DMA((bands,))],
        ),
        compiler_params=pltpu.CompilerParams(vmem_limit_bytes=56 << 20),
        cost_estimate=pl.CostEstimate(flops=2 * n * width * columns, bytes_accessed=8 * n * width, transcendentals=n),
        name="norm_project",
    )(slots, *xs, *pieces, gain, shift, q_bias, v_bias)


def widen_kernel(count, slots, x_ref, *refs):
    os, w_outs = refs[:count], refs[count : 2 * count]
    (out_bias, gain, shift, w_up, up_bias, x_out, o_out, h_out, a_out, slope_out, w_out) = refs[2 * count :]
    j = pl.program_id(0)
    cols = os[0].shape[0]
    for v in range(count):

        @pl.when((j == 0) & (slots[0] == v))
        def _(v=v):
            for i in range(count):
                start = (v ^ i) * cols
                w_out[:, start : start + cols] = w_outs[i][:, :cols]

    for i in range(count):
        o_out[pl.ds(pl.multiple_of(slots[i] * cols, 8), cols), :] = os[i][...]
    x = x_ref[...].astype(F32) + (dot_at(o_out[...], w_out[...]) + out_bias[...])

    @pl.when(j == 0)
    def _():
        x_out[...] = x

    normal, _ = normalise(x)
    h = (normal * gain[...] + shift[...]).astype(BF)
    h_out[...] = h
    value, slope = gelu_both(dot(h, w_up[...]) + up_bias[...])
    a_out[...] = value.astype(BF)
    slope_out[...] = slope


def widen(x_all, os, w_outs, slots, out_bias, gain, shift, w_up, up_bias, rows):
    n, width = x_all.shape
    count, cols, hidden = len(os), os[0].shape[0], up_bias.shape[1]
    shape = jax.ShapeDtypeStruct
    return pl.pallas_call(
        functools.partial(widen_kernel, count),
        out_shape=[
            shape((rows, width), F32),
            shape((width, n), BF),
            shape((n, width), BF),
            shape((n, hidden), BF),
            shape((n, hidden), F32),
            shape((width, width), BF),
        ],
        grid_spec=pltpu.PrefetchScalarGridSpec(
            num_scalar_prefetch=1,
            grid=(count,),
            in_specs=[slot_block(rows, width)]
            + [pl.BlockSpec((cols, rows), lambda i, slots: (0, slots[i]))] * count
            + [kept_block(w_outs[0].shape)] * count
            + [kept_block((1, width))] * 3
            + [kept_block((width, hidden)), kept_block((1, hidden))],
            out_specs=[whole_block((rows, width)), lane_block(width, rows), slot_block(rows, width)]
            + [slot_block(rows, hidden)] * 2
            + [whole_block((width, width))],
        ),
        compiler_params=pltpu.CompilerParams(vmem_limit_bytes=60 << 20),
        cost_estimate=pl.CostEstimate(flops=2 * n * width * (width + hidden), bytes_accessed=16 * n * width, transcendentals=n * hidden),
        name="out_norm_up",
    )(slots, x_all, *os, *w_outs, out_bias, gain, shift, w_up, up_bias)


def narrow_kernel(slots, gy_ref, a_ref, slope_ref, w_up, w_down, *refs):
    gu_out, y_out, dh_out, sum_out = refs[-4:]

    @pl.when(pl.program_id(0) == 0)
    def _():
        sum_out[...] = jnp.zeros_like(sum_out)

    gu = (dot_bt(gy_ref[...], w_down[...]) * slope_ref[...]).astype(BF)
    gu_out[...] = gu
    dh_out[...] = dot_bt(gu, w_up[...]).astype(BF)
    y_out[...] = dot(a_ref[...], w_down[...]).astype(BF)
    sum_out[...] += jnp.sum(gu.astype(F32), axis=0, keepdims=True)


def narrow(gy, active, slope, w_up, w_down, slots, rows, first, count, carried):
    n, width = gy.shape
    hidden = w_up.shape[1]
    shape = jax.ShapeDtypeStruct

    def block(size):
        return pl.BlockSpec((rows, size), lambda i, slots: (slots[first + i], 0))

    return pl.pallas_call(
        narrow_kernel,
        out_shape=[shape((n, hidden), BF), shape((n, width), BF), shape((rows * count, width), BF), shape((1, hidden), F32)],
        grid_spec=pltpu.PrefetchScalarGridSpec(
            num_scalar_prefetch=1,
            grid=(count,),
            in_specs=[block(width), block(hidden), block(hidden)]
            + [kept_block((width, hidden)), kept_block((hidden, width))]
            + [pl.BlockSpec(memory_space=pl.ANY)] * len(carried),
            out_specs=[block(hidden), block(width), row_block(rows, width), whole_block((1, hidden))],
        ),
        input_output_aliases={6 + i: i for i in range(len(carried))},
        compiler_params=pltpu.CompilerParams(vmem_limit_bytes=56 << 20),
        cost_estimate=pl.CostEstimate(flops=6 * rows * count * width * hidden, bytes_accessed=16 * rows * count * width, transcendentals=0),
        name="down_and_back",
    )(slots, gy, active, slope, w_up, w_down, *carried)


def finish_kernel(slots, g_ref, x_ref, w_qkv, dh_out, sum_out, bias_out):
    @pl.when(pl.program_id(0) == 0)
    def _():
        sum_out[...] = jnp.zeros_like(sum_out)
        bias_out[...] = jnp.zeros_like(bias_out)

    g = g_ref[...]
    dh = dot_bt(g, w_qkv[:, : g.shape[1]])
    dh_out[...] = dh.astype(BF)
    normal, _ = normalise(x_ref[...].astype(F32))
    sum_out[0:1, :] += jnp.sum(dh * normal, axis=0, keepdims=True)
    sum_out[1:2, :] += jnp.sum(dh, axis=0, keepdims=True)
    bias_out[...] += jnp.sum(g.astype(F32), axis=0, keepdims=True)


def finish(gqkv, x_all, w_qkv, slots, rows):
    n, width = x_all.shape
    columns = gqkv.shape[1]
    shape = jax.ShapeDtypeStruct
    return pl.pallas_call(
        finish_kernel,
        out_shape=[shape((n, width), BF), shape((8, width), F32), shape((1, columns), F32)],
        grid_spec=pltpu.PrefetchScalarGridSpec(
            num_scalar_prefetch=1,
            grid=(n // rows,),
            in_specs=[slot_block(rows, columns), slot_block(rows, width), kept_block(w_qkv.shape)],
            out_specs=[row_block(rows, width), whole_block((8, width)), whole_block((1, columns))],
        ),
        compiler_params=pltpu.CompilerParams(vmem_limit_bytes=56 << 20),
        cost_estimate=pl.CostEstimate(flops=2 * n * width * columns, bytes_accessed=8 * n * width, transcendentals=n),
        name="project_back",
    )(slots, gqkv, x_all, w_qkv)


def weigh_kernel(count, h_ref, g_ref, o_ref, *refs):
    gas, (out_ref, ga_now) = refs[:count], refs[count:]
    rows = gas[0].shape[0]

    @pl.when(pl.program_id(0) == 0)
    def _():
        for i in range(count):
            ga_now[i * rows : (i + 1) * rows, :] = gas[i][...]

    columns = g_ref.shape[1]
    out_ref[:, :columns] = dot_at(h_ref[...], g_ref[...]).astype(BF)
    out_ref[:, columns:] = dot(o_ref[...], ga_now[...]).astype(BF)


def weigh(h_one, gqkv, o_all, gas):
    n, width = h_one.shape
    rows, cols = gas[0].shape
    columns, tile = gqkv.shape[1], width // 3
    return pl.pallas_call(
        functools.partial(weigh_kernel, len(gas)),
        out_shape=jax.ShapeDtypeStruct((width, columns + cols), BF),
        grid_spec=pl.GridSpec(
            grid=(width // tile,),
            in_specs=[lane_block(n, tile), kept_block((n, columns)), row_block(tile, n)] + [kept_block((rows, cols))] * len(gas),
            out_specs=row_block(tile, columns + cols),
            scratch_shapes=[pltpu.VMEM((n, cols), BF)],
        ),
        compiler_params=pltpu.CompilerParams(vmem_limit_bytes=56 << 20),
        cost_estimate=pl.CostEstimate(flops=2 * n * width * (columns + cols), bytes_accessed=6 * n * width, transcendentals=0),
        name="grads_qkv_out",
    )(h_one, gqkv, o_all, *gas)


def middle_kernel(count, terms, slots, *refs):
    parts, (x_ref, gy_ref, gain, w_out, dx_out, sum_out) = refs[:terms], refs[terms : terms + 6]
    go_outs, ga_outs = refs[terms + 6 : terms + 6 + count], refs[terms + 6 + count :]
    grad = sum(part[...].astype(F32) for part in parts)
    normal, inverse = normalise(x_ref[...])
    dx = gy_ref[...].astype(F32) + norm_back(normal, inverse, gain[...], grad)
    dx_out[...] = dx
    ga = dx.astype(BF)
    sum_out[0:1, :] = jnp.sum(grad * normal, axis=0, keepdims=True)
    sum_out[1:2, :] = jnp.sum(grad, axis=0, keepdims=True)
    sum_out[2:3, :] = jnp.sum(ga.astype(F32), axis=0, keepdims=True)
    go = dot_bt(ga, w_out[...]).astype(BF)
    cols = go_outs[0].shape[1]
    for v in range(count):

        @pl.when(slots[0] == v)
        def _(v=v):
            for i in range(count):
                start = (v ^ i) * cols
                go_outs[i][...] = go[:, start : start + cols]
                ga_outs[i][...] = ga[:, start : start + cols]


def middle(parts, x_one, gy, gain, w_out, slots, count):
    rows, width = x_one.shape
    cols, terms = width // count, len(parts)
    shape = jax.ShapeDtypeStruct
    block = kept_block((rows, width))
    outs = pl.pallas_call(
        functools.partial(middle_kernel, count, terms),
        out_shape=[shape((rows, width), F32), shape((8, width), F32)] + [shape((rows, cols), BF)] * (2 * count),
        grid_spec=pltpu.PrefetchScalarGridSpec(
            num_scalar_prefetch=1,
            grid=(1,),
            in_specs=[block] * (terms + 2) + [kept_block((1, width)), kept_block((width, width))],
            out_specs=[whole_block((rows, width)), whole_block((8, width))] + [whole_block((rows, cols))] * (2 * count),
        ),
        compiler_params=pltpu.CompilerParams(vmem_limit_bytes=56 << 20),
        cost_estimate=pl.CostEstimate(flops=2 * rows * width * width, bytes_accessed=20 * rows * width, transcendentals=rows),
        name="norm_back_out",
    )(slots, *parts, x_one, gy, gain, w_out)
    return outs[0], outs[1], outs[2 : 2 + count], outs[2 + count :]


def swap(value, axis, bits):
    size = lax.axis_size(axis)
    return lax.ppermute(value, axis, [(i, i ^ bits) for i in range(size)])


def hold(values, *earlier):
    return lax.optimization_barrier((values, earlier))[0]


def far_swaps(block):
    return [swap(block, "seq", j) for j in range(2, lax.axis_size("seq"), 2)]


def near_swaps(blocks):
    return [swap(block, "seq", 1) for block in blocks]


def woven(own, near):
    return [block for pair in zip(own, near) for block in pair]


def add_up(terms):
    return sum(term.astype(F32) for term in terms)


def ring_order(size):
    half = size // 2
    return [2 * p if p < half else 2 * (size - 1 - p) + 1 for p in range(size)]


def ring_index(pos, size):
    pos = pos % size
    return jnp.where(pos < size // 2, 2 * pos, 2 * (size - 1 - pos) + 1)


def ring_perms(size):
    order = ring_order(size)
    ahead = [(order[p], order[(p + 1) % size]) for p in range(size)]
    return ahead, [(b, a) for a, b in ahead]


def ring_position(size):
    f = lax.axis_index("fsdp")
    return jnp.where(f % 2 == 0, f // 2, size - 1 - f // 2)


class RingGather:
    def __init__(self, block):
        self.size = lax.axis_size("fsdp")
        self.ahead, self.back = ring_perms(self.size)
        self.pos = ring_position(self.size)
        self.pieces = [block]
        self.one = self.two = block
        self.done = 0

    def indices(self):
        owners = [ring_index(self.pos, self.size)]
        for t in range(1, self.size // 2 + 1):
            owners.append(ring_index(self.pos - t, self.size))
            if t < self.size // 2:
                owners.append(ring_index(self.pos + t, self.size))
        return owners

    def hop(self, *earlier):
        one, two = hold((self.one, self.two), earlier)
        self.done += 1
        self.one = lax.ppermute(one, "fsdp", self.ahead)
        new = [self.one]
        self.pieces.append(self.one)
        if self.done < self.size // 2:
            self.two = lax.ppermute(two, "fsdp", self.back)
            new.append(self.two)
            self.pieces.append(self.two)
        return new


class RingSum:
    def __init__(self, part):
        self.part = part
        self.size = lax.axis_size("fsdp")
        self.half = self.size // 2
        self.ahead, self.back = ring_perms(self.size)
        self.pos = ring_position(self.size)
        self.done = 0
        self.one = self.term(self.half).astype(BF)
        self.two = self.term(1 - self.half).astype(BF)

    def term(self, away):
        return self.part(ring_index(self.pos + away, self.size))

    def hop(self, *earlier):
        one, two = hold((self.one, self.two), earlier)
        self.done += 1
        t, half = self.done, self.half
        one = lax.ppermute(one, "fsdp", self.ahead)
        if t < half:
            two = lax.ppermute(two, "fsdp", self.back)
        self.one, self.two = one, two
        return [one] if t == half else [one, two]

    def add(self, *earlier):
        one, two = hold((self.one, self.two), earlier)
        t, half = self.done, self.half
        self.one = (one.astype(F32) + self.term(half - t)).astype(BF)
        if t < half - 1:
            self.two = (two.astype(F32) + self.term(t + 1 - half)).astype(BF)
        return [self.one, self.two]

    def result(self):
        return self.term(0) + self.one.astype(F32) + self.two.astype(F32)


class TotalSum:
    def __init__(self, vector):
        self.vector = vector
        self.steps = []
        for axis in ("seq", "fsdp"):
            bits = 1
            while bits < lax.axis_size(axis):
                self.steps.append((axis, bits))
                bits *= 2

    def hop(self, *earlier):
        vector = hold(self.vector, earlier)
        axis, bits = self.steps.pop(0)
        self.vector = vector + swap(vector, axis, bits)
        return [self.vector]


def local(
    inputs, image_ids, pad_mask, cotangent, w_qkv, w_out, w_up, w_down, ln1_gain, ln1_shift,
    q_bias, v_bias, out_bias, ln2_gain, ln2_shift, up_bias, down_bias,
):
    ns, nf = lax.axis_size("seq"), lax.axis_size("fsdp")
    s = lax.axis_index("seq")
    rows, width = inputs.shape[1:]
    n = rows * ns
    cols = width // ns
    band = w_up.shape[0]
    strip = w_down.shape[0]
    wide = lanes(-(-strip // ns) * nf)
    sub = wide // nf
    heads = HEADS // ns
    tile = 256
    order = [s ^ j for j in range(ns)]
    slots = jnp.stack([jnp.asarray(i, jnp.int32) for i in order])
    hops = nf // 8

    def row(vector):
        return vector[None, :]

    def own(vector):
        return lax.dynamic_slice_in_dim(vector, s * cols, cols)

    def own_hidden(array):
        count = array.shape[0]
        array = array.reshape(count, nf, strip)
        array = jnp.pad(array, ((0, 0), (0, 0), (0, ns * sub - strip)))
        return lax.dynamic_slice_in_dim(array, s * sub, sub, axis=2).reshape(count, wide)

    first = [lax.dynamic_slice_in_dim(w_qkv, t * width + s * cols, cols, axis=1) for t in range(3)]
    first.append(lax.dynamic_slice_in_dim(w_out, s * cols, cols, axis=1))
    ring_one = RingGather(jnp.concatenate(first, axis=1))
    x_own = inputs[0]
    code = (image_ids * 2 + pad_mask).astype(BF)
    x_pack = jnp.concatenate([x_own, jnp.pad(code, ((0, 15), (0, width - rows)))], axis=0)
    split = rows // 2
    x_parts = hold([x_pack[:split], x_pack[split:]], ring_one.one)
    far_a = far_swaps(x_parts[0])
    done = [far_a, *[ring_one.hop(x_parts) for _ in range(hops)]]
    up_mine = own_hidden(w_up)
    keep = (1 - pad_mask[0]).astype(F32)[:, None]
    gy_own = (cotangent[0].astype(F32) * keep).astype(BF)
    gy_parts = [gy_own[:split], gy_own[split:]]
    down_mine = lax.dynamic_slice_in_dim(jnp.pad(w_down, ((0, ns * sub - strip), (0, 0))), s * sub, sub, axis=0)
    up_part = own_hidden(row(up_bias))
    q_part, v_part = row(own(q_bias)), row(own(v_bias))
    one_slots = jnp.stack([jnp.asarray(i, jnp.int32) for i in order + ring_one.indices()])
    done = [*done, up_mine]

    far_b, gy_parts, slots, one_slots = hold((x_parts[1], gy_parts, slots, one_slots), *done)
    far_b = far_swaps(far_b)
    done = [far_b, gy_parts, slots, one_slots, *[ring_one.hop(*done) for _ in range(hops)]]
    full_up = lax.all_gather(hold(up_mine, *done), "fsdp", axis=0, tiled=True)
    down_mine, up_part, q_part, v_part = hold((down_mine, up_part, q_part, v_part), *done)
    x_pack, far_a, far_b = hold((x_pack, far_a, far_b), *done)
    near, near_a, near_b = near_swaps([x_pack]), near_swaps(far_a), near_swaps(far_b)
    done = [near, near_a, near_b, down_mine, up_part, q_part, v_part, *[ring_one.hop(*done) for _ in range(hops)]]
    x_blocks = [[x_pack], [near[0]]]
    for i in range(ns // 2 - 1):
        x_blocks += [[far_a[i], far_b[i]], [near_a[i], near_b[i]]]
    gy_far_a = far_swaps(hold(gy_parts[0], *done))
    done = [gy_far_a, *[ring_one.hop(*done) for _ in range(hops)]]

    x_blocks, pieces, gy_parts = hold((x_blocks, ring_one.pieces, gy_parts), *done)
    gy_far_b = far_swaps(gy_parts[1])
    x_all, h_one, q, k, v, full_qkv, out_cols, code = project(
        x_blocks, pieces, one_slots, row(ln1_gain), row(ln1_shift), q_part, v_part, rows
    )
    done = [gy_far_b, q, out_cols]
    full_down = lax.all_gather(hold(down_mine, q), "fsdp", axis=0, tiled=True)

    q, k, v, out_cols, gy_parts, gy_far_a, gy_far_b = hold((q, k, v, out_cols, gy_parts, gy_far_a, gy_far_b), *done)
    out_far = far_swaps(out_cols)
    gy_near = [near_swaps([gy_parts[0], *gy_far_a]), near_swaps([gy_parts[1], *gy_far_b])]
    done = [out_far, gy_near]
    o, lse = attention_forward(q, k, v, code, heads, tile)
    o, out_row = hold((o, [out_cols, *out_far]), *done)
    o_row = [o, *far_swaps(o)]
    w_outs = woven(out_row, near_swaps(out_row))
    gy_all = jnp.zeros((n, width), BF)
    gy_rows = [woven([gy_parts[h], *far], near) for h, (far, near) in enumerate(zip((gy_far_a, gy_far_b), gy_near))]
    for h in range(2):
        for j in range(ns):
            gy_all = lax.dynamic_update_slice(gy_all, gy_rows[h][j], (order[j] * rows + h * split, 0))
    done = [o_row, w_outs, gy_all]
    o_row = hold(o_row, *done)
    os = woven(o_row, near_swaps(o_row))

    x_one, o_all, h_two, active, slope, full_out = widen(
        x_all, os, w_outs, slots, row(out_bias), row(ln2_gain), row(ln2_shift), full_up, up_part, rows
    )
    gu, mixed, far_dh, far_sum = narrow(gy_all, active, slope, full_up, full_down, slots, rows, 2, ns - 2, ())

    def cut(array, j):
        return array[j * rows : (j + 1) * rows]

    def summed(a, b):
        return (a.astype(F32) + b.astype(F32)).astype(BF)

    far_near = near_swaps([cut(far_dh, j + 1) for j in range(0, ns - 2, 2)])
    far_held = [summed(cut(far_dh, 2 * i), got) for i, got in enumerate(far_near)]
    gu, mixed, far_held = hold((gu, mixed, far_held))
    terms = [swap(held, "seq", 2 * i + 2) for i, held in enumerate(far_held)]
    gu, mixed, near_dh, near_sum = narrow(gy_all, active, slope, full_up, full_down, slots, rows, 0, 2, (gu, mixed))
    near_dh, gy_all, active = hold((near_dh, gy_all, active))
    terms += [cut(near_dh, 0), swap(cut(near_dh, 1), "seq", 1)]
    grad_down_part = dot_at(active, gy_all).astype(BF)
    down_sum = lax.psum_scatter(grad_down_part, "fsdp", scatter_dimension=0, tiled=True)
    terms = hold(terms, grad_down_part)
    dx_one, sums_two, go_parts, ga_parts = middle(terms, x_one, gy_own, row(ln2_gain), full_out, slots, ns)
    go_parts, h_two, gu, mixed = hold((go_parts, h_two, gu, mixed))
    go_blocks = [block if j == 0 else swap(block, "seq", j) for j, block in enumerate(go_parts)]
    grad_up_part = dot_at(h_two, gu).astype(BF)
    up_sum = lax.psum_scatter(grad_up_part, "fsdp", scatter_dimension=0, tiled=True)

    def mixed_block(j):
        return lax.dynamic_slice_in_dim(mixed, order[j] * rows, rows, axis=0)

    mixed_near = near_swaps([mixed_block(j + 1) for j in range(0, ns, 2)])
    mixed_held = [summed(mixed_block(2 * i), mixed_near[i]) for i in range(1, ns // 2)]
    done = [go_blocks, grad_up_part, mixed_near, mixed_held]
    q, k, v, go_blocks, ga_parts, mixed_held = hold((q, k, v, go_blocks, ga_parts, mixed_held), *done)
    ga_blocks = [block if j == 0 else swap(block, "seq", j) for j, block in enumerate(ga_parts)]
    mixed_far = [swap(block, "seq", 2 * i + 2) for i, block in enumerate(mixed_held)]
    gqkv = attention_backward(q, k, v, o, go_blocks, 0, slots, lse, code, heads, tile)

    gqkv, ga_blocks, mixed_far = hold((gqkv, ga_blocks, mixed_far))
    grad_part = weigh(h_one, gqkv, o_all, ga_blocks)

    def bands(owner):
        return lax.dynamic_slice_in_dim(grad_part, owner * band, band, axis=0).astype(F32)

    ring_sum = RingSum(bands)
    gqkv = hold(gqkv, ring_sum.one, ring_sum.two)

    def ring_round(*earlier):
        new = []
        for _ in range(hops):
            if ring_sum.done:
                ring_sum.add(*earlier)
            new.append(ring_sum.hop(*earlier))
        return new

    done = [ring_round(gqkv)]
    dh_one_part, sums_one, sum_qkv = finish(gqkv, x_all, full_qkv, slots, rows)

    def spread(vector):
        return lax.dynamic_update_slice(jnp.zeros((width,), F32), vector, (s * cols,))

    def spread_hidden(vector):
        shifted = lax.dynamic_update_slice(jnp.zeros((nf, ns * sub), F32), vector.reshape(nf, sub), (0, s * sub))
        return shifted[:, :strip].reshape(nf * strip)

    sum_down_bias = jnp.sum(gy_own.astype(F32), axis=0)
    sum_hidden = spread_hidden((far_sum + near_sum)[0])
    vectors = [
        sums_one[0], sums_one[1], spread(sum_qkv[0, :cols]), spread(sum_qkv[0, 2 * cols :]), sums_two[2],
        sums_two[0], sums_two[1], sum_hidden, sum_down_bias,
    ]
    totals = TotalSum(jnp.concatenate(vectors))
    done += [dh_one_part]
    dh_one_part = hold(dh_one_part, *done)
    dh_near = near_swaps([cut(dh_one_part, j + 1) for j in range(0, ns, 2)])
    done = [dh_near, ring_round(*done), totals.hop(*done)]
    dh_near = hold(dh_near, *done)
    dh_held = [summed(cut(dh_one_part, 2 * i), dh_near[i]) for i in range(1, ns // 2)]
    dh_far_a = [swap(block[:split], "seq", 2 * i + 2) for i, block in enumerate(dh_held)]
    done = [dh_far_a, ring_round(*done)]
    dh_held = hold(dh_held, *done)
    dh_far_b = [swap(block[split:], "seq", 2 * i + 2) for i, block in enumerate(dh_held)]
    done = [dh_far_b, ring_round(*done)]
    total = totals.hop(*done)

    mine = hold(ring_sum.result(), *done)
    grad_out = mine[:, 3 * cols :]
    thirds = [mine[:, t * cols : (t + 1) * cols].astype(BF) for t in range(3)]
    got = []
    for p in range(3):
        perm = [((3 * d + p) % ns, d) for d in range(ns)]
        section = [0] * ns
        for d in range(ns):
            section[(3 * d + p) % ns] = (3 * d + p) // ns
        which = sum(jnp.where(s == i, t, 0) for i, t in enumerate(section))
        piece = jnp.where(which == 0, thirds[0], jnp.where(which == 1, thirds[1], thirds[2]))
        got.append(lax.ppermute(piece, "seq", perm))
    grad_qkv = jnp.concatenate(got, axis=1).astype(F32)
    while totals.steps:
        total = totals.hop(total)

    ratio = nf // ns

    def up_piece(j):
        return lax.dynamic_slice_in_dim(up_sum, order[j] * (ratio * sub), ratio * sub, axis=1)

    def down_piece(j):
        return lax.dynamic_slice_in_dim(down_sum, order[j] * cols, cols, axis=1)

    ups = jnp.zeros((ns, band, ratio * sub), BF)
    downs = jnp.zeros((ns, sub, cols), BF)
    for j in range(ns):
        a, b = up_piece(j), down_piece(j)
        if j:
            a, b = swap(a, "seq", j), swap(b, "seq", j)
        ups = lax.dynamic_update_slice(ups, a[None], (order[j], 0, 0))
        downs = lax.dynamic_update_slice(downs, b[None], (order[j], 0, 0))
    grad_up = jnp.concatenate(
        [
            jnp.concatenate([ups[i, :, h * sub : (h + 1) * sub] for i in range(ns)], axis=1)[:, :strip]
            for h in range(ratio)
        ],
        axis=1,
    ).astype(F32)
    grad_down = downs.reshape(ns * sub, cols)[:strip].astype(F32)

    dh_far = [jnp.concatenate(pair, axis=0) for pair in zip(dh_far_a, dh_far_b)]
    dh_one = add_up([cut(dh_one_part, 0), dh_near[0], *dh_far])
    normal_x, inverse_x = normalise(x_own.astype(F32))
    grad_inputs = (dx_one + norm_back(normal_x, inverse_x, ln1_gain, dh_one)).astype(BF)
    layer_out = (x_one + add_up([mixed_block(0), mixed_near[0], *mixed_far]) + down_bias).astype(BF)
    sums, start = [], 0
    for vector in vectors:
        sums.append(totals.vector[start : start + vector.shape[0]])
        start += vector.shape[0]
    return (layer_out[None], grad_inputs[None], grad_qkv, grad_out, grad_up, grad_down, *sums)


def solution(mesh):
    tokens, weights, shared = P("fsdp", "seq", None), P("fsdp", None), P()
    marks, grads = P("fsdp", "seq"), P("fsdp", "seq")
    return jax.shard_map(
        local,
        mesh=mesh,
        in_specs=(tokens, marks, marks, tokens) + (weights,) * 4 + (shared,) * 9,
        out_specs=(tokens, tokens) + (grads,) * 4 + (shared,) * 9,
        check_vma=False,
    )
```

```python
import functools
import math

import jax
import jax.numpy as jnp
from jax import lax
from jax.experimental import pallas as pl
from jax.experimental.pallas import tpu as pltpu
from jax.sharding import PartitionSpec as P

HEADS = 16
HD = 72
IMG_TOK = 729
EPSILON = 1e-06
SCALING = HD ** (-0.5)
LOG2E = math.log2(math.e)
NEG = -1e30
BF = jnp.bfloat16
F32 = jnp.float32


def windows(heads, width):
    out = []
    for h in range(heads):
        lo = h * HD // 128 * 128
        out.append((lo, min(width, -(-(h * HD + HD) // 128) * 128)))
    return out


def head_lanes(lo, h, shape):
    lane = lax.broadcasted_iota(jnp.int32, shape, 1) + lo
    return (lane >= h * HD) & (lane < h * HD + HD)


def head_pieces(wins, outs):
    pieces = {}
    for (lo, hi), out in zip(wins, outs):
        for c in range(lo, hi, 128):
            part = out[:, c - lo : min(c + 128, hi) - lo]
            pieces[c] = part if c not in pieces else pieces[c] + part
    return pieces.items()


def lanes(width):
    return -(-width // 128) * 128


def load_blocks(blocks, target, slots, first, sems):
    rows = blocks[0].shape[0]
    copies = []
    for i, block in enumerate(blocks):
        start = pl.multiple_of(slots[first + i] * rows, 8)
        copies.append(pltpu.make_async_copy(block, target.at[pl.ds(start, rows)], sems.at[i]))
        copies[-1].start()
    for copy in copies:
        copy.wait()


def marks(code):
    ids = lax.shift_right_logical(code, 1)
    keys = jnp.where((code & 1) == 0, ids, -1)
    return ids.astype(F32), keys.astype(F32)


def key_tiles(mine, ids, tile):
    before = jnp.sum(jnp.where(ids < jnp.min(mine), 1.0, 0.0)).astype(jnp.int32)
    upto = jnp.sum(jnp.where(ids <= jnp.max(mine), 1.0, 0.0)).astype(jnp.int32)
    return before // tile, (upto + tile - 1) // tile


def most_tiles(tile, length):
    return min(length // tile, -(-(tile + 2 * IMG_TOK) // tile) + 1)


def column(row, width):
    return jnp.broadcast_to(row, (width, row.shape[1])).T


def forward_kernel(heads, tile, q_ref, k_ref, v_ref, code_ref, o_ref, lse_ref):
    i = pl.program_id(0)
    mine, _ = marks(code_ref[0:1, pl.ds(pl.multiple_of(i * tile, tile), tile)])
    lo, hi = key_tiles(mine, marks(code_ref[0:1, :])[0], tile)
    wins = windows(heads, q_ref.shape[1])

    def attend(count):
        size = count * tile
        rows = pl.ds(pl.multiple_of(lo * tile, tile), size)
        rel = lax.broadcasted_iota(jnp.int32, (tile, size), 0) - lax.broadcasted_iota(jnp.int32, (tile, size), 1)
        allowed = (jnp.concatenate([column(mine, 128)] * (size // 128), axis=1) == marks(code_ref[0:1, rows])[1]) | (rel == (lo - i) * tile)
        lane = lax.broadcasted_iota(jnp.int32, (tile, 128), 1)
        lse = jnp.zeros((tile, 128), F32)
        outs = []

        def scores(h):
            a, b = wins[h]
            w = q_ref[:, a:b]
            w = jnp.where(head_lanes(a, h, w.shape), w, jnp.zeros_like(w))
            return dot_bt(w, k_ref[rows, a:b])

        raw = scores(0)
        for h, (a, b) in enumerate(wins):
            s = jnp.where(allowed, raw * (SCALING * LOG2E), NEG)
            if h + 1 < heads:
                raw = scores(h + 1)
            top = jnp.max(s, axis=1, keepdims=True)
            p = jnp.exp2(s - top)
            total = jnp.sum(p, axis=1, keepdims=True)
            out = jnp.dot(p.astype(BF), v_ref[rows, a:b], preferred_element_type=F32) * (1.0 / total)
            outs.append(jnp.where(head_lanes(a, h, out.shape), out, 0.0))
            lse = jnp.where(lane == h, top + jnp.log2(total), lse)
        for c, part in head_pieces(wins, outs):
            o_ref[c : c + part.shape[1], :] = part.T.astype(BF)
        lse_ref[...] = lse.T[: lse_ref.shape[0], :]

    for count in range(1, most_tiles(tile, k_ref.shape[0]) + 1):
        pl.when(hi - lo == count)(functools.partial(attend, count))


def whole_block(shape):
    return pl.BlockSpec(shape, lambda *_: (0, 0))


def kept_block(shape):
    return pl.BlockSpec(shape, lambda *_: (0, 0), pipeline_mode=pl.Buffered(1))


def row_block(tile, width):
    return pl.BlockSpec((tile, width), lambda i, *_: (i, 0))


def lane_block(height, tile):
    return pl.BlockSpec((height, tile), lambda i, *_: (0, i))


def slot_block(tile, width):
    return pl.BlockSpec((tile, width), lambda i, slots: (slots[i], 0))


def attention_forward(q, k, v, code, heads, tile):
    n, width = q.shape
    return pl.pallas_call(
        functools.partial(forward_kernel, heads, tile),
        out_shape=(jax.ShapeDtypeStruct((width, n), BF), jax.ShapeDtypeStruct((8, n), F32)),
        grid_spec=pl.GridSpec(
            grid=(n // tile,),
            in_specs=[row_block(tile, width), whole_block((n, width)), whole_block((n, width)), whole_block((8, n))],
            out_specs=[lane_block(width, tile), lane_block(8, tile)],
        ),
        compiler_params=pltpu.CompilerParams(vmem_limit_bytes=56 << 20),
        cost_estimate=pl.CostEstimate(flops=4 * n * n * 128 * heads, bytes_accessed=10 * n * width, transcendentals=n * n * heads),
        name="attention_forward",
    )(q, k, v, code)


def backward_kernel(heads, tile, count, first, slots, q_ref, k_ref, v_ref, o_ref, lse_ref, code_ref, *refs):
    blocks, (out_ref, go_ref, dk_acc, dv_acc, kid_ref, sems) = refs[:count], refs[count:]
    i = pl.program_id(0)
    qid, _ = marks(code_ref[0:1, pl.ds(pl.multiple_of(i * tile, tile), tile)])
    lo, hi = key_tiles(qid, marks(code_ref[0:1, :])[0], tile)
    width = q_ref.shape[1]
    wins = windows(heads, width)

    @pl.when(i == 0)
    def _():
        load_blocks(blocks, go_ref, slots, 0, sems)
        dk_acc[...] = jnp.zeros_like(dk_acc)
        dv_acc[...] = jnp.zeros_like(dv_acc)
        for t in range(0, kid_ref.shape[0], tile):
            kid_ref[t : t + tile, :] = column(marks(code_ref[0:1, t : t + tile])[1], 128)

    here = pl.ds(pl.multiple_of(i * tile, tile), tile)

    def attend(tiles):
        size = tiles * tile
        rows = pl.ds(pl.multiple_of(lo * tile, tile), size)
        rel = lax.broadcasted_iota(jnp.int32, (size, tile), 1) - lax.broadcasted_iota(jnp.int32, (size, tile), 0)
        allowed = (jnp.concatenate([kid_ref[rows, :]] * (tile // 128), axis=1) == qid) | (rel == (lo - i) * tile)
        go = go_ref[here, first : first + width]
        product = go.astype(F32).T * o_ref[...].astype(F32)
        outs = []

        def products(h):
            a, b = wins[h]
            on = head_lanes(a, h, (tile, b - a))
            query = jnp.where(on, q_ref[:, a:b], jnp.zeros((tile, b - a), BF))
            grad = jnp.where(on, go[:, a:b], jnp.zeros((tile, b - a), BF))
            return query, grad, dot_bt(k_ref[rows, a:b], query), dot_bt(v_ref[rows, a:b], grad)

        ready = products(0)
        for h, (a, b) in enumerate(wins):
            query, grad, s, dp = ready
            if h + 1 < heads:
                ready = products(h + 1)
            inner = jnp.sum(product[h * HD : (h + 1) * HD, :], axis=0, keepdims=True)
            on = head_lanes(a, h, (tile, b - a))
            key = k_ref[rows, a:b]
            p = jnp.exp2(jnp.where(allowed, s * (SCALING * LOG2E) - lse_ref[h : h + 1, :], NEG))
            ds = (p * (dp - inner)).astype(BF)
            dv_acc[rows, a:b] += dot(p.astype(BF), grad)
            dk_acc[rows, a:b] += dot(ds, query)
            outs.append(jnp.where(on, dot_at(ds, key) * SCALING, 0.0))
        for c, part in head_pieces(wins, outs):
            out_ref[here, c : c + part.shape[1]] = part.astype(BF)

    for tiles in range(1, most_tiles(tile, k_ref.shape[0]) + 1):
        pl.when(hi - lo == tiles)(functools.partial(attend, tiles))

    @pl.when(i == pl.num_programs(0) - 1)
    def _():
        out_ref[:, width : 2 * width] = (dk_acc[...] * SCALING).astype(BF)
        out_ref[:, 2 * width : 3 * width] = dv_acc[...].astype(BF)


def attention_backward(q, k, v, o, go_blocks, first, slots, lse, code, heads, tile):
    n, width = q.shape
    count = len(go_blocks)
    return pl.pallas_call(
        functools.partial(backward_kernel, heads, tile, count, first),
        out_shape=jax.ShapeDtypeStruct((n, 3 * width), BF),
        grid_spec=pltpu.PrefetchScalarGridSpec(
            num_scalar_prefetch=1,
            grid=(n // tile,),
            in_specs=[
                row_block(tile, width),
                whole_block((n, width)),
                whole_block((n, width)),
                lane_block(width, tile),
                lane_block(8, tile),
                whole_block((8, n)),
            ]
            + [pl.BlockSpec(memory_space=pl.ANY)] * count,
            out_specs=whole_block((n, 3 * width)),
            scratch_shapes=[
                pltpu.VMEM((n, go_blocks[0].shape[1]), BF),
                pltpu.VMEM((n, width), F32),
                pltpu.VMEM((n, width), F32),
                pltpu.VMEM((n, 128), F32),
                pltpu.SemaphoreType.DMA((count,)),
            ],
        ),
        compiler_params=pltpu.CompilerParams(vmem_limit_bytes=56 << 20),
        cost_estimate=pl.CostEstimate(flops=10 * n * n * 128 * heads, bytes_accessed=16 * n * width, transcendentals=n * n * heads),
        name="attention_backward",
    )(slots, q, k, v, o, lse, code, *go_blocks)


def normalise(values):
    average = jnp.mean(values, axis=-1, keepdims=True)
    centred = values - average
    spread = jnp.mean(centred * centred, axis=-1, keepdims=True)
    inverse = lax.rsqrt(spread + EPSILON)
    return centred * inverse, inverse


def norm_back(normal, inverse, gain, grad):
    scaled = grad * gain
    first = jnp.mean(scaled, axis=-1, keepdims=True)
    second = jnp.mean(scaled * normal, axis=-1, keepdims=True)
    return (scaled - first - normal * second) * inverse


def gelu_both(u):
    root = math.sqrt(2.0 / math.pi)
    bent = jnp.tanh(root * (u + 0.044715 * u * u * u))
    half = 0.5 * (1.0 + bent)
    slope = half + 0.5 * u * (1.0 - bent * bent) * (root + 3 * 0.044715 * root * u * u)
    return u * half, slope


def dot(a, b):
    return jnp.dot(a, b, preferred_element_type=F32)


def dot_bt(a, b):
    return lax.dot_general(a, b, (((1,), (1,)), ((), ())), preferred_element_type=F32)


def dot_at(a, b):
    return lax.dot_general(a, b, (((0,), (0,)), ((), ())), preferred_element_type=F32)


def row_parts(rows):
    return [slice(0, 256), slice(256, rows)]


def project_kernel(counts, bands, slots, *refs):
    xs, pieces = refs[: sum(counts)], refs[sum(counts) : sum(counts) + bands]
    gain, shift, q_bias, v_bias, x_out, h_out, q_out, k_out, v_out, w_out, out_out, code_out, x_now, sems = refs[
        sum(counts) + bands :
    ]
    j = pl.program_id(0)
    rows, cols = q_out.shape

    @pl.when(j == 0)
    def _():
        load_blocks(pieces, w_out, slots, len(counts), sems)
        out_out[:, :cols] = w_out[:, 3 * cols :]

    at = 0
    for i, count in enumerate(counts):

        @pl.when(j == i)
        def _(parts=xs[at : at + count]):
            start = 0
            for part in parts:
                size = min(part.shape[0], rows - start)
                x_now[start : start + size, :] = part[:size, :]
                start += size
            last = parts[-1].shape[0] - 16
            code = parts[-1][last:, :rows].astype(F32)[0:1, :]
            code_out[...] = jnp.broadcast_to(code, code_out.shape).astype(jnp.int32)

        at += count
    x = x_now[...]
    x_out[...] = x
    normal, _ = normalise(x.astype(F32))
    h = (normal * gain[...] + shift[...]).astype(BF)
    h_out[...] = h
    projected = dot(h, w_out[...])
    q_out[...] = (projected[:, :cols] + q_bias[...]).astype(BF)
    k_out[...] = projected[:, cols : 2 * cols].astype(BF)
    v_out[...] = (projected[:, 2 * cols : 3 * cols] + v_bias[...]).astype(BF)


def project(xs, pieces, slots, gain, shift, q_bias, v_bias, rows):
    width, cols, bands = xs[0][0].shape[1], q_bias.shape[1], len(pieces)
    counts = tuple(len(parts) for parts in xs)
    xs = [part for parts in xs for part in parts]
    n, columns = rows * len(counts), pieces[0].shape[1]
    shape = jax.ShapeDtypeStruct
    return pl.pallas_call(
        functools.partial(project_kernel, counts, bands),
        out_shape=[shape((n, width), BF)] * 2
        + [shape((n, cols), BF)] * 3
        + [shape((width, columns), BF), shape((width, lanes(cols)), BF), shape((8, n), jnp.int32)],
        grid_spec=pltpu.PrefetchScalarGridSpec(
            num_scalar_prefetch=1,
            grid=(len(counts),),
            in_specs=[kept_block(part.shape) for part in xs]
            + [pl.BlockSpec(memory_space=pl.ANY)] * bands
            + [kept_block((1, width))] * 2
            + [kept_block((1, cols))] * 2,
            out_specs=[slot_block(rows, width)] * 2
            + [slot_block(rows, cols)] * 3
            + [
                whole_block((width, columns)),
                whole_block((width, lanes(cols))),
                pl.BlockSpec((8, rows), lambda i, slots: (0, slots[i])),
            ],
            scratch_shapes=[pltpu.VMEM((rows, width), BF), pltpu.SemaphoreType.DMA((bands,))],
        ),
        compiler_params=pltpu.CompilerParams(vmem_limit_bytes=56 << 20),
        cost_estimate=pl.CostEstimate(flops=2 * n * width * columns, bytes_accessed=8 * n * width, transcendentals=n),
        name="norm_project",
    )(slots, *xs, *pieces, gain, shift, q_bias, v_bias)


def widen_kernel(count, slots, x_ref, *refs):
    os, w_outs = refs[:count], refs[count : 2 * count]
    (out_bias, gain, shift, w_up, up_bias, x_out, o_out, h_out, a_out, slope_out, w_out) = refs[2 * count :]
    j = pl.program_id(0)
    cols = os[0].shape[0]
    for v in range(count):

        @pl.when((j == 0) & (slots[0] == v))
        def _(v=v):
            for i in range(count):
                start = (v ^ i) * cols
                w_out[:, start : start + cols] = w_outs[i][:, :cols]

    for i in range(count):
        o_out[pl.ds(pl.multiple_of(slots[i] * cols, 8), cols), :] = os[i][...]
    parts = row_parts(x_ref.shape[0])

    def branch(part):
        return dot_at(o_out[:, part], w_out[...])

    def norm(part, product):
        x = x_ref[part, :].astype(F32) + (product + out_bias[...])
        x_out[part, :] = jnp.where(j == 0, x, x_out[part, :])
        h = (normalise(x)[0] * gain[...] + shift[...]).astype(BF)
        h_out[part, :] = h
        return h

    def bend(part, u):
        value, slope = gelu_both(u + up_bias[...])
        a_out[part, :] = value.astype(BF)
        slope_out[part, :] = slope.astype(BF)

    products, us = {}, {}
    for t in range(len(parts) + 2):
        if t < len(parts):
            products[t] = branch(parts[t])
        if 0 <= t - 1 < len(parts):
            us[t - 1] = dot(norm(parts[t - 1], products[t - 1]), w_up[...])
        if 0 <= t - 2 < len(parts):
            bend(parts[t - 2], us[t - 2])


def widen(x_all, os, w_outs, slots, out_bias, gain, shift, w_up, up_bias, rows):
    n, width = x_all.shape
    count, cols, hidden = len(os), os[0].shape[0], up_bias.shape[1]
    shape = jax.ShapeDtypeStruct
    return pl.pallas_call(
        functools.partial(widen_kernel, count),
        out_shape=[
            shape((rows, width), F32),
            shape((width, n), BF),
            shape((n, width), BF),
            shape((n, hidden), BF),
            shape((n, hidden), BF),
            shape((width, width), BF),
        ],
        grid_spec=pltpu.PrefetchScalarGridSpec(
            num_scalar_prefetch=1,
            grid=(count,),
            in_specs=[slot_block(rows, width)]
            + [pl.BlockSpec((cols, rows), lambda i, slots: (0, slots[i]))] * count
            + [kept_block(w_outs[0].shape)] * count
            + [kept_block((1, width))] * 3
            + [kept_block((width, hidden)), kept_block((1, hidden))],
            out_specs=[whole_block((rows, width)), lane_block(width, rows), slot_block(rows, width)]
            + [slot_block(rows, hidden)] * 2
            + [whole_block((width, width))],
        ),
        compiler_params=pltpu.CompilerParams(vmem_limit_bytes=60 << 20),
        cost_estimate=pl.CostEstimate(flops=2 * n * width * (width + hidden), bytes_accessed=16 * n * width, transcendentals=n * hidden),
        name="out_norm_up",
    )(slots, x_all, *os, *w_outs, out_bias, gain, shift, w_up, up_bias)


def narrow_kernel(count, slots, gy_ref, a_ref, slope_ref, w_up, w_down, *refs):
    dh_outs = refs[len(refs) - 1 - count : -1]
    gu_out, y_out = refs[len(refs) - 3 - count : len(refs) - 1 - count]
    sum_out = refs[-1]

    @pl.when(pl.program_id(0) == 0)
    def _():
        sum_out[...] = jnp.zeros_like(sum_out)

    gu = (dot_bt(gy_ref[...], w_down[...]) * slope_ref[...]).astype(BF)
    gu_out[...] = gu
    dh = dot_bt(gu, w_up[...]).astype(BF)
    for i in range(count):

        @pl.when(pl.program_id(0) == i)
        def _(i=i):
            dh_outs[i][...] = dh

    y_out[...] = dot(a_ref[...], w_down[...]).astype(BF)
    sum_out[...] += jnp.sum(gu.astype(F32), axis=0, keepdims=True)


def narrow(gy, active, slope, w_up, w_down, slots, rows, first, count, carried):
    n, width = gy.shape
    hidden = w_up.shape[1]
    shape = jax.ShapeDtypeStruct

    def block(size):
        return pl.BlockSpec((rows, size), lambda i, slots: (slots[first + i], 0))

    return pl.pallas_call(
        functools.partial(narrow_kernel, count),
        out_shape=[shape((n, hidden), BF), shape((n, width), BF)]
        + [shape((rows, width), BF)] * count
        + [shape((1, hidden), F32)],
        grid_spec=pltpu.PrefetchScalarGridSpec(
            num_scalar_prefetch=1,
            grid=(count,),
            in_specs=[block(width), block(hidden), block(hidden)]
            + [kept_block((width, hidden)), kept_block((hidden, width))]
            + [pl.BlockSpec(memory_space=pl.ANY)] * len(carried),
            out_specs=[block(hidden), block(width)] + [whole_block((rows, width))] * count + [whole_block((1, hidden))],
        ),
        input_output_aliases={6 + i: i for i in range(len(carried))},
        compiler_params=pltpu.CompilerParams(vmem_limit_bytes=56 << 20),
        cost_estimate=pl.CostEstimate(flops=6 * rows * count * width * hidden, bytes_accessed=16 * rows * count * width, transcendentals=0),
        name="down_and_back",
    )(slots, gy, active, slope, w_up, w_down, *carried)


def finish_kernel(count, slots, g_ref, x_ref, w_qkv, mid_ref, far_ref, near_ref, dh_out, sum_out, bias_acc):
    j = pl.program_id(0)

    @pl.when(j == 0)
    def _():
        sum_out[...] = jnp.zeros_like(sum_out)
        bias_acc[...] = jnp.zeros_like(bias_acc)

    g = g_ref[...]
    dh = dot_bt(g, w_qkv[:, : g.shape[1]])
    dh_out[...] = dh.astype(BF)
    normal, _ = normalise(x_ref[...].astype(F32))
    sum_out[0:1, :] += jnp.sum(dh * normal, axis=0, keepdims=True)
    sum_out[1:2, :] += jnp.sum(dh, axis=0, keepdims=True)
    bias_acc[...] += jnp.sum(g.astype(F32), axis=0, keepdims=True)
    cols, wide = g.shape[1] // 3, far_ref.shape[1]

    @pl.when(j == count - 1)
    def _():
        sum_out[4:5, :] = mid_ref[2:3, :]
        sum_out[5:7, :] = mid_ref[0:2, :]
        sum_out[7:8, :] = mid_ref[3:4, :]
        for v in range(count):

            @pl.when(slots[0] == v)
            def _(v=v):
                sum_out[2:3, v * cols : (v + 1) * cols] = bias_acc[:, :cols]
                sum_out[3:4, v * cols : (v + 1) * cols] = bias_acc[:, 2 * cols :]
                sum_out[8 + v : 9 + v, :wide] = far_ref[...] + near_ref[...]


def finish(gqkv, x_all, w_qkv, mid, far_sum, near_sum, slots, rows):
    n, width = x_all.shape
    columns, count, wide = gqkv.shape[1], n // rows, far_sum.shape[1]
    height = -(-(8 + count) // 8) * 8
    shape = jax.ShapeDtypeStruct
    return pl.pallas_call(
        functools.partial(finish_kernel, count),
        out_shape=[shape((n, width), BF), shape((height, width), F32)],
        grid_spec=pltpu.PrefetchScalarGridSpec(
            num_scalar_prefetch=1,
            grid=(count,),
            in_specs=[slot_block(rows, columns), slot_block(rows, width), kept_block(w_qkv.shape)]
            + [kept_block(mid.shape), kept_block((1, wide)), kept_block((1, wide))],
            out_specs=[row_block(rows, width), whole_block((height, width))],
            scratch_shapes=[pltpu.VMEM((1, columns), F32)],
        ),
        compiler_params=pltpu.CompilerParams(vmem_limit_bytes=56 << 20),
        cost_estimate=pl.CostEstimate(flops=2 * n * width * columns, bytes_accessed=8 * n * width, transcendentals=n),
        name="project_back",
    )(slots, gqkv, x_all, w_qkv, mid, far_sum, near_sum)


def settle_kernel(count, slots, *refs):
    ups, downs, (up_out, down_out) = refs[:count], refs[count : 2 * count], refs[2 * count :]
    strip = down_out.shape[1]
    sub = downs[0].shape[0]
    ratio = ups[0].shape[1] // sub
    for v in range(count):

        @pl.when(slots[0] == v)
        def _(v=v):
            for i in range(count):
                start = (v ^ i) * sub
                size = min(sub, strip - start)
                if size > 0:
                    down_out[:, start : start + size] = downs[i][:size, :].astype(F32).T
                    for h in range(ratio):
                        piece = ups[i][:, h * sub : h * sub + size]
                        up_out[:, h * strip + start : h * strip + start + size] = piece.astype(F32)


def settle(ups, downs, slots, strip):
    band, sub, cols = ups[0].shape[0], downs[0].shape[0], downs[0].shape[1]
    ratio, count = ups[0].shape[1] // sub, len(ups)
    shape = jax.ShapeDtypeStruct
    return pl.pallas_call(
        functools.partial(settle_kernel, count),
        out_shape=[shape((band, ratio * strip), F32), shape((cols, strip), F32)],
        grid_spec=pltpu.PrefetchScalarGridSpec(
            num_scalar_prefetch=1,
            grid=(1,),
            in_specs=[kept_block(ups[0].shape)] * count + [kept_block(downs[0].shape)] * count,
            out_specs=[whole_block((band, ratio * strip)), whole_block((cols, strip))],
        ),
        compiler_params=pltpu.CompilerParams(vmem_limit_bytes=56 << 20),
        name="settle_hidden",
    )(slots, *ups, *downs)


def weigh_kernel(count, h_ref, g_ref, o_ref, *refs):
    gas, (out_ref, ga_now) = refs[:count], refs[count:]
    rows = gas[0].shape[0]

    @pl.when(pl.program_id(0) == 0)
    def _():
        for i in range(count):
            ga_now[i * rows : (i + 1) * rows, :] = gas[i][...]

    columns = g_ref.shape[1]
    out_ref[:, :columns] = dot_at(h_ref[...], g_ref[...]).astype(BF)
    out_ref[:, columns:] = dot(o_ref[...], ga_now[...]).astype(BF)


def weigh(h_one, gqkv, o_all, gas):
    n, width = h_one.shape
    rows, cols = gas[0].shape
    columns, tile = gqkv.shape[1], width // 3
    return pl.pallas_call(
        functools.partial(weigh_kernel, len(gas)),
        out_shape=jax.ShapeDtypeStruct((width, columns + cols), BF),
        grid_spec=pl.GridSpec(
            grid=(width // tile,),
            in_specs=[lane_block(n, tile), kept_block((n, columns)), row_block(tile, n)] + [kept_block((rows, cols))] * len(gas),
            out_specs=row_block(tile, columns + cols),
            scratch_shapes=[pltpu.VMEM((n, cols), BF)],
        ),
        compiler_params=pltpu.CompilerParams(vmem_limit_bytes=56 << 20),
        cost_estimate=pl.CostEstimate(flops=2 * n * width * (columns + cols), bytes_accessed=6 * n * width, transcendentals=0),
        name="grads_qkv_out",
    )(h_one, gqkv, o_all, *gas)


def middle_kernel(count, terms, slots, *refs):
    parts, (x_ref, gy_ref, gain, w_out, dx_out, sum_out) = refs[:terms], refs[terms : terms + 6]
    go_outs, ga_outs = refs[terms + 6 : terms + 6 + count], refs[terms + 6 + count :]
    grad = sum(part[...].astype(F32) for part in parts)
    normal, inverse = normalise(x_ref[...])
    dx = gy_ref[...].astype(F32) + norm_back(normal, inverse, gain[...], grad)
    dx_out[...] = dx
    ga = dx.astype(BF)
    sum_out[0:1, :] = jnp.sum(grad * normal, axis=0, keepdims=True)
    sum_out[1:2, :] = jnp.sum(grad, axis=0, keepdims=True)
    sum_out[2:3, :] = jnp.sum(ga.astype(F32), axis=0, keepdims=True)
    sum_out[3:4, :] = jnp.sum(gy_ref[...].astype(F32), axis=0, keepdims=True)
    go = dot_bt(ga, w_out[...]).astype(BF)
    cols = go_outs[0].shape[1]
    for v in range(count):

        @pl.when(slots[0] == v)
        def _(v=v):
            for i in range(count):
                start = (v ^ i) * cols
                go_outs[i][...] = go[:, start : start + cols]
                ga_outs[i][...] = ga[:, start : start + cols]


def middle(parts, x_one, gy, gain, w_out, slots, count):
    rows, width = x_one.shape
    cols, terms = width // count, len(parts)
    shape = jax.ShapeDtypeStruct
    block = kept_block((rows, width))
    outs = pl.pallas_call(
        functools.partial(middle_kernel, count, terms),
        out_shape=[shape((rows, width), F32), shape((8, width), F32)] + [shape((rows, cols), BF)] * (2 * count),
        grid_spec=pltpu.PrefetchScalarGridSpec(
            num_scalar_prefetch=1,
            grid=(1,),
            in_specs=[block] * (terms + 2) + [kept_block((1, width)), kept_block((width, width))],
            out_specs=[whole_block((rows, width)), whole_block((8, width))] + [whole_block((rows, cols))] * (2 * count),
        ),
        compiler_params=pltpu.CompilerParams(vmem_limit_bytes=56 << 20),
        cost_estimate=pl.CostEstimate(flops=2 * rows * width * width, bytes_accessed=20 * rows * width, transcendentals=rows),
        name="norm_back_out",
    )(slots, *parts, x_one, gy, gain, w_out)
    return outs[0], outs[1], outs[2 : 2 + count], outs[2 + count :]


def swap(value, axis, bits):
    size = lax.axis_size(axis)
    return lax.ppermute(value, axis, [(i, i ^ bits) for i in range(size)])


def hold(values, *earlier):
    return lax.optimization_barrier((values, earlier))[0]


def far_swaps(block):
    return [swap(block, "seq", j) for j in range(2, lax.axis_size("seq"), 2)]


def near_swaps(blocks):
    return [swap(block, "seq", 1) for block in blocks]


def woven(own, near):
    return [block for pair in zip(own, near) for block in pair]


def add_up(terms):
    return sum(term.astype(F32) for term in terms)


def ring_order(size):
    half = size // 2
    return [2 * p if p < half else 2 * (size - 1 - p) + 1 for p in range(size)]


def ring_index(pos, size):
    pos = pos % size
    return jnp.where(pos < size // 2, 2 * pos, 2 * (size - 1 - pos) + 1)


def ring_perms(size):
    order = ring_order(size)
    ahead = [(order[p], order[(p + 1) % size]) for p in range(size)]
    return ahead, [(b, a) for a, b in ahead]


def ring_position(size):
    f = lax.axis_index("fsdp")
    return jnp.where(f % 2 == 0, f // 2, size - 1 - f // 2)


class RingGather:
    def __init__(self, block):
        self.size = lax.axis_size("fsdp")
        self.ahead, self.back = ring_perms(self.size)
        self.pos = ring_position(self.size)
        self.pieces = [block]
        self.one = self.two = block
        self.done = 0

    def indices(self):
        owners = [ring_index(self.pos, self.size)]
        for t in range(1, self.size // 2 + 1):
            owners.append(ring_index(self.pos - t, self.size))
            if t < self.size // 2:
                owners.append(ring_index(self.pos + t, self.size))
        return owners

    def hop(self, *earlier):
        one, two = hold((self.one, self.two), earlier)
        self.done += 1
        self.one = lax.ppermute(one, "fsdp", self.ahead)
        new = [self.one]
        self.pieces.append(self.one)
        if self.done < self.size // 2:
            self.two = lax.ppermute(two, "fsdp", self.back)
            new.append(self.two)
            self.pieces.append(self.two)
        return new


class RingSum:
    def __init__(self, part):
        self.part = part
        self.size = lax.axis_size("fsdp")
        self.half = self.size // 2
        self.ahead, self.back = ring_perms(self.size)
        self.pos = ring_position(self.size)
        self.done = 0
        self.one = self.term(self.half).astype(BF)
        self.two = self.term(1 - self.half).astype(BF)

    def term(self, away):
        return self.part(ring_index(self.pos + away, self.size))

    def hop(self, *earlier):
        one, two = hold((self.one, self.two), earlier)
        self.done += 1
        t, half = self.done, self.half
        one = lax.ppermute(one, "fsdp", self.ahead)
        if t < half:
            two = lax.ppermute(two, "fsdp", self.back)
        self.one, self.two = one, two
        return [one] if t == half else [one, two]

    def add(self, *earlier):
        one, two = hold((self.one, self.two), earlier)
        t, half = self.done, self.half
        self.one = (one.astype(F32) + self.term(half - t)).astype(BF)
        if t < half - 1:
            self.two = (two.astype(F32) + self.term(t + 1 - half)).astype(BF)
        return [self.one, self.two]

    def result(self):
        return self.term(0) + self.one.astype(F32) + self.two.astype(F32)


class TotalSum:
    def __init__(self, vector):
        self.vector = vector
        self.steps = []
        for axis in ("seq", "fsdp"):
            bits = 1
            while bits < lax.axis_size(axis):
                self.steps.append((axis, bits))
                bits *= 2

    def hop(self, *earlier):
        vector = hold(self.vector, earlier)
        axis, bits = self.steps.pop(0)
        self.vector = vector + swap(vector, axis, bits)
        return [self.vector]


def local(
    inputs, image_ids, pad_mask, cotangent, w_qkv, w_out, w_up, w_down, ln1_gain, ln1_shift,
    q_bias, v_bias, out_bias, ln2_gain, ln2_shift, up_bias, down_bias,
):
    ns, nf = lax.axis_size("seq"), lax.axis_size("fsdp")
    s = lax.axis_index("seq")
    rows, width = inputs.shape[1:]
    n = rows * ns
    cols = width // ns
    band = w_up.shape[0]
    strip = w_down.shape[0]
    wide = lanes(-(-strip // ns) * nf)
    sub = wide // nf
    heads = HEADS // ns
    tile = 256
    order = [s ^ j for j in range(ns)]
    slots = jnp.stack([jnp.asarray(i, jnp.int32) for i in order])
    hops = nf // 8

    def row(vector):
        return vector[None, :]

    def own(vector):
        return lax.dynamic_slice_in_dim(vector, s * cols, cols)

    def own_hidden(array):
        count = array.shape[0]
        array = array.reshape(count, nf, strip)
        array = jnp.pad(array, ((0, 0), (0, 0), (0, ns * sub - strip)))
        return lax.dynamic_slice_in_dim(array, s * sub, sub, axis=2).reshape(count, wide)

    first = [lax.dynamic_slice_in_dim(w_qkv, t * width + s * cols, cols, axis=1) for t in range(3)]
    first.append(lax.dynamic_slice_in_dim(w_out, s * cols, cols, axis=1))
    ring_one = RingGather(jnp.concatenate(first, axis=1))
    x_own = inputs[0]
    code = (image_ids * 2 + pad_mask).astype(BF)
    x_pack = jnp.concatenate([x_own, jnp.pad(code, ((0, 15), (0, width - rows)))], axis=0)
    split = rows // 2
    x_parts = [x_pack[:split], x_pack[split:]]
    far_a = far_swaps(x_parts[0])
    done = [far_a, *[ring_one.hop() for _ in range(hops)]]
    up_mine = own_hidden(w_up)
    keep = (1 - pad_mask[0]).astype(F32)[:, None]
    gy_own = (cotangent[0].astype(F32) * keep).astype(BF)
    gy_parts = [gy_own[:split], gy_own[split:]]
    down_mine = lax.dynamic_slice_in_dim(jnp.pad(w_down, ((0, ns * sub - strip), (0, 0))), s * sub, sub, axis=0)
    up_part = own_hidden(row(up_bias))
    q_part, v_part = row(own(q_bias)), row(own(v_bias))
    one_slots = jnp.stack([jnp.asarray(i, jnp.int32) for i in order + ring_one.indices()])
    done = [*done, up_mine]

    far_b, gy_parts, slots, one_slots = hold((x_parts[1], gy_parts, slots, one_slots), *done)
    far_b = far_swaps(far_b)
    done = [far_b, gy_parts, slots, one_slots, *[ring_one.hop(*done) for _ in range(hops)]]
    full_up = lax.all_gather(hold(up_mine, *done), "fsdp", axis=0, tiled=True)
    down_mine, up_part, q_part, v_part = hold((down_mine, up_part, q_part, v_part), *done)
    x_pack, far_a, far_b = hold((x_pack, far_a, far_b), *done)
    near, near_a, near_b = near_swaps([x_pack]), near_swaps(far_a), near_swaps(far_b)
    done = [near, near_a, near_b, down_mine, up_part, q_part, v_part, *[ring_one.hop(*done) for _ in range(hops)]]
    x_blocks = [[x_pack], [near[0]]]
    for i in range(ns // 2 - 1):
        x_blocks += [[far_a[i], far_b[i]], [near_a[i], near_b[i]]]
    gy_far_a = far_swaps(hold(gy_parts[0], *done))
    done = [gy_far_a, *[ring_one.hop(*done) for _ in range(hops)]]

    x_blocks, pieces, gy_parts = hold((x_blocks, ring_one.pieces, gy_parts), *done)
    gy_far_b = far_swaps(gy_parts[1])
    x_all, h_one, q, k, v, full_qkv, out_cols, code = project(
        x_blocks, pieces, one_slots, row(ln1_gain), row(ln1_shift), q_part, v_part, rows
    )
    full_down = lax.all_gather(hold(down_mine, q), "fsdp", axis=0, tiled=True)

    out_cols, gy_parts, gy_far_a, gy_far_b = hold((out_cols, gy_parts, gy_far_a, gy_far_b), q)
    out_far = far_swaps(out_cols)
    o, lse = attention_forward(q, k, v, code, heads, 384 if rows % 384 == 0 else tile)
    o, gy_parts, gy_far_a, gy_far_b, out_row = hold((o, gy_parts, gy_far_a, gy_far_b, [out_cols, *out_far]), o)
    o_row = [o, *far_swaps(o)]
    gy_near = [near_swaps([gy_parts[0], *gy_far_a]), near_swaps([gy_parts[1], *gy_far_b])]
    w_outs = woven(out_row, near_swaps(out_row))
    gy_all = jnp.zeros((n, width), BF)
    gy_rows = [woven([gy_parts[h], *far], near) for h, (far, near) in enumerate(zip((gy_far_a, gy_far_b), gy_near))]
    for h in range(2):
        for j in range(ns):
            gy_all = lax.dynamic_update_slice(gy_all, gy_rows[h][j], (order[j] * rows + h * split, 0))
    done = [o_row, w_outs, gy_all]
    o_row = hold(o_row, *done)
    os = woven(o_row, near_swaps(o_row))

    x_one, o_all, h_two, active, slope, full_out = widen(
        x_all, os, w_outs, slots, row(out_bias), row(ln2_gain), row(ln2_shift), full_up, up_part, rows
    )
    gu, mixed, *far_dh, far_sum = narrow(gy_all, active, slope, full_up, full_down, slots, rows, 2, ns - 2, ())

    def cut(array, j):
        return array[j * rows : (j + 1) * rows]

    def summed(a, b):
        return (a.astype(F32) + b.astype(F32)).astype(BF)

    far_near = near_swaps(far_dh[1::2])
    active, gy_all = hold((active, gy_all), far_dh)
    grad_down_part = dot_at(active, gy_all).astype(BF)
    down_sum = lax.psum_scatter(grad_down_part, "fsdp", scatter_dimension=0, tiled=True)
    far_near, gy_all, active = hold((far_near, gy_all, active), grad_down_part)
    far_held = [summed(far_dh[2 * i], got) for i, got in enumerate(far_near)]
    gu, mixed, far_held = hold((gu, mixed, far_held))
    terms = [swap(held, "seq", 2 * i + 2) for i, held in enumerate(far_held)]
    gu, mixed, *near_dh, near_sum = narrow(gy_all, active, slope, full_up, full_down, slots, rows, 0, 2, (gu, mixed))
    terms += [near_dh[0], swap(near_dh[1], "seq", 1)]
    dx_one, sums_two, go_parts, ga_parts = middle(terms, x_one, gy_own, row(ln2_gain), full_out, slots, ns)
    go_parts, h_two, gu, mixed = hold((go_parts, h_two, gu, mixed))
    go_blocks = [block if j == 0 else swap(block, "seq", j) for j, block in enumerate(go_parts)]
    grad_up_part = dot_at(h_two, gu).astype(BF)
    up_sum = lax.psum_scatter(grad_up_part, "fsdp", scatter_dimension=0, tiled=True)

    def mixed_block(j):
        return lax.dynamic_slice_in_dim(mixed, order[j] * rows, rows, axis=0)

    mixed_near = near_swaps([mixed_block(j + 1) for j in range(0, ns, 2)])
    mixed_held = [summed(mixed_block(2 * i), mixed_near[i]) for i in range(1, ns // 2)]
    done = [go_blocks, grad_up_part, mixed_near, mixed_held]
    q, k, v, go_blocks, ga_parts, mixed_held = hold((q, k, v, go_blocks, ga_parts, mixed_held), *done)
    ga_blocks = [block if j == 0 else swap(block, "seq", j) for j, block in enumerate(ga_parts)]
    mixed_far = [swap(block, "seq", 2 * i + 2) for i, block in enumerate(mixed_held)]
    gqkv = attention_backward(q, k, v, o, go_blocks, 0, slots, lse, code, heads, tile)

    gqkv, ga_blocks, down_sum = hold((gqkv, ga_blocks, down_sum))

    def exchanged(pieces):
        return [piece if j == 0 else swap(piece, "seq", j) for j, piece in enumerate(pieces)]

    downs = exchanged([lax.dynamic_slice_in_dim(down_sum, order[j] * cols, cols, axis=1) for j in range(ns)])
    grad_part = weigh(h_one, gqkv, o_all, ga_blocks)

    def bands(owner):
        return lax.dynamic_slice_in_dim(grad_part, owner * band, band, axis=0).astype(F32)

    ring_sum = RingSum(bands)

    def ring_round(*earlier):
        new = []
        for _ in range(hops):
            if ring_sum.done:
                ring_sum.add(*earlier)
            new.append(ring_sum.hop(*earlier))
        return new

    gqkv = hold(gqkv, ring_sum.one, ring_sum.two)
    done = [ring_round(gqkv)]
    dh_one_part, sums_one = finish(gqkv, x_all, full_qkv, sums_two, far_sum, near_sum, slots, rows)
    totals = TotalSum(sums_one)
    done += [dh_one_part, mixed_far, downs]
    dh_one_part = hold(dh_one_part, *done)
    dh_near = near_swaps([cut(dh_one_part, j + 1) for j in range(0, ns, 2)])
    done = [dh_near, ring_round(*done), totals.hop(*done)]
    dh_near = hold(dh_near, *done)
    dh_held = [summed(cut(dh_one_part, 2 * i), dh_near[i]) for i in range(1, ns // 2)]
    dh_far_a = [swap(block[:split], "seq", 2 * i + 2) for i, block in enumerate(dh_held)]
    done = [dh_far_a, ring_round(*done), totals.hop(*done)]
    dh_held = hold(dh_held, *done)
    dh_far_b = [swap(block[split:], "seq", 2 * i + 2) for i, block in enumerate(dh_held)]
    done = [dh_far_b, ring_round(*done), totals.hop(*done)]

    mine = hold(ring_sum.result(), *done)
    grad_out = mine[:, 3 * cols :]
    thirds = [mine[:, t * cols : (t + 1) * cols].astype(BF) for t in range(3)]
    got = []
    for p in range(3):
        perm = [((3 * d + p) % ns, d) for d in range(ns)]
        section = [0] * ns
        for d in range(ns):
            section[(3 * d + p) % ns] = (3 * d + p) // ns
        which = sum(jnp.where(s == i, t, 0) for i, t in enumerate(section))
        piece = jnp.where(which == 0, thirds[0], jnp.where(which == 1, thirds[1], thirds[2]))
        got.append(lax.ppermute(piece, "seq", perm))
    grad_qkv = jnp.concatenate(got, axis=1).astype(F32)
    total = totals.hop(*done)
    while totals.steps:
        total = totals.hop(total)

    share = nf // ns * sub
    ups = exchanged([lax.dynamic_slice_in_dim(up_sum, order[j] * share, share, axis=1) for j in range(ns)])
    grad_up, grad_down_t = settle(ups, downs, slots, strip)

    dh_far = [jnp.concatenate(pair, axis=0) for pair in zip(dh_far_a, dh_far_b)]
    dh_one = add_up([cut(dh_one_part, 0), dh_near[0], *dh_far])
    normal_x, inverse_x = normalise(x_own.astype(F32))
    grad_inputs = (dx_one + norm_back(normal_x, inverse_x, ln1_gain, dh_one)).astype(BF)
    layer_out = (x_one + add_up([mixed_block(0), mixed_near[0], *mixed_far]) + down_bias).astype(BF)
    total = totals.vector
    sum_hidden = jnp.swapaxes(total[8 : 8 + ns, :wide].reshape(ns, nf, sub), 0, 1).reshape(nf, ns * sub)
    sums = [total[i] for i in range(8)]
    sums.insert(7, sum_hidden[:, :strip].reshape(nf * strip))
    return (layer_out[None], grad_inputs[None], grad_qkv, grad_out, grad_up, grad_down_t.T, *sums)


def solution(mesh):
    tokens, weights, shared = P("fsdp", "seq", None), P("fsdp", None), P()
    marks, grads = P("fsdp", "seq"), P("fsdp", "seq")
    return jax.shard_map(
        local,
        mesh=mesh,
        in_specs=(tokens, marks, marks, tokens) + (weights,) * 4 + (shared,) * 9,
        out_specs=(tokens, tokens) + (grads,) * 4 + (shared,) * 9,
        check_vma=False,
    )
```

```python
import functools
import math

import jax
import jax.numpy as jnp
from jax import lax
from jax.experimental import pallas as pl
from jax.experimental.pallas import tpu as pltpu
from jax.sharding import PartitionSpec as P

HEADS = 16
HD = 72
IMG_TOK = 729
EPSILON = 1e-06
SCALING = HD ** (-0.5)
LOG2E = math.log2(math.e)
NEG = -1e30
BF = jnp.bfloat16
F32 = jnp.float32


def windows(heads, width):
    out = []
    for h in range(heads):
        lo = h * HD // 128 * 128
        out.append((lo, min(width, -(-(h * HD + HD) // 128) * 128)))
    return out


def head_lanes(lo, h, shape):
    lane = lax.broadcasted_iota(jnp.int32, shape, 1) + lo
    return (lane >= h * HD) & (lane < h * HD + HD)


def head_pieces(wins, outs):
    pieces = {}
    for (lo, hi), out in zip(wins, outs):
        for c in range(lo, hi, 128):
            part = out[:, c - lo : min(c + 128, hi) - lo]
            pieces[c] = part if c not in pieces else pieces[c] + part
    return pieces.items()


def lanes(width):
    return -(-width // 128) * 128


def load_blocks(blocks, target, slots, first, sems):
    rows = blocks[0].shape[0]
    copies = []
    for i, block in enumerate(blocks):
        start = pl.multiple_of(slots[first + i] * rows, 8)
        copies.append(pltpu.make_async_copy(block, target.at[pl.ds(start, rows)], sems.at[i]))
        copies[-1].start()
    for copy in copies:
        copy.wait()


def marks(code):
    ids = lax.shift_right_logical(code, 1)
    keys = jnp.where((code & 1) == 0, ids, -1)
    return ids.astype(F32), keys.astype(F32)


def key_tiles(mine, ids, tile):
    before = jnp.sum(jnp.where(ids < jnp.min(mine), 1.0, 0.0)).astype(jnp.int32)
    upto = jnp.sum(jnp.where(ids <= jnp.max(mine), 1.0, 0.0)).astype(jnp.int32)
    return before // tile, (upto + tile - 1) // tile


def most_tiles(tile, length):
    return min(length // tile, -(-(tile + 2 * IMG_TOK) // tile) + 1)


def column(row, width):
    return jnp.broadcast_to(row, (width, row.shape[1])).T


def forward_kernel(heads, tile, q_ref, k_ref, v_ref, code_ref, o_ref, lse_ref):
    i = pl.program_id(0)
    mine, _ = marks(code_ref[0:1, pl.ds(pl.multiple_of(i * tile, tile), tile)])
    lo, hi = key_tiles(mine, marks(code_ref[0:1, :])[0], tile)
    wins = windows(heads, q_ref.shape[1])

    def attend(count):
        size = count * tile
        rows = pl.ds(pl.multiple_of(lo * tile, tile), size)
        rel = lax.broadcasted_iota(jnp.int32, (tile, size), 0) - lax.broadcasted_iota(jnp.int32, (tile, size), 1)
        allowed = (jnp.concatenate([column(mine, 128)] * (size // 128), axis=1) == marks(code_ref[0:1, rows])[1]) | (rel == (lo - i) * tile)
        lane = lax.broadcasted_iota(jnp.int32, (tile, 128), 1)
        lse = jnp.zeros((tile, 128), F32)
        outs = []

        def scores(h):
            a, b = wins[h]
            w = q_ref[:, a:b]
            w = jnp.where(head_lanes(a, h, w.shape), w, jnp.zeros_like(w))
            return dot_bt(w, k_ref[rows, a:b])

        raw = scores(0)
        for h, (a, b) in enumerate(wins):
            s = jnp.where(allowed, raw * (SCALING * LOG2E), NEG)
            if h + 1 < heads:
                raw = scores(h + 1)
            top = jnp.max(s, axis=1, keepdims=True)
            p = jnp.exp2(s - top)
            total = jnp.sum(p, axis=1, keepdims=True)
            out = jnp.dot(p.astype(BF), v_ref[rows, a:b], preferred_element_type=F32) * (1.0 / total)
            outs.append(jnp.where(head_lanes(a, h, out.shape), out, 0.0))
            lse = jnp.where(lane == h, top + jnp.log2(total), lse)
        for c, part in head_pieces(wins, outs):
            o_ref[c : c + part.shape[1], :] = part.T.astype(BF)
        lse_ref[...] = lse.T[: lse_ref.shape[0], :]

    for count in range(1, most_tiles(tile, k_ref.shape[0]) + 1):
        pl.when(hi - lo == count)(functools.partial(attend, count))


def whole_block(shape):
    return pl.BlockSpec(shape, lambda *_: (0, 0))


def kept_block(shape):
    return pl.BlockSpec(shape, lambda *_: (0, 0), pipeline_mode=pl.Buffered(1))


def row_block(tile, width):
    return pl.BlockSpec((tile, width), lambda i, *_: (i, 0))


def lane_block(height, tile):
    return pl.BlockSpec((height, tile), lambda i, *_: (0, i))


def slot_block(tile, width):
    return pl.BlockSpec((tile, width), lambda i, slots: (slots[i], 0))


def attention_forward(q, k, v, code, heads, tile):
    n, width = q.shape
    return pl.pallas_call(
        functools.partial(forward_kernel, heads, tile),
        out_shape=(jax.ShapeDtypeStruct((width, n), BF), jax.ShapeDtypeStruct((8, n), F32)),
        grid_spec=pl.GridSpec(
            grid=(n // tile,),
            in_specs=[row_block(tile, width), whole_block((n, width)), whole_block((n, width)), whole_block((8, n))],
            out_specs=[lane_block(width, tile), lane_block(8, tile)],
        ),
        compiler_params=pltpu.CompilerParams(vmem_limit_bytes=56 << 20),
        cost_estimate=pl.CostEstimate(flops=4 * n * n * 128 * heads, bytes_accessed=10 * n * width, transcendentals=n * n * heads),
        name="attention_forward",
    )(q, k, v, code)


def backward_kernel(heads, tile, count, first, slots, q_ref, k_ref, v_ref, o_ref, lse_ref, code_ref, *refs):
    blocks, (out_ref, go_ref, dk_acc, dv_acc, kid_ref, sems) = refs[:count], refs[count:]
    i = pl.program_id(0)
    qid, _ = marks(code_ref[0:1, pl.ds(pl.multiple_of(i * tile, tile), tile)])
    lo, hi = key_tiles(qid, marks(code_ref[0:1, :])[0], tile)
    width = q_ref.shape[1]
    wins = windows(heads, width)

    @pl.when(i == 0)
    def _():
        copies = []
        for t, block in enumerate(blocks):
            size = block.shape[1]
            there = go_ref.at[:, pl.ds(pl.multiple_of(slots[t] * size, 128), size)]
            copies.append(pltpu.make_async_copy(block, there, sems.at[t]))
            copies[-1].start()
        for copy in copies:
            copy.wait()
        dk_acc[...] = jnp.zeros_like(dk_acc)
        dv_acc[...] = jnp.zeros_like(dv_acc)
        for t in range(0, kid_ref.shape[0], tile):
            kid_ref[t : t + tile, :] = column(marks(code_ref[0:1, t : t + tile])[1], 128)

    here = pl.ds(pl.multiple_of(i * tile, tile), tile)

    def attend(tiles):
        size = tiles * tile
        rows = pl.ds(pl.multiple_of(lo * tile, tile), size)
        rel = lax.broadcasted_iota(jnp.int32, (size, tile), 1) - lax.broadcasted_iota(jnp.int32, (size, tile), 0)
        allowed = (jnp.concatenate([kid_ref[rows, :]] * (tile // 128), axis=1) == qid) | (rel == (lo - i) * tile)
        go = go_ref[:, here]
        product = go.astype(F32) * o_ref[...].astype(F32)
        outs = []

        def products(h):
            a, b = wins[h]
            on = head_lanes(a, h, (tile, b - a))
            query = jnp.where(on, q_ref[:, a:b], jnp.zeros((tile, b - a), BF))
            unit = lax.broadcasted_iota(jnp.int32, (b - a, tile), 0) + a
            grad = jnp.where((unit >= h * HD) & (unit < h * HD + HD), go[a:b, :], jnp.zeros((b - a, tile), BF))
            return query, grad, dot_bt(k_ref[rows, a:b], query), dot(v_ref[rows, a:b], grad)

        ready = products(0)
        for h, (a, b) in enumerate(wins):
            query, grad, s, dp = ready
            if h + 1 < heads:
                ready = products(h + 1)
            inner = jnp.sum(product[h * HD : (h + 1) * HD, :], axis=0, keepdims=True)
            on = head_lanes(a, h, (tile, b - a))
            key = k_ref[rows, a:b]
            p = jnp.exp2(jnp.where(allowed, s * (SCALING * LOG2E) - lse_ref[h : h + 1, :], NEG))
            ds = (p * (dp - inner)).astype(BF)
            dv_acc[rows, a:b] += dot_bt(p.astype(BF), grad)
            dk_acc[rows, a:b] += dot(ds, query)
            outs.append(jnp.where(on, dot_at(ds, key) * SCALING, 0.0))
        for c, part in head_pieces(wins, outs):
            out_ref[here, c : c + part.shape[1]] = part.astype(BF)

    for tiles in range(1, most_tiles(tile, k_ref.shape[0]) + 1):
        pl.when(hi - lo == tiles)(functools.partial(attend, tiles))

    @pl.when(i == pl.num_programs(0) - 1)
    def _():
        out_ref[:, width : 2 * width] = (dk_acc[...] * SCALING).astype(BF)
        out_ref[:, 2 * width : 3 * width] = dv_acc[...].astype(BF)


def attention_backward(q, k, v, o, go_blocks, first, slots, lse, code, heads, tile):
    n, width = q.shape
    count = len(go_blocks)
    return pl.pallas_call(
        functools.partial(backward_kernel, heads, tile, count, first),
        out_shape=jax.ShapeDtypeStruct((n, 3 * width), BF),
        grid_spec=pltpu.PrefetchScalarGridSpec(
            num_scalar_prefetch=1,
            grid=(n // tile,),
            in_specs=[
                row_block(tile, width),
                whole_block((n, width)),
                whole_block((n, width)),
                lane_block(width, tile),
                lane_block(8, tile),
                whole_block((8, n)),
            ]
            + [pl.BlockSpec(memory_space=pl.ANY)] * count,
            out_specs=whole_block((n, 3 * width)),
            scratch_shapes=[
                pltpu.VMEM((go_blocks[0].shape[0], n), BF),
                pltpu.VMEM((n, width), F32),
                pltpu.VMEM((n, width), F32),
                pltpu.VMEM((n, 128), F32),
                pltpu.SemaphoreType.DMA((count,)),
            ],
        ),
        compiler_params=pltpu.CompilerParams(vmem_limit_bytes=56 << 20),
        cost_estimate=pl.CostEstimate(flops=10 * n * n * 128 * heads, bytes_accessed=16 * n * width, transcendentals=n * n * heads),
        name="attention_backward",
    )(slots, q, k, v, o, lse, code, *go_blocks)


def normalise(values):
    average = jnp.mean(values, axis=-1, keepdims=True)
    centred = values - average
    spread = jnp.mean(centred * centred, axis=-1, keepdims=True)
    inverse = lax.rsqrt(spread + EPSILON)
    return centred * inverse, inverse


def norm_back(normal, inverse, gain, grad):
    scaled = grad * gain
    first = jnp.mean(scaled, axis=-1, keepdims=True)
    second = jnp.mean(scaled * normal, axis=-1, keepdims=True)
    return (scaled - first - normal * second) * inverse


def gelu_both(u):
    root = math.sqrt(2.0 / math.pi)
    bent = jnp.tanh(root * (u + 0.044715 * u * u * u))
    half = 0.5 * (1.0 + bent)
    slope = half + 0.5 * u * (1.0 - bent * bent) * (root + 3 * 0.044715 * root * u * u)
    return u * half, slope


def dot(a, b):
    return jnp.dot(a, b, preferred_element_type=F32)


def dot_bt(a, b):
    return lax.dot_general(a, b, (((1,), (1,)), ((), ())), preferred_element_type=F32)


def dot_at(a, b):
    return lax.dot_general(a, b, (((0,), (0,)), ((), ())), preferred_element_type=F32)


def row_parts(rows):
    return [slice(0, 256), slice(256, rows)]


def project_kernel(counts, bands, slots, *refs):
    xs, pieces = refs[: sum(counts)], refs[sum(counts) : sum(counts) + bands]
    gain, shift, q_bias, v_bias, x_out, h_out, q_out, k_out, v_out, w_out, out_out, code_out, x_now, sems = refs[
        sum(counts) + bands :
    ]
    j = pl.program_id(0)
    rows, cols = q_out.shape

    @pl.when(j == 0)
    def _():
        load_blocks(pieces, w_out, slots, len(counts), sems)
        out_out[:, :cols] = w_out[:, 3 * cols :]

    at = 0
    for i, count in enumerate(counts):

        @pl.when(j == i)
        def _(parts=xs[at : at + count]):
            start = 0
            for part in parts:
                size = min(part.shape[0], rows - start)
                x_now[start : start + size, :] = part[:size, :]
                start += size
            last = parts[-1].shape[0] - 16
            code = parts[-1][last:, :rows].astype(F32)[0:1, :]
            code_out[...] = jnp.broadcast_to(code, code_out.shape).astype(jnp.int32)

        at += count
    x = x_now[...]
    x_out[...] = x
    normal, _ = normalise(x.astype(F32))
    h = (normal * gain[...] + shift[...]).astype(BF)
    h_out[...] = h
    projected = dot(h, w_out[...])
    q_out[...] = (projected[:, :cols] + q_bias[...]).astype(BF)
    k_out[...] = projected[:, cols : 2 * cols].astype(BF)
    v_out[...] = (projected[:, 2 * cols : 3 * cols] + v_bias[...]).astype(BF)


def project(xs, pieces, slots, gain, shift, q_bias, v_bias, rows):
    width, cols, bands = xs[0][0].shape[1], q_bias.shape[1], len(pieces)
    counts = tuple(len(parts) for parts in xs)
    xs = [part for parts in xs for part in parts]
    n, columns = rows * len(counts), pieces[0].shape[1]
    shape = jax.ShapeDtypeStruct
    return pl.pallas_call(
        functools.partial(project_kernel, counts, bands),
        out_shape=[shape((n, width), BF)] * 2
        + [shape((n, cols), BF)] * 3
        + [shape((width, columns), BF), shape((width, lanes(cols)), BF), shape((8, n), jnp.int32)],
        grid_spec=pltpu.PrefetchScalarGridSpec(
            num_scalar_prefetch=1,
            grid=(len(counts),),
            in_specs=[kept_block(part.shape) for part in xs]
            + [pl.BlockSpec(memory_space=pl.ANY)] * bands
            + [kept_block((1, width))] * 2
            + [kept_block((1, cols))] * 2,
            out_specs=[slot_block(rows, width)] * 2
            + [slot_block(rows, cols)] * 3
            + [
                whole_block((width, columns)),
                whole_block((width, lanes(cols))),
                pl.BlockSpec((8, rows), lambda i, slots: (0, slots[i])),
            ],
            scratch_shapes=[pltpu.VMEM((rows, width), BF), pltpu.SemaphoreType.DMA((bands,))],
        ),
        compiler_params=pltpu.CompilerParams(vmem_limit_bytes=56 << 20),
        cost_estimate=pl.CostEstimate(flops=2 * n * width * columns, bytes_accessed=8 * n * width, transcendentals=n),
        name="norm_project",
    )(slots, *xs, *pieces, gain, shift, q_bias, v_bias)


def widen_kernel(count, slots, x_ref, *refs):
    os, w_outs = refs[:count], refs[count : 2 * count]
    (out_bias, gain, shift, w_up, up_bias, x_out, o_out, h_out, a_out, slope_out, w_out) = refs[2 * count :]
    j = pl.program_id(0)
    cols = os[0].shape[0]
    for v in range(count):

        @pl.when((j == 0) & (slots[0] == v))
        def _(v=v):
            for i in range(count):
                start = (v ^ i) * cols
                w_out[:, start : start + cols] = w_outs[i][:, :cols]

    for i in range(count):
        o_out[pl.ds(pl.multiple_of(slots[i] * cols, 8), cols), :] = os[i][...]
    parts = row_parts(x_ref.shape[0])

    def branch(part):
        return dot_at(o_out[:, part], w_out[...])

    def norm(part, product):
        x = x_ref[part, :].astype(F32) + (product + out_bias[...])
        x_out[part, :] = jnp.where(j == 0, x, x_out[part, :])
        h = (normalise(x)[0] * gain[...] + shift[...]).astype(BF)
        h_out[part, :] = h
        return h

    def bend(part, u):
        value, slope = gelu_both(u + up_bias[...])
        a_out[part, :] = value.astype(BF)
        slope_out[part, :] = slope.astype(BF)

    products, us = {}, {}
    for t in range(len(parts) + 2):
        if t < len(parts):
            products[t] = branch(parts[t])
        if 0 <= t - 1 < len(parts):
            us[t - 1] = dot(norm(parts[t - 1], products[t - 1]), w_up[...])
        if 0 <= t - 2 < len(parts):
            bend(parts[t - 2], us[t - 2])


def widen(x_all, os, w_outs, slots, out_bias, gain, shift, w_up, up_bias, rows):
    n, width = x_all.shape
    count, cols, hidden = len(os), os[0].shape[0], up_bias.shape[1]
    shape = jax.ShapeDtypeStruct
    return pl.pallas_call(
        functools.partial(widen_kernel, count),
        out_shape=[
            shape((rows, width), F32),
            shape((width, n), BF),
            shape((n, width), BF),
            shape((n, hidden), BF),
            shape((n, hidden), BF),
            shape((width, width), BF),
        ],
        grid_spec=pltpu.PrefetchScalarGridSpec(
            num_scalar_prefetch=1,
            grid=(count,),
            in_specs=[slot_block(rows, width)]
            + [pl.BlockSpec((cols, rows), lambda i, slots: (0, slots[i]))] * count
            + [kept_block(w_outs[0].shape)] * count
            + [kept_block((1, width))] * 3
            + [kept_block((width, hidden)), kept_block((1, hidden))],
            out_specs=[whole_block((rows, width)), lane_block(width, rows), slot_block(rows, width)]
            + [slot_block(rows, hidden)] * 2
            + [whole_block((width, width))],
        ),
        compiler_params=pltpu.CompilerParams(vmem_limit_bytes=60 << 20),
        cost_estimate=pl.CostEstimate(flops=2 * n * width * (width + hidden), bytes_accessed=16 * n * width, transcendentals=n * hidden),
        name="out_norm_up",
    )(slots, x_all, *os, *w_outs, out_bias, gain, shift, w_up, up_bias)


def narrow_kernel(count, slots, gy_ref, a_ref, slope_ref, w_up, w_down, *refs):
    dh_outs = refs[len(refs) - 1 - count : -1]
    gu_out, y_out = refs[len(refs) - 3 - count : len(refs) - 1 - count]
    sum_out = refs[-1]

    @pl.when(pl.program_id(0) == 0)
    def _():
        sum_out[...] = jnp.zeros_like(sum_out)

    gu = (dot_bt(gy_ref[...], w_down[...]) * slope_ref[...]).astype(BF)
    gu_out[...] = gu
    dh = dot_bt(gu, w_up[...]).astype(BF)
    for i in range(count):

        @pl.when(pl.program_id(0) == i)
        def _(i=i):
            dh_outs[i][...] = dh

    y_out[...] = dot(a_ref[...], w_down[...]).astype(BF)
    sum_out[...] += jnp.sum(gu.astype(F32), axis=0, keepdims=True)


def narrow(gy, active, slope, w_up, w_down, slots, rows, first, count, carried):
    n, width = gy.shape
    hidden = w_up.shape[1]
    shape = jax.ShapeDtypeStruct

    def block(size):
        return pl.BlockSpec((rows, size), lambda i, slots: (slots[first + i], 0))

    return pl.pallas_call(
        functools.partial(narrow_kernel, count),
        out_shape=[shape((n, hidden), BF), shape((n, width), BF)]
        + [shape((rows, width), BF)] * count
        + [shape((1, hidden), F32)],
        grid_spec=pltpu.PrefetchScalarGridSpec(
            num_scalar_prefetch=1,
            grid=(count,),
            in_specs=[block(width), block(hidden), block(hidden)]
            + [kept_block((width, hidden)), kept_block((hidden, width))]
            + [pl.BlockSpec(memory_space=pl.ANY)] * len(carried),
            out_specs=[block(hidden), block(width)] + [whole_block((rows, width))] * count + [whole_block((1, hidden))],
        ),
        input_output_aliases={6 + i: i for i in range(len(carried))},
        compiler_params=pltpu.CompilerParams(vmem_limit_bytes=56 << 20),
        cost_estimate=pl.CostEstimate(flops=6 * rows * count * width * hidden, bytes_accessed=16 * rows * count * width, transcendentals=0),
        name="down_and_back",
    )(slots, gy, active, slope, w_up, w_down, *carried)


def finish_kernel(count, slots, g_ref, x_ref, w_qkv, mid_ref, far_ref, near_ref, dh_out, sum_out, bias_acc):
    j = pl.program_id(0)

    @pl.when(j == 0)
    def _():
        sum_out[...] = jnp.zeros_like(sum_out)
        bias_acc[...] = jnp.zeros_like(bias_acc)

    g = g_ref[...]
    dh = dot_bt(g, w_qkv[:, : g.shape[1]])
    dh_out[...] = dh.astype(BF)
    normal, _ = normalise(x_ref[...].astype(F32))
    sum_out[0:1, :] += jnp.sum(dh * normal, axis=0, keepdims=True)
    sum_out[1:2, :] += jnp.sum(dh, axis=0, keepdims=True)
    bias_acc[...] += jnp.sum(g.astype(F32), axis=0, keepdims=True)
    cols, wide = g.shape[1] // 3, far_ref.shape[1]

    @pl.when(j == count - 1)
    def _():
        sum_out[4:5, :] = mid_ref[2:3, :]
        sum_out[5:7, :] = mid_ref[0:2, :]
        sum_out[7:8, :] = mid_ref[3:4, :]
        for v in range(count):

            @pl.when(slots[0] == v)
            def _(v=v):
                sum_out[2:3, v * cols : (v + 1) * cols] = bias_acc[:, :cols]
                sum_out[3:4, v * cols : (v + 1) * cols] = bias_acc[:, 2 * cols :]
                sum_out[8 + v : 9 + v, :wide] = far_ref[...] + near_ref[...]


def finish(gqkv, x_all, w_qkv, mid, far_sum, near_sum, slots, rows):
    n, width = x_all.shape
    columns, count, wide = gqkv.shape[1], n // rows, far_sum.shape[1]
    height = -(-(8 + count) // 8) * 8
    shape = jax.ShapeDtypeStruct
    return pl.pallas_call(
        functools.partial(finish_kernel, count),
        out_shape=[shape((n, width), BF), shape((height, width), F32)],
        grid_spec=pltpu.PrefetchScalarGridSpec(
            num_scalar_prefetch=1,
            grid=(count,),
            in_specs=[slot_block(rows, columns), slot_block(rows, width), kept_block(w_qkv.shape)]
            + [kept_block(mid.shape), kept_block((1, wide)), kept_block((1, wide))],
            out_specs=[row_block(rows, width), whole_block((height, width))],
            scratch_shapes=[pltpu.VMEM((1, columns), F32)],
        ),
        compiler_params=pltpu.CompilerParams(vmem_limit_bytes=56 << 20),
        cost_estimate=pl.CostEstimate(flops=2 * n * width * columns, bytes_accessed=8 * n * width, transcendentals=n),
        name="project_back",
    )(slots, gqkv, x_all, w_qkv, mid, far_sum, near_sum)


def settle_kernel(count, slots, *refs):
    ups, downs, (up_out, down_out) = refs[:count], refs[count : 2 * count], refs[2 * count :]
    strip = down_out.shape[1]
    sub = downs[0].shape[0]
    ratio = ups[0].shape[1] // sub
    for v in range(count):

        @pl.when(slots[0] == v)
        def _(v=v):
            for i in range(count):
                start = (v ^ i) * sub
                size = min(sub, strip - start)
                if size > 0:
                    down_out[:, start : start + size] = downs[i][:size, :].astype(F32).T
                    for h in range(ratio):
                        piece = ups[i][:, h * sub : h * sub + size]
                        up_out[:, h * strip + start : h * strip + start + size] = piece.astype(F32)


def settle(ups, downs, slots, strip):
    band, sub, cols = ups[0].shape[0], downs[0].shape[0], downs[0].shape[1]
    ratio, count = ups[0].shape[1] // sub, len(ups)
    shape = jax.ShapeDtypeStruct
    return pl.pallas_call(
        functools.partial(settle_kernel, count),
        out_shape=[shape((band, ratio * strip), F32), shape((cols, strip), F32)],
        grid_spec=pltpu.PrefetchScalarGridSpec(
            num_scalar_prefetch=1,
            grid=(1,),
            in_specs=[kept_block(ups[0].shape)] * count + [kept_block(downs[0].shape)] * count,
            out_specs=[whole_block((band, ratio * strip)), whole_block((cols, strip))],
        ),
        compiler_params=pltpu.CompilerParams(vmem_limit_bytes=56 << 20),
        name="settle_hidden",
    )(slots, *ups, *downs)


def weigh_kernel(count, h_ref, g_ref, o_ref, *refs):
    gas, (out_ref, ga_now) = refs[:count], refs[count:]
    rows = gas[0].shape[0]

    @pl.when(pl.program_id(0) == 0)
    def _():
        for i in range(count):
            ga_now[i * rows : (i + 1) * rows, :] = gas[i][...]

    columns = g_ref.shape[1]
    out_ref[:, :columns] = dot_at(h_ref[...], g_ref[...]).astype(BF)
    out_ref[:, columns:] = dot(o_ref[...], ga_now[...]).astype(BF)


def weigh(h_one, gqkv, o_all, gas):
    n, width = h_one.shape
    rows, cols = gas[0].shape
    columns, tile = gqkv.shape[1], width // 3
    return pl.pallas_call(
        functools.partial(weigh_kernel, len(gas)),
        out_shape=jax.ShapeDtypeStruct((width, columns + cols), BF),
        grid_spec=pl.GridSpec(
            grid=(width // tile,),
            in_specs=[lane_block(n, tile), kept_block((n, columns)), row_block(tile, n)] + [kept_block((rows, cols))] * len(gas),
            out_specs=row_block(tile, columns + cols),
            scratch_shapes=[pltpu.VMEM((n, cols), BF)],
        ),
        compiler_params=pltpu.CompilerParams(vmem_limit_bytes=56 << 20),
        cost_estimate=pl.CostEstimate(flops=2 * n * width * (columns + cols), bytes_accessed=6 * n * width, transcendentals=0),
        name="grads_qkv_out",
    )(h_one, gqkv, o_all, *gas)


def middle_kernel(count, terms, slots, *refs):
    parts, (x_ref, gy_ref, gain, w_out, dx_out, sum_out) = refs[:terms], refs[terms : terms + 6]
    go_outs, ga_outs = refs[terms + 6 : terms + 6 + count], refs[terms + 6 + count :]
    grad = sum(part[...].astype(F32) for part in parts)
    normal, inverse = normalise(x_ref[...])
    dx = gy_ref[...].astype(F32) + norm_back(normal, inverse, gain[...], grad)
    dx_out[...] = dx
    ga = dx.astype(BF)
    sum_out[0:1, :] = jnp.sum(grad * normal, axis=0, keepdims=True)
    sum_out[1:2, :] = jnp.sum(grad, axis=0, keepdims=True)
    sum_out[2:3, :] = jnp.sum(ga.astype(F32), axis=0, keepdims=True)
    sum_out[3:4, :] = jnp.sum(gy_ref[...].astype(F32), axis=0, keepdims=True)
    cols = ga_outs[0].shape[1]
    for i in range(count):
        rows = pl.ds(pl.multiple_of(slots[i] * cols, 8), cols)
        go_outs[i][...] = dot_bt(w_out[rows, :], ga).astype(BF)
    for v in range(count):

        @pl.when(slots[0] == v)
        def _(v=v):
            for i in range(count):
                start = (v ^ i) * cols
                ga_outs[i][...] = ga[:, start : start + cols]


def middle(parts, x_one, gy, gain, w_out, slots, count):
    rows, width = x_one.shape
    cols, terms = width // count, len(parts)
    shape = jax.ShapeDtypeStruct
    block = kept_block((rows, width))
    outs = pl.pallas_call(
        functools.partial(middle_kernel, count, terms),
        out_shape=[shape((rows, width), F32), shape((8, width), F32)]
        + [shape((cols, rows), BF)] * count
        + [shape((rows, cols), BF)] * count,
        grid_spec=pltpu.PrefetchScalarGridSpec(
            num_scalar_prefetch=1,
            grid=(1,),
            in_specs=[block] * (terms + 2) + [kept_block((1, width)), kept_block((width, width))],
            out_specs=[whole_block((rows, width)), whole_block((8, width))]
            + [whole_block((cols, rows))] * count
            + [whole_block((rows, cols))] * count,
        ),
        compiler_params=pltpu.CompilerParams(vmem_limit_bytes=56 << 20),
        cost_estimate=pl.CostEstimate(flops=2 * rows * width * width, bytes_accessed=20 * rows * width, transcendentals=rows),
        name="norm_back_out",
    )(slots, *parts, x_one, gy, gain, w_out)
    return outs[0], outs[1], outs[2 : 2 + count], outs[2 + count :]


def swap(value, axis, bits):
    size = lax.axis_size(axis)
    return lax.ppermute(value, axis, [(i, i ^ bits) for i in range(size)])


def hold(values, *earlier):
    return lax.optimization_barrier((values, earlier))[0]


def far_swaps(block):
    return [swap(block, "seq", j) for j in range(2, lax.axis_size("seq"), 2)]


def near_swaps(blocks):
    return [swap(block, "seq", 1) for block in blocks]


def woven(own, near):
    return [block for pair in zip(own, near) for block in pair]


def add_up(terms):
    return sum(term.astype(F32) for term in terms)


def ring_order(size):
    half = size // 2
    return [2 * p if p < half else 2 * (size - 1 - p) + 1 for p in range(size)]


def ring_index(pos, size):
    pos = pos % size
    return jnp.where(pos < size // 2, 2 * pos, 2 * (size - 1 - pos) + 1)


def ring_perms(size):
    order = ring_order(size)
    ahead = [(order[p], order[(p + 1) % size]) for p in range(size)]
    return ahead, [(b, a) for a, b in ahead]


def ring_position(size):
    f = lax.axis_index("fsdp")
    return jnp.where(f % 2 == 0, f // 2, size - 1 - f // 2)


class RingGather:
    def __init__(self, block):
        self.size = lax.axis_size("fsdp")
        self.ahead, self.back = ring_perms(self.size)
        self.pos = ring_position(self.size)
        self.pieces = [block]
        self.one = self.two = block
        self.done = 0

    def indices(self):
        owners = [ring_index(self.pos, self.size)]
        for t in range(1, self.size // 2 + 1):
            owners.append(ring_index(self.pos - t, self.size))
            if t < self.size // 2:
                owners.append(ring_index(self.pos + t, self.size))
        return owners

    def hop(self, *earlier):
        one, two = hold((self.one, self.two), earlier)
        self.done += 1
        self.one = lax.ppermute(one, "fsdp", self.ahead)
        new = [self.one]
        self.pieces.append(self.one)
        if self.done < self.size // 2:
            self.two = lax.ppermute(two, "fsdp", self.back)
            new.append(self.two)
            self.pieces.append(self.two)
        return new


class RingSum:
    def __init__(self, part):
        self.part = part
        self.size = lax.axis_size("fsdp")
        self.half = self.size // 2
        self.ahead, self.back = ring_perms(self.size)
        self.pos = ring_position(self.size)
        self.done = 0
        self.one = self.term(self.half).astype(BF)
        self.two = self.term(1 - self.half).astype(BF)

    def term(self, away):
        return self.part(ring_index(self.pos + away, self.size))

    def hop(self, *earlier):
        one, two = hold((self.one, self.two), earlier)
        self.done += 1
        t, half = self.done, self.half
        one = lax.ppermute(one, "fsdp", self.ahead)
        if t < half:
            two = lax.ppermute(two, "fsdp", self.back)
        self.one, self.two = one, two
        return [one] if t == half else [one, two]

    def add(self, *earlier):
        one, two = hold((self.one, self.two), earlier)
        t, half = self.done, self.half
        self.one = (one.astype(F32) + self.term(half - t)).astype(BF)
        if t < half - 1:
            self.two = (two.astype(F32) + self.term(t + 1 - half)).astype(BF)
        return [self.one, self.two]

    def result(self):
        return self.term(0) + self.one.astype(F32) + self.two.astype(F32)


class TotalSum:
    def __init__(self, vector):
        self.vector = vector
        self.steps = []
        for axis in ("seq", "fsdp"):
            bits = lax.axis_size(axis) // 2
            while bits:
                self.steps.append((axis, bits))
                bits //= 2

    def hop(self, *earlier):
        vector = hold(self.vector, earlier)
        axis, bits = self.steps.pop(0)
        self.vector = vector + swap(vector, axis, bits)
        return [self.vector]


def local(
    inputs, image_ids, pad_mask, cotangent, w_qkv, w_out, w_up, w_down, ln1_gain, ln1_shift,
    q_bias, v_bias, out_bias, ln2_gain, ln2_shift, up_bias, down_bias,
):
    ns, nf = lax.axis_size("seq"), lax.axis_size("fsdp")
    s = lax.axis_index("seq")
    rows, width = inputs.shape[1:]
    n = rows * ns
    cols = width // ns
    band = w_up.shape[0]
    strip = w_down.shape[0]
    wide = lanes(-(-strip // ns) * nf)
    sub = wide // nf
    heads = HEADS // ns
    tile = 256
    order = [s ^ j for j in range(ns)]
    slots = jnp.stack([jnp.asarray(i, jnp.int32) for i in order])
    hops = nf // 8

    def row(vector):
        return vector[None, :]

    def own(vector):
        return lax.dynamic_slice_in_dim(vector, s * cols, cols)

    def own_hidden(array):
        count = array.shape[0]
        array = array.reshape(count, nf, strip)
        array = jnp.pad(array, ((0, 0), (0, 0), (0, ns * sub - strip)))
        return lax.dynamic_slice_in_dim(array, s * sub, sub, axis=2).reshape(count, wide)

    first = [lax.dynamic_slice_in_dim(w_qkv, t * width + s * cols, cols, axis=1) for t in range(3)]
    first.append(lax.dynamic_slice_in_dim(w_out, s * cols, cols, axis=1))
    ring_one = RingGather(jnp.concatenate(first, axis=1))
    x_own = inputs[0]
    code = (image_ids * 2 + pad_mask).astype(BF)
    x_pack = jnp.concatenate([x_own, jnp.pad(code, ((0, 15), (0, width - rows)))], axis=0)
    split = rows // 2
    x_parts = hold([x_pack[:split], x_pack[split:]], ring_one.one)
    far_a = far_swaps(x_parts[0])
    done = [far_a, *[ring_one.hop() for _ in range(hops)]]
    up_mine = own_hidden(w_up)
    keep = (1 - pad_mask[0]).astype(F32)[:, None]
    gy_own = (cotangent[0].astype(F32) * keep).astype(BF)
    gy_parts = [gy_own[:split], gy_own[split:]]
    down_mine = lax.dynamic_slice_in_dim(jnp.pad(w_down, ((0, ns * sub - strip), (0, 0))), s * sub, sub, axis=0)
    up_part = own_hidden(row(up_bias))
    q_part, v_part = row(own(q_bias)), row(own(v_bias))
    one_slots = jnp.stack([jnp.asarray(i, jnp.int32) for i in order + ring_one.indices()])
    done = [*done, up_mine]

    far_b, gy_parts, slots, one_slots = hold((x_parts[1], gy_parts, slots, one_slots), *done)
    far_b = far_swaps(far_b)
    done = [far_b, gy_parts, slots, one_slots, *[ring_one.hop(*done) for _ in range(hops)]]
    full_up = lax.all_gather(hold(up_mine, *done), "fsdp", axis=0, tiled=True)
    down_mine, up_part, q_part, v_part = hold((down_mine, up_part, q_part, v_part), *done)
    x_pack, far_a, far_b = hold((x_pack, far_a, far_b), *done)
    near, near_a, near_b = near_swaps([x_pack]), near_swaps(far_a), near_swaps(far_b)
    done = [near, near_a, near_b, down_mine, up_part, q_part, v_part, *[ring_one.hop(*done) for _ in range(hops)]]
    x_blocks = [[x_pack], [near[0]]]
    for i in range(ns // 2 - 1):
        x_blocks += [[far_a[i], far_b[i]], [near_a[i], near_b[i]]]
    gy_far_a = far_swaps(hold(gy_parts[0], *done))
    done = [gy_far_a, *[ring_one.hop(*done) for _ in range(hops)]]

    x_blocks, pieces, gy_parts = hold((x_blocks, ring_one.pieces, gy_parts), *done)
    gy_far_b = far_swaps(gy_parts[1])
    x_all, h_one, q, k, v, full_qkv, out_cols, code = project(
        x_blocks, pieces, one_slots, row(ln1_gain), row(ln1_shift), q_part, v_part, rows
    )
    full_down = lax.all_gather(hold(down_mine, q), "fsdp", axis=0, tiled=True)

    out_cols, gy_parts, gy_far_a, gy_far_b = hold((out_cols, gy_parts, gy_far_a, gy_far_b), q)
    out_far = far_swaps(out_cols)
    o, lse = attention_forward(q, k, v, code, heads, 384 if rows % 384 == 0 else tile)
    o, gy_parts, gy_far_a, gy_far_b, out_row = hold((o, gy_parts, gy_far_a, gy_far_b, [out_cols, *out_far]), o)
    o_row = [o, *far_swaps(o)]
    gy_near = [near_swaps([gy_parts[0], *gy_far_a]), near_swaps([gy_parts[1], *gy_far_b])]
    w_outs = woven(out_row, near_swaps(out_row))
    gy_all = jnp.zeros((n, width), BF)
    gy_rows = [woven([gy_parts[h], *far], near) for h, (far, near) in enumerate(zip((gy_far_a, gy_far_b), gy_near))]
    for h in range(2):
        for j in range(ns):
            gy_all = lax.dynamic_update_slice(gy_all, gy_rows[h][j], (order[j] * rows + h * split, 0))
    done = [o_row, w_outs, gy_all]
    o_row = hold(o_row, *done)
    os = woven(o_row, near_swaps(o_row))

    x_one, o_all, h_two, active, slope, full_out = widen(
        x_all, os, w_outs, slots, row(out_bias), row(ln2_gain), row(ln2_shift), full_up, up_part, rows
    )
    grad_down_part = dot_at(active, gy_all).astype(BF)
    down_sum = lax.psum_scatter(grad_down_part, "fsdp", scatter_dimension=0, tiled=True)
    active, gy_all = hold((active, gy_all), grad_down_part)
    gu, mixed, *far_dh, far_sum = narrow(gy_all, active, slope, full_up, full_down, slots, rows, 2, ns - 2, ())

    def cut(array, j):
        return array[j * rows : (j + 1) * rows]

    def summed(a, b):
        return (a.astype(F32) + b.astype(F32)).astype(BF)

    far_near = near_swaps(far_dh[1::2])
    far_near, gy_all, active = hold((far_near, gy_all, active), far_dh)
    far_held = [summed(far_dh[2 * i], got) for i, got in enumerate(far_near)]
    gu, mixed, far_held = hold((gu, mixed, far_held))
    terms = [swap(held, "seq", 2 * i + 2) for i, held in enumerate(far_held)]
    gu, mixed, *near_dh, near_sum = narrow(gy_all, active, slope, full_up, full_down, slots, rows, 0, 2, (gu, mixed))
    near_dh, terms = hold((near_dh, terms))
    terms += [near_dh[0], swap(near_dh[1], "seq", 1)]
    dx_one, sums_two, go_parts, ga_parts = middle(terms, x_one, gy_own, row(ln2_gain), full_out, slots, ns)
    go_parts, h_two, gu, mixed = hold((go_parts, h_two, gu, mixed))
    go_blocks = [block if j == 0 else swap(block, "seq", j) for j, block in enumerate(go_parts)]
    grad_up_part = dot_at(h_two, gu).astype(BF)
    up_sum = lax.psum_scatter(grad_up_part, "fsdp", scatter_dimension=0, tiled=True)

    def mixed_block(j):
        return lax.dynamic_slice_in_dim(mixed, order[j] * rows, rows, axis=0)

    mixed_near = near_swaps([mixed_block(j + 1) for j in range(0, ns, 2)])
    mixed_held = [summed(mixed_block(2 * i), mixed_near[i]) for i in range(1, ns // 2)]
    done = [go_blocks, grad_up_part, mixed_near, mixed_held]
    q, k, v, go_blocks, ga_parts, mixed_held = hold((q, k, v, go_blocks, ga_parts, mixed_held), *done)
    ga_blocks = [block if j == 0 else swap(block, "seq", j) for j, block in enumerate(ga_parts)]
    mixed_far = [swap(block, "seq", 2 * i + 2) for i, block in enumerate(mixed_held)]
    gqkv = attention_backward(q, k, v, o, go_blocks, 0, slots, lse, code, heads, tile)

    gqkv, ga_blocks, down_sum = hold((gqkv, ga_blocks, down_sum))

    def exchanged(pieces):
        return [piece if j == 0 else swap(piece, "seq", j) for j, piece in enumerate(pieces)]

    downs = exchanged([lax.dynamic_slice_in_dim(down_sum, order[j] * cols, cols, axis=1) for j in range(ns)])
    grad_part = weigh(h_one, gqkv, o_all, ga_blocks)

    def bands(owner):
        return lax.dynamic_slice_in_dim(grad_part, owner * band, band, axis=0).astype(F32)

    ring_sum = RingSum(bands)

    def ring_round(*earlier):
        new = []
        for _ in range(hops):
            if ring_sum.done:
                ring_sum.add(*earlier)
            new.append(ring_sum.hop(*earlier))
        return new

    gqkv = hold(gqkv, ring_sum.one, ring_sum.two)
    done = [ring_round(gqkv)]
    dh_one_part, sums_one = finish(gqkv, x_all, full_qkv, sums_two, far_sum, near_sum, slots, rows)
    totals = TotalSum(sums_one)
    done += [dh_one_part, mixed_far, downs]
    dh_one_part = hold(dh_one_part, *done)
    dh_near = near_swaps([cut(dh_one_part, j + 1) for j in range(0, ns, 2)])
    done = [dh_near, ring_round(*done), totals.hop(*done)]
    dh_near = hold(dh_near, *done)
    dh_held = [summed(cut(dh_one_part, 2 * i), dh_near[i]) for i in range(1, ns // 2)]
    dh_far_a = [swap(block[:split], "seq", 2 * i + 2) for i, block in enumerate(dh_held)]
    done = [dh_far_a, up_sum, ring_round(*done), totals.hop(*done)]
    dh_held = hold(dh_held, *done)
    dh_far_b = [swap(block[split:], "seq", 2 * i + 2) for i, block in enumerate(dh_held)]
    done = [dh_far_b, ring_round(*done), totals.hop(*done)]

    mine = hold(ring_sum.result(), *done)
    grad_out = mine[:, 3 * cols :]
    thirds = [mine[:, t * cols : (t + 1) * cols].astype(BF) for t in range(3)]
    got = []
    for p in range(3):
        perm = [((3 * d + p) % ns, d) for d in range(ns)]
        section = [0] * ns
        for d in range(ns):
            section[(3 * d + p) % ns] = (3 * d + p) // ns
        which = sum(jnp.where(s == i, t, 0) for i, t in enumerate(section))
        piece = jnp.where(which == 0, thirds[0], jnp.where(which == 1, thirds[1], thirds[2]))
        got.append(lax.ppermute(piece, "seq", perm))
    grad_qkv = jnp.concatenate(got, axis=1).astype(F32)
    total = totals.hop(*done)
    while totals.steps:
        total = totals.hop(total)

    share = nf // ns * sub
    ups = exchanged([lax.dynamic_slice_in_dim(up_sum, order[j] * share, share, axis=1) for j in range(ns)])
    grad_up, grad_down_t = settle(ups, downs, slots, strip)

    dh_far = [jnp.concatenate(pair, axis=0) for pair in zip(dh_far_a, dh_far_b)]
    dh_one = add_up([cut(dh_one_part, 0), dh_near[0], *dh_far])
    normal_x, inverse_x = normalise(x_own.astype(F32))
    grad_inputs = (dx_one + norm_back(normal_x, inverse_x, ln1_gain, dh_one)).astype(BF)
    layer_out = (x_one + add_up([mixed_block(0), mixed_near[0], *mixed_far]) + down_bias).astype(BF)
    total = totals.vector
    sum_hidden = jnp.swapaxes(total[8 : 8 + ns, :wide].reshape(ns, nf, sub), 0, 1).reshape(nf, ns * sub)
    sums = [total[i] for i in range(8)]
    sums.insert(7, sum_hidden[:, :strip].reshape(nf * strip))
    return (layer_out[None], grad_inputs[None], grad_qkv, grad_out, grad_up, grad_down_t.T, *sums)


def solution(mesh):
    tokens, weights, shared = P("fsdp", "seq", None), P("fsdp", None), P()
    marks, grads = P("fsdp", "seq"), P("fsdp", "seq")
    return jax.shard_map(
        local,
        mesh=mesh,
        in_specs=(tokens, marks, marks, tokens) + (weights,) * 4 + (shared,) * 9,
        out_specs=(tokens, tokens) + (grads,) * 4 + (shared,) * 9,
        check_vma=False,
    )
```

```python
import functools
import math

import jax
import jax.numpy as jnp
from jax import lax
from jax.experimental import pallas as pl
from jax.experimental.pallas import tpu as pltpu
from jax.sharding import PartitionSpec as P

HEADS = 16
HD = 72
IMG_TOK = 729
EPSILON = 1e-06
SCALING = HD ** (-0.5)
LOG2E = math.log2(math.e)
NEG = -1e30
BF = jnp.bfloat16
F32 = jnp.float32


def windows(heads, width):
    out = []
    for h in range(heads):
        lo = h * HD // 128 * 128
        out.append((lo, min(width, -(-(h * HD + HD) // 128) * 128)))
    return out


def head_lanes(lo, h, shape):
    lane = lax.broadcasted_iota(jnp.int32, shape, 1) + lo
    return (lane >= h * HD) & (lane < h * HD + HD)


def head_pieces(wins, outs):
    pieces = {}
    for (lo, hi), out in zip(wins, outs):
        for c in range(lo, hi, 128):
            part = out[:, c - lo : min(c + 128, hi) - lo]
            pieces[c] = part if c not in pieces else pieces[c] + part
    return pieces.items()


def lanes(width):
    return -(-width // 128) * 128


def load_blocks(blocks, target, slots, first, sems):
    rows = blocks[0].shape[0]
    copies = []
    for i, block in enumerate(blocks):
        start = pl.multiple_of(slots[first + i] * rows, 8)
        copies.append(pltpu.make_async_copy(block, target.at[pl.ds(start, rows)], sems.at[i]))
        copies[-1].start()
    for copy in copies:
        copy.wait()


def marks(code):
    ids = lax.shift_right_logical(code, 1)
    keys = jnp.where((code & 1) == 0, ids, -1)
    return ids.astype(F32), keys.astype(F32)


def key_tiles(mine, ids, tile):
    before = jnp.sum(jnp.where(ids < jnp.min(mine), 1.0, 0.0)).astype(jnp.int32)
    upto = jnp.sum(jnp.where(ids <= jnp.max(mine), 1.0, 0.0)).astype(jnp.int32)
    return before // tile, (upto + tile - 1) // tile


def most_tiles(tile, length):
    return min(length // tile, -(-(tile + 2 * IMG_TOK) // tile) + 1)


def column(row, width):
    return jnp.broadcast_to(row, (width, row.shape[1])).T


def forward_kernel(heads, tile, q_ref, k_ref, v_ref, code_ref, o_ref, lse_ref):
    i = pl.program_id(0)
    mine, _ = marks(code_ref[0:1, pl.ds(pl.multiple_of(i * tile, tile), tile)])
    lo, hi = key_tiles(mine, marks(code_ref[0:1, :])[0], tile)
    wins = windows(heads, q_ref.shape[1])

    def attend(count):
        size = count * tile
        rows = pl.ds(pl.multiple_of(lo * tile, tile), size)
        rel = lax.broadcasted_iota(jnp.int32, (tile, size), 0) - lax.broadcasted_iota(jnp.int32, (tile, size), 1)
        allowed = (jnp.concatenate([column(mine, 128)] * (size // 128), axis=1) == marks(code_ref[0:1, rows])[1]) | (rel == (lo - i) * tile)
        lane = lax.broadcasted_iota(jnp.int32, (tile, 128), 1)
        lse = jnp.zeros((tile, 128), F32)
        outs = []

        def scores(h):
            a, b = wins[h]
            w = q_ref[:, a:b]
            w = jnp.where(head_lanes(a, h, w.shape), w, jnp.zeros_like(w))
            return dot_bt(w, k_ref[rows, a:b])

        raw = scores(0)
        for h, (a, b) in enumerate(wins):
            s = jnp.where(allowed, raw * (SCALING * LOG2E), NEG)
            if h + 1 < heads:
                raw = scores(h + 1)
            top = jnp.max(s, axis=1, keepdims=True)
            p = jnp.exp2(s - top)
            total = jnp.sum(p, axis=1, keepdims=True)
            out = jnp.dot(p.astype(BF), v_ref[rows, a:b], preferred_element_type=F32) * (1.0 / total)
            outs.append(jnp.where(head_lanes(a, h, out.shape), out, 0.0))
            lse = jnp.where(lane == h, top + jnp.log2(total), lse)
        for c, part in head_pieces(wins, outs):
            o_ref[c : c + part.shape[1], :] = part.T.astype(BF)
        lse_ref[...] = lse.T[: lse_ref.shape[0], :]

    for count in range(1, most_tiles(tile, k_ref.shape[0]) + 1):
        pl.when(hi - lo == count)(functools.partial(attend, count))


def whole_block(shape):
    return pl.BlockSpec(shape, lambda *_: (0, 0))


def kept_block(shape):
    return pl.BlockSpec(shape, lambda *_: (0, 0), pipeline_mode=pl.Buffered(1))


def row_block(tile, width):
    return pl.BlockSpec((tile, width), lambda i, *_: (i, 0))


def lane_block(height, tile):
    return pl.BlockSpec((height, tile), lambda i, *_: (0, i))


def slot_block(tile, width):
    return pl.BlockSpec((tile, width), lambda i, slots: (slots[i], 0))


def attention_forward(q, k, v, code, heads, tile):
    n, width = q.shape
    return pl.pallas_call(
        functools.partial(forward_kernel, heads, tile),
        out_shape=(jax.ShapeDtypeStruct((width, n), BF), jax.ShapeDtypeStruct((8, n), F32)),
        grid_spec=pl.GridSpec(
            grid=(n // tile,),
            in_specs=[row_block(tile, width), whole_block((n, width)), whole_block((n, width)), whole_block((8, n))],
            out_specs=[lane_block(width, tile), lane_block(8, tile)],
        ),
        compiler_params=pltpu.CompilerParams(vmem_limit_bytes=56 << 20),
        cost_estimate=pl.CostEstimate(flops=4 * n * n * 128 * heads, bytes_accessed=10 * n * width, transcendentals=n * n * heads),
        name="attention_forward",
    )(q, k, v, code)


def backward_kernel(heads, tile, count, first, slots, q_ref, k_ref, v_ref, o_ref, lse_ref, code_ref, *refs):
    blocks, (out_ref, go_ref, dk_acc, dv_acc, kid_ref, sems) = refs[:count], refs[count:]
    i = pl.program_id(0)
    qid, _ = marks(code_ref[0:1, pl.ds(pl.multiple_of(i * tile, tile), tile)])
    lo, hi = key_tiles(qid, marks(code_ref[0:1, :])[0], tile)
    width = q_ref.shape[1]
    wins = windows(heads, width)

    @pl.when(i == 0)
    def _():
        copies = []
        for t, block in enumerate(blocks):
            size = block.shape[1]
            there = go_ref.at[:, pl.ds(pl.multiple_of(slots[t] * size, 128), size)]
            copies.append(pltpu.make_async_copy(block, there, sems.at[t]))
            copies[-1].start()
        for copy in copies:
            copy.wait()
        dk_acc[...] = jnp.zeros_like(dk_acc)
        dv_acc[...] = jnp.zeros_like(dv_acc)
        for t in range(0, kid_ref.shape[0], tile):
            kid_ref[t : t + tile, :] = column(marks(code_ref[0:1, t : t + tile])[1], 128)

    here = pl.ds(pl.multiple_of(i * tile, tile), tile)

    def attend(tiles):
        size = tiles * tile
        rows = pl.ds(pl.multiple_of(lo * tile, tile), size)
        rel = lax.broadcasted_iota(jnp.int32, (size, tile), 1) - lax.broadcasted_iota(jnp.int32, (size, tile), 0)
        allowed = (jnp.concatenate([kid_ref[rows, :]] * (tile // 128), axis=1) == qid) | (rel == (lo - i) * tile)
        go = go_ref[:, here]
        product = go.astype(F32) * o_ref[...].astype(F32)
        outs = []

        def products(h):
            a, b = wins[h]
            on = head_lanes(a, h, (tile, b - a))
            query = jnp.where(on, q_ref[:, a:b], jnp.zeros((tile, b - a), BF))
            unit = lax.broadcasted_iota(jnp.int32, (b - a, tile), 0) + a
            grad = jnp.where((unit >= h * HD) & (unit < h * HD + HD), go[a:b, :], jnp.zeros((b - a, tile), BF))
            return query, grad, dot_bt(k_ref[rows, a:b], query), dot(v_ref[rows, a:b], grad)

        ready = products(0)
        for h, (a, b) in enumerate(wins):
            query, grad, s, dp = ready
            if h + 1 < heads:
                ready = products(h + 1)
            inner = jnp.sum(product[h * HD : (h + 1) * HD, :], axis=0, keepdims=True)
            on = head_lanes(a, h, (tile, b - a))
            key = k_ref[rows, a:b]
            p = jnp.exp2(jnp.where(allowed, s * (SCALING * LOG2E) - lse_ref[h : h + 1, :], NEG))
            ds = (p * (dp - inner)).astype(BF)
            dv_acc[rows, a:b] += dot_bt(p.astype(BF), grad)
            dk_acc[rows, a:b] += dot(ds, query)
            outs.append(jnp.where(on, dot_at(ds, key) * SCALING, 0.0))
        for c, part in head_pieces(wins, outs):
            out_ref[here, c : c + part.shape[1]] = part.astype(BF)

    for tiles in range(1, most_tiles(tile, k_ref.shape[0]) + 1):
        pl.when(hi - lo == tiles)(functools.partial(attend, tiles))

    @pl.when(i == pl.num_programs(0) - 1)
    def _():
        out_ref[:, width : 2 * width] = (dk_acc[...] * SCALING).astype(BF)
        out_ref[:, 2 * width : 3 * width] = dv_acc[...].astype(BF)


def attention_backward(q, k, v, o, go_blocks, first, slots, lse, code, heads, tile):
    n, width = q.shape
    count = len(go_blocks)
    return pl.pallas_call(
        functools.partial(backward_kernel, heads, tile, count, first),
        out_shape=jax.ShapeDtypeStruct((n, 3 * width), BF),
        grid_spec=pltpu.PrefetchScalarGridSpec(
            num_scalar_prefetch=1,
            grid=(n // tile,),
            in_specs=[
                row_block(tile, width),
                whole_block((n, width)),
                whole_block((n, width)),
                lane_block(width, tile),
                lane_block(8, tile),
                whole_block((8, n)),
            ]
            + [pl.BlockSpec(memory_space=pl.ANY)] * count,
            out_specs=whole_block((n, 3 * width)),
            scratch_shapes=[
                pltpu.VMEM((go_blocks[0].shape[0], n), BF),
                pltpu.VMEM((n, width), F32),
                pltpu.VMEM((n, width), F32),
                pltpu.VMEM((n, 128), F32),
                pltpu.SemaphoreType.DMA((count,)),
            ],
        ),
        compiler_params=pltpu.CompilerParams(vmem_limit_bytes=56 << 20),
        cost_estimate=pl.CostEstimate(flops=10 * n * n * 128 * heads, bytes_accessed=16 * n * width, transcendentals=n * n * heads),
        name="attention_backward",
    )(slots, q, k, v, o, lse, code, *go_blocks)


def normalise(values):
    average = jnp.mean(values, axis=-1, keepdims=True)
    centred = values - average
    spread = jnp.mean(centred * centred, axis=-1, keepdims=True)
    inverse = lax.rsqrt(spread + EPSILON)
    return centred * inverse, inverse


def norm_back(normal, inverse, gain, grad):
    scaled = grad * gain
    first = jnp.mean(scaled, axis=-1, keepdims=True)
    second = jnp.mean(scaled * normal, axis=-1, keepdims=True)
    return (scaled - first - normal * second) * inverse


def gelu_both(u):
    root = math.sqrt(2.0 / math.pi)
    bent = jnp.tanh(root * (u + 0.044715 * u * u * u))
    half = 0.5 * (1.0 + bent)
    slope = half + 0.5 * u * (1.0 - bent * bent) * (root + 3 * 0.044715 * root * u * u)
    return u * half, slope


def dot(a, b):
    return jnp.dot(a, b, preferred_element_type=F32)


def dot_bt(a, b):
    return lax.dot_general(a, b, (((1,), (1,)), ((), ())), preferred_element_type=F32)


def dot_at(a, b):
    return lax.dot_general(a, b, (((0,), (0,)), ((), ())), preferred_element_type=F32)


def row_parts(rows):
    return [slice(0, 256), slice(256, rows)]


def deal_kernel(count, strips, slots, w_ref, out_ref):
    strip, sub = w_ref.shape[1] // strips, out_ref.shape[1] // strips
    out_ref[...] = jnp.zeros_like(out_ref)
    for v in range(count):
        size = min(sub, strip - v * sub)
        if size > 0:

            @pl.when(slots[0] == v)
            def _(v=v, size=size):
                for f in range(strips):
                    start = f * strip + v * sub
                    out_ref[:, f * sub : f * sub + size] = w_ref[:, start : start + size]


def deal(w_up, slots, count, strips, wide):
    band, hidden = w_up.shape
    return pl.pallas_call(
        functools.partial(deal_kernel, count, strips),
        out_shape=jax.ShapeDtypeStruct((band, wide), BF),
        grid_spec=pltpu.PrefetchScalarGridSpec(
            num_scalar_prefetch=1,
            grid=(1,),
            in_specs=[kept_block((band, hidden))],
            out_specs=whole_block((band, wide)),
        ),
        cost_estimate=pl.CostEstimate(flops=0, bytes_accessed=2 * band * (hidden + wide), transcendentals=0),
        name="deal_hidden",
    )(slots, w_up)


def project_kernel(counts, bands, slots, *refs):
    xs, pieces = refs[: sum(counts)], refs[sum(counts) : sum(counts) + bands]
    gain, shift, q_bias, v_bias, x_out, h_out, q_out, k_out, v_out, w_out, out_out, code_out, x_now, sems = refs[
        sum(counts) + bands :
    ]
    j = pl.program_id(0)
    rows, cols = q_out.shape

    @pl.when(j == 0)
    def _():
        load_blocks(pieces, w_out, slots, len(counts), sems)
        out_out[:, :cols] = w_out[:, 3 * cols :]

    at = 0
    for i, count in enumerate(counts):

        @pl.when(j == i)
        def _(parts=xs[at : at + count]):
            start = 0
            for part in parts:
                size = min(part.shape[0], rows - start)
                x_now[start : start + size, :] = part[:size, :]
                start += size
            last = parts[-1].shape[0] - 16
            code = parts[-1][last:, :rows].astype(F32)[0:1, :]
            code_out[...] = jnp.broadcast_to(code, code_out.shape).astype(jnp.int32)

        at += count
    x = x_now[...]
    x_out[...] = x
    normal, _ = normalise(x.astype(F32))
    h = (normal * gain[...] + shift[...]).astype(BF)
    h_out[...] = h
    projected = dot(h, w_out[...])
    q_out[...] = (projected[:, :cols] + q_bias[...]).astype(BF)
    k_out[...] = projected[:, cols : 2 * cols].astype(BF)
    v_out[...] = (projected[:, 2 * cols : 3 * cols] + v_bias[...]).astype(BF)


def project(xs, pieces, slots, gain, shift, q_bias, v_bias, rows):
    width, cols, bands = xs[0][0].shape[1], q_bias.shape[1], len(pieces)
    counts = tuple(len(parts) for parts in xs)
    xs = [part for parts in xs for part in parts]
    n, columns = rows * len(counts), pieces[0].shape[1]
    shape = jax.ShapeDtypeStruct
    return pl.pallas_call(
        functools.partial(project_kernel, counts, bands),
        out_shape=[shape((n, width), BF)] * 2
        + [shape((n, cols), BF)] * 3
        + [shape((width, columns), BF), shape((width, lanes(cols)), BF), shape((8, n), jnp.int32)],
        grid_spec=pltpu.PrefetchScalarGridSpec(
            num_scalar_prefetch=1,
            grid=(len(counts),),
            in_specs=[kept_block(part.shape) for part in xs]
            + [pl.BlockSpec(memory_space=pl.ANY)] * bands
            + [kept_block((1, width))] * 2
            + [kept_block((1, cols))] * 2,
            out_specs=[slot_block(rows, width)] * 2
            + [slot_block(rows, cols)] * 3
            + [
                whole_block((width, columns)),
                whole_block((width, lanes(cols))),
                pl.BlockSpec((8, rows), lambda i, slots: (0, slots[i])),
            ],
            scratch_shapes=[pltpu.VMEM((rows, width), BF), pltpu.SemaphoreType.DMA((bands,))],
        ),
        compiler_params=pltpu.CompilerParams(vmem_limit_bytes=56 << 20),
        cost_estimate=pl.CostEstimate(flops=2 * n * width * columns, bytes_accessed=8 * n * width, transcendentals=n),
        name="norm_project",
    )(slots, *xs, *pieces, gain, shift, q_bias, v_bias)


def widen_kernel(count, slots, x_ref, *refs):
    os, w_outs = refs[:count], refs[count : 2 * count]
    (out_bias, gain, shift, w_up, up_bias, x_out, o_out, h_out, a_out, slope_out, w_out) = refs[2 * count :]
    j = pl.program_id(0)
    cols = os[0].shape[0]
    for v in range(count):

        @pl.when((j == 0) & (slots[0] == v))
        def _(v=v):
            for i in range(count):
                start = (v ^ i) * cols
                w_out[:, start : start + cols] = w_outs[i][:, :cols]

    for i in range(count):
        o_out[pl.ds(pl.multiple_of(slots[i] * cols, 8), cols), :] = os[i][...]
    parts = row_parts(x_ref.shape[0])

    def branch(part):
        return dot_at(o_out[:, part], w_out[...])

    def norm(part, product):
        x = x_ref[part, :].astype(F32) + (product + out_bias[...])
        x_out[part, :] = jnp.where(j == 0, x, x_out[part, :])
        h = (normalise(x)[0] * gain[...] + shift[...]).astype(BF)
        h_out[part, :] = h
        return h

    def bend(part, u):
        value, slope = gelu_both(u + up_bias[...])
        a_out[part, :] = value.astype(BF)
        slope_out[part, :] = slope.astype(BF)

    products, us = {}, {}
    for t in range(len(parts) + 2):
        if t < len(parts):
            products[t] = branch(parts[t])
        if 0 <= t - 1 < len(parts):
            us[t - 1] = dot(norm(parts[t - 1], products[t - 1]), w_up[...])
        if 0 <= t - 2 < len(parts):
            bend(parts[t - 2], us[t - 2])


def widen(x_all, os, w_outs, slots, out_bias, gain, shift, w_up, up_bias, rows):
    n, width = x_all.shape
    count, cols, hidden = len(os), os[0].shape[0], up_bias.shape[1]
    shape = jax.ShapeDtypeStruct
    return pl.pallas_call(
        functools.partial(widen_kernel, count),
        out_shape=[
            shape((rows, width), F32),
            shape((width, n), BF),
            shape((n, width), BF),
            shape((n, hidden), BF),
            shape((n, hidden), BF),
            shape((width, width), BF),
        ],
        grid_spec=pltpu.PrefetchScalarGridSpec(
            num_scalar_prefetch=1,
            grid=(count,),
            in_specs=[slot_block(rows, width)]
            + [pl.BlockSpec((cols, rows), lambda i, slots: (0, slots[i]))] * count
            + [kept_block(w_outs[0].shape)] * count
            + [kept_block((1, width))] * 3
            + [kept_block((width, hidden)), kept_block((1, hidden))],
            out_specs=[whole_block((rows, width)), lane_block(width, rows), slot_block(rows, width)]
            + [slot_block(rows, hidden)] * 2
            + [whole_block((width, width))],
        ),
        compiler_params=pltpu.CompilerParams(vmem_limit_bytes=60 << 20),
        cost_estimate=pl.CostEstimate(flops=2 * n * width * (width + hidden), bytes_accessed=16 * n * width, transcendentals=n * hidden),
        name="out_norm_up",
    )(slots, x_all, *os, *w_outs, out_bias, gain, shift, w_up, up_bias)


def narrow_kernel(count, slots, gy_ref, a_ref, slope_ref, w_up, w_down, *refs):
    dh_outs = refs[len(refs) - 1 - count : -1]
    gu_out, y_out = refs[len(refs) - 3 - count : len(refs) - 1 - count]
    sum_out = refs[-1]

    @pl.when(pl.program_id(0) == 0)
    def _():
        sum_out[...] = jnp.zeros_like(sum_out)

    gu = (dot_bt(gy_ref[...], w_down[...]) * slope_ref[...]).astype(BF)
    gu_out[...] = gu
    dh = dot_bt(gu, w_up[...]).astype(BF)
    for i in range(count):

        @pl.when(pl.program_id(0) == i)
        def _(i=i):
            dh_outs[i][...] = dh

    y_out[...] = dot(a_ref[...], w_down[...]).astype(BF)
    sum_out[...] += jnp.sum(gu.astype(F32), axis=0, keepdims=True)


def narrow(gy, active, slope, w_up, w_down, slots, rows, first, count, carried):
    n, width = gy.shape
    hidden = w_up.shape[1]
    shape = jax.ShapeDtypeStruct

    def block(size):
        return pl.BlockSpec((rows, size), lambda i, slots: (slots[first + i], 0))

    return pl.pallas_call(
        functools.partial(narrow_kernel, count),
        out_shape=[shape((n, hidden), BF), shape((n, width), BF)]
        + [shape((rows, width), BF)] * count
        + [shape((1, hidden), F32)],
        grid_spec=pltpu.PrefetchScalarGridSpec(
            num_scalar_prefetch=1,
            grid=(count,),
            in_specs=[block(width), block(hidden), block(hidden)]
            + [kept_block((width, hidden)), kept_block((hidden, width))]
            + [pl.BlockSpec(memory_space=pl.ANY)] * len(carried),
            out_specs=[block(hidden), block(width)] + [whole_block((rows, width))] * count + [whole_block((1, hidden))],
        ),
        input_output_aliases={6 + i: i for i in range(len(carried))},
        compiler_params=pltpu.CompilerParams(vmem_limit_bytes=56 << 20),
        cost_estimate=pl.CostEstimate(flops=6 * rows * count * width * hidden, bytes_accessed=16 * rows * count * width, transcendentals=0),
        name="down_and_back",
    )(slots, gy, active, slope, w_up, w_down, *carried)


def finish_kernel(count, slots, g_ref, x_ref, w_qkv, mid_ref, far_ref, near_ref, dh_out, sum_out, bias_acc):
    j = pl.program_id(0)

    @pl.when(j == 0)
    def _():
        sum_out[...] = jnp.zeros_like(sum_out)
        bias_acc[...] = jnp.zeros_like(bias_acc)

    g = g_ref[...]
    dh = dot_bt(g, w_qkv[:, : g.shape[1]])
    dh_out[...] = dh.astype(BF)
    normal, _ = normalise(x_ref[...].astype(F32))
    sum_out[0:1, :] += jnp.sum(dh * normal, axis=0, keepdims=True)
    sum_out[1:2, :] += jnp.sum(dh, axis=0, keepdims=True)
    bias_acc[...] += jnp.sum(g.astype(F32), axis=0, keepdims=True)
    cols, wide = g.shape[1] // 3, far_ref.shape[1]

    @pl.when(j == count - 1)
    def _():
        sum_out[4:5, :] = mid_ref[2:3, :]
        sum_out[5:7, :] = mid_ref[0:2, :]
        sum_out[7:8, :] = mid_ref[3:4, :]
        for v in range(count):

            @pl.when(slots[0] == v)
            def _(v=v):
                sum_out[2:3, v * cols : (v + 1) * cols] = bias_acc[:, :cols]
                sum_out[3:4, v * cols : (v + 1) * cols] = bias_acc[:, 2 * cols :]
                sum_out[8 + v : 9 + v, :wide] = far_ref[...] + near_ref[...]


def finish(gqkv, x_all, w_qkv, mid, far_sum, near_sum, slots, rows):
    n, width = x_all.shape
    columns, count, wide = gqkv.shape[1], n // rows, far_sum.shape[1]
    height = -(-(8 + count) // 8) * 8
    shape = jax.ShapeDtypeStruct
    return pl.pallas_call(
        functools.partial(finish_kernel, count),
        out_shape=[shape((n, width), BF), shape((height, width), F32)],
        grid_spec=pltpu.PrefetchScalarGridSpec(
            num_scalar_prefetch=1,
            grid=(count,),
            in_specs=[slot_block(rows, columns), slot_block(rows, width), kept_block(w_qkv.shape)]
            + [kept_block(mid.shape), kept_block((1, wide)), kept_block((1, wide))],
            out_specs=[row_block(rows, width), whole_block((height, width))],
            scratch_shapes=[pltpu.VMEM((1, columns), F32)],
        ),
        compiler_params=pltpu.CompilerParams(vmem_limit_bytes=56 << 20),
        cost_estimate=pl.CostEstimate(flops=2 * n * width * columns, bytes_accessed=8 * n * width, transcendentals=n),
        name="project_back",
    )(slots, gqkv, x_all, w_qkv, mid, far_sum, near_sum)


def settle_kernel(count, slots, *refs):
    ups, downs, (up_out, down_out) = refs[:count], refs[count : 2 * count], refs[2 * count :]
    strip = down_out.shape[1]
    sub = downs[0].shape[0]
    ratio = ups[0].shape[1] // sub
    for v in range(count):

        @pl.when(slots[0] == v)
        def _(v=v):
            for i in range(count):
                start = (v ^ i) * sub
                size = min(sub, strip - start)
                if size > 0:
                    down_out[:, start : start + size] = downs[i][:size, :].astype(F32).T
                    for h in range(ratio):
                        piece = ups[i][:, h * sub : h * sub + size]
                        up_out[:, h * strip + start : h * strip + start + size] = piece.astype(F32)


def settle(ups, downs, slots, strip):
    band, sub, cols = ups[0].shape[0], downs[0].shape[0], downs[0].shape[1]
    ratio, count = ups[0].shape[1] // sub, len(ups)
    shape = jax.ShapeDtypeStruct
    return pl.pallas_call(
        functools.partial(settle_kernel, count),
        out_shape=[shape((band, ratio * strip), F32), shape((cols, strip), F32)],
        grid_spec=pltpu.PrefetchScalarGridSpec(
            num_scalar_prefetch=1,
            grid=(1,),
            in_specs=[kept_block(ups[0].shape)] * count + [kept_block(downs[0].shape)] * count,
            out_specs=[whole_block((band, ratio * strip)), whole_block((cols, strip))],
        ),
        compiler_params=pltpu.CompilerParams(vmem_limit_bytes=56 << 20),
        name="settle_hidden",
    )(slots, *ups, *downs)


def weigh_kernel(count, h_ref, g_ref, o_ref, *refs):
    gas, (out_ref, ga_now) = refs[:count], refs[count:]
    rows = gas[0].shape[0]

    @pl.when(pl.program_id(0) == 0)
    def _():
        for i in range(count):
            ga_now[i * rows : (i + 1) * rows, :] = gas[i][...]

    columns = g_ref.shape[1]
    out_ref[:, :columns] = dot_at(h_ref[...], g_ref[...]).astype(BF)
    out_ref[:, columns:] = dot(o_ref[...], ga_now[...]).astype(BF)


def weigh(h_one, gqkv, o_all, gas):
    n, width = h_one.shape
    rows, cols = gas[0].shape
    columns, tile = gqkv.shape[1], width // 3
    return pl.pallas_call(
        functools.partial(weigh_kernel, len(gas)),
        out_shape=jax.ShapeDtypeStruct((width, columns + cols), BF),
        grid_spec=pl.GridSpec(
            grid=(width // tile,),
            in_specs=[lane_block(n, tile), kept_block((n, columns)), row_block(tile, n)] + [kept_block((rows, cols))] * len(gas),
            out_specs=row_block(tile, columns + cols),
            scratch_shapes=[pltpu.VMEM((n, cols), BF)],
        ),
        compiler_params=pltpu.CompilerParams(vmem_limit_bytes=56 << 20),
        cost_estimate=pl.CostEstimate(flops=2 * n * width * (columns + cols), bytes_accessed=6 * n * width, transcendentals=0),
        name="grads_qkv_out",
    )(h_one, gqkv, o_all, *gas)


def middle_kernel(count, terms, slots, *refs):
    parts, (x_ref, gy_ref, gain, w_out, dx_out, sum_out) = refs[:terms], refs[terms : terms + 6]
    go_outs, ga_outs = refs[terms + 6 : terms + 6 + count], refs[terms + 6 + count :]
    grad = sum(part[...].astype(F32) for part in parts)
    normal, inverse = normalise(x_ref[...])
    dx = gy_ref[...].astype(F32) + norm_back(normal, inverse, gain[...], grad)
    dx_out[...] = dx
    ga = dx.astype(BF)
    sum_out[0:1, :] = jnp.sum(grad * normal, axis=0, keepdims=True)
    sum_out[1:2, :] = jnp.sum(grad, axis=0, keepdims=True)
    sum_out[2:3, :] = jnp.sum(ga.astype(F32), axis=0, keepdims=True)
    sum_out[3:4, :] = jnp.sum(gy_ref[...].astype(F32), axis=0, keepdims=True)
    cols = ga_outs[0].shape[1]
    for i in range(count):
        rows = pl.ds(pl.multiple_of(slots[i] * cols, 8), cols)
        go_outs[i][...] = dot_bt(w_out[rows, :], ga).astype(BF)
    for v in range(count):

        @pl.when(slots[0] == v)
        def _(v=v):
            for i in range(count):
                start = (v ^ i) * cols
                ga_outs[i][...] = ga[:, start : start + cols]


def middle(parts, x_one, gy, gain, w_out, slots, count):
    rows, width = x_one.shape
    cols, terms = width // count, len(parts)
    shape = jax.ShapeDtypeStruct
    block = kept_block((rows, width))
    outs = pl.pallas_call(
        functools.partial(middle_kernel, count, terms),
        out_shape=[shape((rows, width), F32), shape((8, width), F32)]
        + [shape((cols, rows), BF)] * count
        + [shape((rows, cols), BF)] * count,
        grid_spec=pltpu.PrefetchScalarGridSpec(
            num_scalar_prefetch=1,
            grid=(1,),
            in_specs=[block] * (terms + 2) + [kept_block((1, width)), kept_block((width, width))],
            out_specs=[whole_block((rows, width)), whole_block((8, width))]
            + [whole_block((cols, rows))] * count
            + [whole_block((rows, cols))] * count,
        ),
        compiler_params=pltpu.CompilerParams(vmem_limit_bytes=56 << 20),
        cost_estimate=pl.CostEstimate(flops=2 * rows * width * width, bytes_accessed=20 * rows * width, transcendentals=rows),
        name="norm_back_out",
    )(slots, *parts, x_one, gy, gain, w_out)
    return outs[0], outs[1], outs[2 : 2 + count], outs[2 + count :]


def swap(value, axis, bits):
    size = lax.axis_size(axis)
    return lax.ppermute(value, axis, [(i, i ^ bits) for i in range(size)])


def hold(values, *earlier):
    return lax.optimization_barrier((values, earlier))[0]


def far_swaps(block):
    return [swap(block, "seq", j) for j in range(2, lax.axis_size("seq"), 2)]


def near_swaps(blocks):
    return [swap(block, "seq", 1) for block in blocks]


def woven(own, near):
    return [block for pair in zip(own, near) for block in pair]


def add_up(terms):
    return sum(term.astype(F32) for term in terms)


def ring_order(size):
    half = size // 2
    return [2 * p if p < half else 2 * (size - 1 - p) + 1 for p in range(size)]


def ring_index(pos, size):
    pos = pos % size
    return jnp.where(pos < size // 2, 2 * pos, 2 * (size - 1 - pos) + 1)


def ring_perms(size):
    order = ring_order(size)
    ahead = [(order[p], order[(p + 1) % size]) for p in range(size)]
    return ahead, [(b, a) for a, b in ahead]


def ring_position(size):
    f = lax.axis_index("fsdp")
    return jnp.where(f % 2 == 0, f // 2, size - 1 - f // 2)


class RingGather:
    def __init__(self, block):
        self.size = lax.axis_size("fsdp")
        self.ahead, self.back = ring_perms(self.size)
        self.pos = ring_position(self.size)
        self.pieces = [block]
        self.one = self.two = block
        self.done = 0

    def indices(self):
        owners = [ring_index(self.pos, self.size)]
        for t in range(1, self.size // 2 + 1):
            owners.append(ring_index(self.pos - t, self.size))
            if t < self.size // 2:
                owners.append(ring_index(self.pos + t, self.size))
        return owners

    def hop(self, *earlier):
        one, two = hold((self.one, self.two), earlier)
        self.done += 1
        self.one = lax.ppermute(one, "fsdp", self.ahead)
        new = [self.one]
        self.pieces.append(self.one)
        if self.done < self.size // 2:
            self.two = lax.ppermute(two, "fsdp", self.back)
            new.append(self.two)
            self.pieces.append(self.two)
        return new


class RingSum:
    def __init__(self, part):
        self.part = part
        self.size = lax.axis_size("fsdp")
        self.half = self.size // 2
        self.ahead, self.back = ring_perms(self.size)
        self.pos = ring_position(self.size)
        self.done = 0
        self.one = self.term(self.half).astype(BF)
        self.two = self.term(1 - self.half).astype(BF)

    def term(self, away):
        return self.part(ring_index(self.pos + away, self.size))

    def hop(self, *earlier):
        one, two = hold((self.one, self.two), earlier)
        self.done += 1
        t, half = self.done, self.half
        one = lax.ppermute(one, "fsdp", self.ahead)
        if t < half:
            two = lax.ppermute(two, "fsdp", self.back)
        self.one, self.two = one, two
        return [one] if t == half else [one, two]

    def add(self, *earlier):
        one, two = hold((self.one, self.two), earlier)
        t, half = self.done, self.half
        self.one = (one.astype(F32) + self.term(half - t)).astype(BF)
        if t < half - 1:
            self.two = (two.astype(F32) + self.term(t + 1 - half)).astype(BF)
        return [self.one, self.two]

    def result(self):
        return self.term(0) + self.one.astype(F32) + self.two.astype(F32)


class TotalSum:
    def __init__(self, vector):
        self.vector = vector
        self.steps = []
        for axis in ("seq", "fsdp"):
            bits = lax.axis_size(axis) // 2
            while bits:
                self.steps.append((axis, bits))
                bits //= 2

    def hop(self, *earlier):
        vector = hold(self.vector, earlier)
        axis, bits = self.steps.pop(0)
        self.vector = vector + swap(vector, axis, bits)
        return [self.vector]


def local(
    inputs, image_ids, pad_mask, cotangent, w_qkv, w_out, w_up, w_down, ln1_gain, ln1_shift,
    q_bias, v_bias, out_bias, ln2_gain, ln2_shift, up_bias, down_bias,
):
    ns, nf = lax.axis_size("seq"), lax.axis_size("fsdp")
    s = lax.axis_index("seq")
    rows, width = inputs.shape[1:]
    n = rows * ns
    cols = width // ns
    band = w_up.shape[0]
    strip = w_down.shape[0]
    wide = lanes(-(-strip // ns) * nf)
    sub = wide // nf
    heads = HEADS // ns
    tile = 256
    order = [s ^ j for j in range(ns)]
    slots = jnp.stack([jnp.asarray(i, jnp.int32) for i in order])
    hops = nf // 8

    def row(vector):
        return vector[None, :]

    def own(vector):
        return lax.dynamic_slice_in_dim(vector, s * cols, cols)

    def own_hidden(array):
        count = array.shape[0]
        array = array.reshape(count, nf, strip)
        array = jnp.pad(array, ((0, 0), (0, 0), (0, ns * sub - strip)))
        return lax.dynamic_slice_in_dim(array, s * sub, sub, axis=2).reshape(count, wide)

    first = [lax.dynamic_slice_in_dim(w_qkv, t * width + s * cols, cols, axis=1) for t in range(3)]
    first.append(lax.dynamic_slice_in_dim(w_out, s * cols, cols, axis=1))
    ring_one = RingGather(jnp.concatenate(first, axis=1))
    x_own = inputs[0]
    code = (image_ids * 2 + pad_mask).astype(BF)
    x_pack = jnp.concatenate([x_own, jnp.pad(code, ((0, 15), (0, width - rows)))], axis=0)
    split = rows // 2
    x_parts = hold([x_pack[:split], x_pack[split:]], ring_one.one)
    far_a = far_swaps(x_parts[0])
    done = [far_a, *[ring_one.hop() for _ in range(hops)]]
    up_mine = deal(w_up, slots, ns, nf, wide)
    keep = (1 - pad_mask[0]).astype(F32)[:, None]
    gy_own = (cotangent[0].astype(F32) * keep).astype(BF)
    gy_parts = [gy_own[:split], gy_own[split:]]
    down_mine = lax.dynamic_slice_in_dim(jnp.pad(w_down, ((0, ns * sub - strip), (0, 0))), s * sub, sub, axis=0)
    up_part = own_hidden(row(up_bias))
    q_part, v_part = row(own(q_bias)), row(own(v_bias))
    one_slots = jnp.stack([jnp.asarray(i, jnp.int32) for i in order + ring_one.indices()])
    done = [*done, up_mine]

    far_b, gy_parts, slots, one_slots = hold((x_parts[1], gy_parts, slots, one_slots), *done)
    far_b = far_swaps(far_b)
    done = [far_b, gy_parts, slots, one_slots, *[ring_one.hop(*done) for _ in range(hops)]]
    full_up = lax.all_gather(hold(up_mine, *done), "fsdp", axis=0, tiled=True)
    down_mine, up_part, q_part, v_part = hold((down_mine, up_part, q_part, v_part), *done)
    x_pack, far_a, far_b = hold((x_pack, far_a, far_b), *done)
    near, near_a, near_b = near_swaps([x_pack]), near_swaps(far_a), near_swaps(far_b)
    done = [near, near_a, near_b, down_mine, up_part, q_part, v_part, *[ring_one.hop(*done) for _ in range(hops)]]
    x_blocks = [[x_pack], [near[0]]]
    for i in range(ns // 2 - 1):
        x_blocks += [[far_a[i], far_b[i]], [near_a[i], near_b[i]]]
    gy_far_a = far_swaps(hold(gy_parts[0], *done))
    done = [gy_far_a, *[ring_one.hop(*done) for _ in range(hops)]]

    x_blocks, pieces, gy_parts = hold((x_blocks, ring_one.pieces, gy_parts), *done)
    gy_far_b = far_swaps(gy_parts[1])
    x_all, h_one, q, k, v, full_qkv, out_cols, code = project(
        x_blocks, pieces, one_slots, row(ln1_gain), row(ln1_shift), q_part, v_part, rows
    )
    full_down = lax.all_gather(hold(down_mine, q), "fsdp", axis=0, tiled=True)

    out_cols, gy_parts, gy_far_a, gy_far_b = hold((out_cols, gy_parts, gy_far_a, gy_far_b), q)
    out_far = far_swaps(out_cols)
    o, lse = attention_forward(q, k, v, code, heads, 384 if rows % 384 == 0 else tile)
    o, gy_parts, gy_far_a, gy_far_b, out_row = hold((o, gy_parts, gy_far_a, gy_far_b, [out_cols, *out_far]), o)
    o_row = [o, *far_swaps(o)]
    gy_near = [near_swaps([gy_parts[0], *gy_far_a]), near_swaps([gy_parts[1], *gy_far_b])]
    w_outs = woven(out_row, near_swaps(out_row))
    gy_all = jnp.zeros((n, width), BF)
    gy_rows = [woven([gy_parts[h], *far], near) for h, (far, near) in enumerate(zip((gy_far_a, gy_far_b), gy_near))]
    for h in range(2):
        for j in range(ns):
            gy_all = lax.dynamic_update_slice(gy_all, gy_rows[h][j], (order[j] * rows + h * split, 0))
    done = [o_row, w_outs, gy_all]
    o_row = hold(o_row, *done)
    os = woven(o_row, near_swaps(o_row))

    x_one, o_all, h_two, active, slope, full_out = widen(
        x_all, os, w_outs, slots, row(out_bias), row(ln2_gain), row(ln2_shift), full_up, up_part, rows
    )
    grad_down_part = dot_at(active, gy_all).astype(BF)
    down_sum = lax.psum_scatter(grad_down_part, "fsdp", scatter_dimension=0, tiled=True)
    active, gy_all = hold((active, gy_all), grad_down_part)
    gu, mixed, *far_dh, far_sum = narrow(gy_all, active, slope, full_up, full_down, slots, rows, 2, ns - 2, ())

    def cut(array, j):
        return array[j * rows : (j + 1) * rows]

    def summed(a, b):
        return (a.astype(F32) + b.astype(F32)).astype(BF)

    far_near = near_swaps(far_dh[1::2])
    far_near, gy_all, active = hold((far_near, gy_all, active), far_dh)
    far_held = [summed(far_dh[2 * i], got) for i, got in enumerate(far_near)]
    gu, mixed, far_held = hold((gu, mixed, far_held))
    terms = [swap(held, "seq", 2 * i + 2) for i, held in enumerate(far_held)]
    gu, mixed, *near_dh, near_sum = narrow(gy_all, active, slope, full_up, full_down, slots, rows, 0, 2, (gu, mixed))
    near_dh, terms = hold((near_dh, terms))
    terms += [near_dh[0], swap(near_dh[1], "seq", 1)]
    dx_one, sums_two, go_parts, ga_parts = middle(terms, x_one, gy_own, row(ln2_gain), full_out, slots, ns)
    go_parts, h_two, gu, mixed = hold((go_parts, h_two, gu, mixed))
    go_blocks = [block if j == 0 else swap(block, "seq", j) for j, block in enumerate(go_parts)]
    grad_up_part = dot_at(h_two, gu).astype(BF)
    up_sum = lax.psum_scatter(grad_up_part, "fsdp", scatter_dimension=0, tiled=True)

    def mixed_block(j):
        return lax.dynamic_slice_in_dim(mixed, order[j] * rows, rows, axis=0)

    mixed_near = near_swaps([mixed_block(j + 1) for j in range(0, ns, 2)])
    mixed_held = [summed(mixed_block(2 * i), mixed_near[i]) for i in range(1, ns // 2)]
    done = [go_blocks, grad_up_part, mixed_near, mixed_held]
    q, k, v, go_blocks, ga_parts, mixed_held = hold((q, k, v, go_blocks, ga_parts, mixed_held), *done)
    ga_blocks = [block if j == 0 else swap(block, "seq", j) for j, block in enumerate(ga_parts)]
    mixed_far = [swap(block, "seq", 2 * i + 2) for i, block in enumerate(mixed_held)]
    gqkv = attention_backward(q, k, v, o, go_blocks, 0, slots, lse, code, heads, tile)

    gqkv, ga_blocks, down_sum = hold((gqkv, ga_blocks, down_sum))

    def exchanged(pieces):
        return [piece if j == 0 else swap(piece, "seq", j) for j, piece in enumerate(pieces)]

    downs = exchanged([lax.dynamic_slice_in_dim(down_sum, order[j] * cols, cols, axis=1) for j in range(ns)])
    grad_part = weigh(h_one, gqkv, o_all, ga_blocks)

    def bands(owner):
        return lax.dynamic_slice_in_dim(grad_part, owner * band, band, axis=0).astype(F32)

    ring_sum = RingSum(bands)

    def ring_round(*earlier):
        new = []
        for _ in range(hops):
            if ring_sum.done:
                ring_sum.add(*earlier)
            new.append(ring_sum.hop(*earlier))
        return new

    gqkv = hold(gqkv, ring_sum.one, ring_sum.two)
    done = [ring_round(gqkv)]
    dh_one_part, sums_one = finish(gqkv, x_all, full_qkv, sums_two, far_sum, near_sum, slots, rows)
    totals = TotalSum(sums_one)
    done += [dh_one_part, mixed_far, downs]
    dh_one_part = hold(dh_one_part, *done)
    dh_near = near_swaps([cut(dh_one_part, j + 1) for j in range(0, ns, 2)])
    done = [dh_near, ring_round(*done), totals.hop(*done)]
    dh_near = hold(dh_near, *done)
    dh_held = [summed(cut(dh_one_part, 2 * i), dh_near[i]) for i in range(1, ns // 2)]
    dh_far_a = [swap(block[:split], "seq", 2 * i + 2) for i, block in enumerate(dh_held)]
    done = [dh_far_a, up_sum, ring_round(*done), totals.hop(*done)]
    dh_held = hold(dh_held, *done)
    dh_far_b = [swap(block[split:], "seq", 2 * i + 2) for i, block in enumerate(dh_held)]
    done = [dh_far_b, ring_round(*done), totals.hop(*done)]

    mine = hold(ring_sum.result(), *done)
    grad_out = mine[:, 3 * cols :]
    thirds = [mine[:, t * cols : (t + 1) * cols].astype(BF) for t in range(3)]
    got = []
    for p in range(3):
        perm = [((3 * d + p) % ns, d) for d in range(ns)]
        section = [0] * ns
        for d in range(ns):
            section[(3 * d + p) % ns] = (3 * d + p) // ns
        which = sum(jnp.where(s == i, t, 0) for i, t in enumerate(section))
        piece = jnp.where(which == 0, thirds[0], jnp.where(which == 1, thirds[1], thirds[2]))
        got.append(lax.ppermute(piece, "seq", perm))
    grad_qkv = jnp.concatenate(got, axis=1).astype(F32)
    total = totals.hop(*done)
    while totals.steps:
        total = totals.hop(total)

    share = nf // ns * sub
    ups = exchanged([lax.dynamic_slice_in_dim(up_sum, order[j] * share, share, axis=1) for j in range(ns)])
    grad_up, grad_down_t = settle(ups, downs, slots, strip)

    dh_far = [jnp.concatenate(pair, axis=0) for pair in zip(dh_far_a, dh_far_b)]
    dh_one = add_up([cut(dh_one_part, 0), dh_near[0], *dh_far])
    normal_x, inverse_x = normalise(x_own.astype(F32))
    grad_inputs = (dx_one + norm_back(normal_x, inverse_x, ln1_gain, dh_one)).astype(BF)
    layer_out = (x_one + add_up([mixed_block(0), mixed_near[0], *mixed_far]) + down_bias).astype(BF)
    total = totals.vector
    sum_hidden = jnp.swapaxes(total[8 : 8 + ns, :wide].reshape(ns, nf, sub), 0, 1).reshape(nf, ns * sub)
    sums = [total[i] for i in range(8)]
    sums.insert(7, sum_hidden[:, :strip].reshape(nf * strip))
    return (layer_out[None], grad_inputs[None], grad_qkv, grad_out, grad_up, grad_down_t.T, *sums)


def solution(mesh):
    tokens, weights, shared = P("fsdp", "seq", None), P("fsdp", None), P()
    marks, grads = P("fsdp", "seq"), P("fsdp", "seq")
    return jax.shard_map(
        local,
        mesh=mesh,
        in_specs=(tokens, marks, marks, tokens) + (weights,) * 4 + (shared,) * 9,
        out_specs=(tokens, tokens) + (grads,) * 4 + (shared,) * 9,
        check_vma=False,
    )
```
